32 devices in a mesh: batch: 2 (over x), seq: 16 (over z, y, core).
Axes of the slice: x: 2, y: 2, z: 4, core: 2. Of those that a mesh axis runs over, the one named last changes fastest.
Arguments:
- inputs: bfloat16 [2, 2048, 1024], P('batch', 'seq'), may hold values from -6 to 6
- seg_ids: int32 [2, 2048], P('batch', 'seq'), may hold values from 0 to 3, never falling along the last dimension, each value on 1 to 1024 neighbouring positions
- gain_attn: bfloat16 [1024], P('batch'), may hold values from 0.5 to 1.5
- w_query: bfloat16 [1024, 512], P('batch'), may hold values from -0.1875 to 0.1875
- w_key: bfloat16 [1024, 512], P('batch'), may hold values from -0.1875 to 0.1875
- w_value: bfloat16 [1024, 1024], P('batch'), may hold values from -0.1875 to 0.1875
- w_outgate: bfloat16 [1024, 1024], P('batch'), may hold values from -0.1875 to 0.1875
- w_rank_in: bfloat16 [1024, 16], P('batch'), may hold values from -0.1875 to 0.1875
- w_rank_out: bfloat16 [16, 512], P(None, 'batch'), may hold values from -1.5 to 1.5
- rank_bias: bfloat16 [512], P('batch'), may hold values from -0.5 to 6
- head_gain: bfloat16 [256], P('batch'), may hold values from 0.5 to 1.5
- w_output: bfloat16 [1024, 1024], P(None, 'batch'), may hold values from -0.1875 to 0.1875
- gain_ffn: bfloat16 [1024], P('batch'), may hold values from 0.5 to 1.5
- w_gate: bfloat16 [1024, 2816], P('batch'), may hold values from -0.1875 to 0.1875
- w_up: bfloat16 [1024, 2816], P('batch'), may hold values from -0.1875 to 0.1875
- w_down: bfloat16 [2816, 1024], P('batch'), may hold values from -0.109375 to 0.109375
- cotangent: bfloat16 [2, 2048, 1024], P('batch', 'seq'), may hold values from -6 to 6
Outputs:
- output: bfloat16 [2, 2048, 1024], P('batch', 'seq')
- grad_inputs: bfloat16 [2, 2048, 1024], P('batch', 'seq')
- grad_gain_attn: float32 [1024], P('batch')
- grad_w_query: float32 [1024, 512], P('batch')
- grad_w_key: float32 [1024, 512], P('batch')
- grad_w_value: float32 [1024, 1024], P('batch')
- grad_w_outgate: float32 [1024, 1024], P('batch')
- grad_w_rank_in: float32 [1024, 16], P('batch')
- grad_w_rank_out: float32 [16, 512], P(None, 'batch')
- grad_rank_bias: float32 [512], P('batch')
- grad_head_gain: float32 [256], P('batch')
- grad_w_output: float32 [1024, 1024], P(None, 'batch')
- grad_gain_ffn: float32 [1024], P('batch')
- grad_w_gate: float32 [1024, 2816], P('batch')
- grad_w_up: float32 [1024, 2816], P('batch')
- grad_w_down: float32 [2816, 1024], P('batch')
The draws below stay inside these ranges and needn't reach their ends.
Inputs may be any that keep to these rules, and one draw needn't show every extreme that they name: `seg_ids`: along each sequence document ids never fall; each document holds 1 to 1024 tokens and one holds exactly 1024.
All inputs are finite; a program needn't handle non-finite values.
Results may differ from the reference program's by a relative error of at most 0.023.
Values may be sent and summed in bfloat16 or wider, within the bound.
A program may use at most 192 MiB of HBM per device.

```python
import math
import jax
import jax.numpy as jnp
import numpy as np
from jax import lax

D = 1024
HEADS = 4
DK = 128
DV = 256
RANK = 16
FF = 2816
SPAN = 64
KEYS = 512
VALS = 1024
SEQ_LEN = 2048
SEQS = 2
SEG_MOST = 1024
SEG_COUNT = 4


def draw_rank_bias(key, part):
    pick_key, fast_key, slow_key = jax.random.split(key, 3)
    share = 0.5
    slow_pick = jax.random.bernoulli(pick_key, share, (KEYS,))
    fast_vals = jax.random.uniform(fast_key, (KEYS,), jnp.float32, -0.5, 1.0)
    slow_base = min(math.log(SEG_MOST / 37.0), 3.5) + 1.5
    slow_vals = slow_base + jax.random.uniform(slow_key, (KEYS,), jnp.float32)
    return jnp.where(slow_pick, slow_vals, fast_vals).astype(jnp.bfloat16)


def level_of(own_key, extent, cuts, least, top_value):
    def one(dim, parts):
        steps = jax.random.uniform(jax.random.fold_in(jax.random.fold_in(own_key, 6), dim), (parts,), jnp.float32, least / len(cuts), top_value / len(cuts))
        return jnp.repeat(jnp.exp(steps), extent[dim] // parts).reshape((-1,) + (1,) * (len(extent) - dim - 1))

    level = one(*cuts[0])
    for cut in cuts[1:]:
        level = level * one(*cut)
    return level


def length_profile(amount, total, bound, slope):
    loads = [(1 << 20) // math.isqrt(standing ** slope) + 1 for standing in range(2, amount + 1)]
    spare, counts = total - bound - (amount - 1), [1] * (amount - 1)
    while spare > 0:
        candidates = [i for i in range(amount - 1) if counts[i] < bound]
        mass, left = sum([loads[i] for i in candidates]), spare
        for i in candidates:
            extra = min(bound - counts[i], max(1, left * loads[i] // mass), spare)
            counts[i] = counts[i] + extra
            spare = spare - extra
    return np.array([bound] + counts)


def ragged(stream_key, amount, total, most, skew):
    if amount == 2:
        one = jax.random.randint(stream_key, (), max(1, total - most), min(most, total - 1) + 1)
        return jnp.stack([one, total - one])
    lengths = jnp.asarray(length_profile(amount, total, most, skew), jnp.int32)
    twos = (amount - 1) // 2
    donor, sink = lengths[1:1 + 2 * twos:2], lengths[2:2 + 2 * twos:2]
    slack = jnp.minimum(donor - 1, most - sink)
    moved = jax.random.randint(jax.random.fold_in(stream_key, 1), (twos,), 0, 1 << 20) % (slack + 1)
    lengths = lengths.at[1:1 + 2 * twos:2].set(donor - moved).at[2:2 + 2 * twos:2].set(sink + moved)
    return lengths[jax.random.permutation(jax.random.fold_in(stream_key, 2), amount)]


def gaussian(own_key, dims, deviation, reach, shards=(), dtype=jnp.bfloat16):
    drawn = jax.random.normal(own_key, dims, jnp.float32) * deviation
    if len(shards) > 0:
        drawn = level_of(own_key, dims, shards, -0.22, 0.18) * drawn
    return jnp.clip(drawn, min=-reach, max=reach).astype(dtype)


def setup_inputs(seed: int = 0) -> dict:
    arg_keys = jax.random.split(jax.random.key(seed), 18)
    inputs = gaussian(arg_keys[0], (SEQS, SEQ_LEN, D), 1.0, 6.0, ((0, 2), (1, 16)))
    seg_ids = jax.vmap(lambda own: jnp.searchsorted(jnp.cumsum(ragged(own, SEG_COUNT, SEQ_LEN, SEG_MOST, 2)), jnp.arange(SEQ_LEN), side="right"))(jax.random.split(arg_keys[1], SEQS)).reshape((SEQS, SEQ_LEN)).astype(jnp.int32)
    gain_attn = jnp.clip(1.0 + 0.1 * jax.random.normal(arg_keys[2], (D,), jnp.float32), 0.5, 1.5).astype(jnp.bfloat16)
    w_query = gaussian(arg_keys[3], (D, KEYS), D ** -0.5, 0.1875, ((0, 2),))
    w_key = gaussian(arg_keys[4], (D, KEYS), D ** -0.5, 0.1875, ((0, 2),))
    w_value = gaussian(arg_keys[5], (D, VALS), D ** -0.5, 0.1875, ((0, 2),))
    w_outgate = gaussian(arg_keys[6], (D, VALS), D ** -0.5, 0.1875, ((0, 2),))
    w_rank_in = gaussian(arg_keys[7], (D, RANK), D ** -0.5, 0.1875, ((0, 2),))
    w_rank_out = gaussian(arg_keys[8], (RANK, KEYS), RANK ** -0.5, 1.5, ((1, 2),))
    rank_bias = draw_rank_bias(jax.random.fold_in(arg_keys[17], 71), 0)
    head_gain = jnp.clip(1.0 + 0.1 * jax.random.normal(arg_keys[10], (DV,), jnp.float32), 0.5, 1.5).astype(jnp.bfloat16)
    w_output = gaussian(arg_keys[11], (VALS, D), VALS ** -0.5, 0.1875, ((1, 2),))
    gain_ffn = jnp.clip(1.0 + 0.1 * jax.random.normal(arg_keys[12], (D,), jnp.float32), 0.5, 1.5).astype(jnp.bfloat16)
    w_gate = gaussian(arg_keys[13], (D, FF), D ** -0.5, 0.1875, ((0, 2),))
    w_up = gaussian(arg_keys[14], (D, FF), D ** -0.5, 0.1875, ((0, 2),))
    w_down = gaussian(arg_keys[15], (FF, D), FF ** -0.5, 0.109375, ((0, 2),))
    cotangent = gaussian(arg_keys[16], (SEQS, SEQ_LEN, D), 1.0, 6.0, ((0, 2), (1, 16)))
    return {"inputs": inputs, "seg_ids": seg_ids, "gain_attn": gain_attn, "w_query": w_query, "w_key": w_key, "w_value": w_value, "w_outgate": w_outgate, "w_rank_in": w_rank_in, "w_rank_out": w_rank_out, "rank_bias": rank_bias, "head_gain": head_gain, "w_output": w_output, "gain_ffn": gain_ffn, "w_gate": w_gate, "w_up": w_up, "w_down": w_down, "cotangent": cotangent}


norm_eps = 1e-05
head_eps = 0.1
top_prec = lax.Precision.HIGHEST

def rms_scale(values_in):
    return lax.rsqrt(lax.optimization_barrier(jnp.mean(values_in * values_in, axis=-1, keepdims=True)) + norm_eps)

def head_rms(values_in):
    return lax.rsqrt(lax.optimization_barrier(jnp.mean(values_in * values_in, axis=-1, keepdims=True)) + head_eps)

def span_step(carried_in, inputs_now):
    state_now, prior_id = carried_in
    queries, key_rows, value_rows, decays, seg_now = inputs_now
    span_len = queries.shape[0]
    cumulative = jnp.cumsum(decays, axis=0)
    first_id = seg_now[0]
    state_now = state_now * (prior_id == first_id).astype(jnp.float32)
    within_doc = (seg_now == first_id).astype(jnp.float32)
    query_dec = queries * jnp.exp(cumulative)
    key_dec = key_rows * jnp.exp(-cumulative)
    scores = jnp.einsum('thc,shc->hts', query_dec, key_dec, precision=top_prec)
    row_pos = lax.broadcasted_iota(jnp.int32, (span_len, span_len), 0)
    col_pos = lax.broadcasted_iota(jnp.int32, (span_len, span_len), 1)
    allowed = jnp.logical_and(col_pos <= row_pos, seg_now[:, None] == seg_now[None, :]).astype(jnp.float32)
    scores = scores * allowed[None]
    span_out = jnp.einsum('hts,shv->thv', scores, value_rows, precision=top_prec)
    span_out = span_out + within_doc[:, None, None] * jnp.einsum('thc,hcv->thv', query_dec, state_now, precision=top_prec)
    last_cumul = cumulative[-1]
    end_doc = (seg_now == seg_now[-1]).astype(jnp.float32)
    key_end = key_rows * jnp.exp(last_cumul[None] - cumulative) * end_doc[:, None, None]
    next_state = (jnp.exp(last_cumul) * within_doc[-1])[:, :, None] * state_now
    next_state = next_state + jnp.einsum('shc,shv->hcv', key_end, value_rows, precision=top_prec)
    return ((next_state, seg_now[-1]), span_out)

def gla_run(queries, key_rows, value_rows, decays, seg_row, start_state, prior_id):
    tok_count = queries.shape[0]
    num_spans = tok_count // SPAN

    def blocks(array_in):
        return array_in.reshape((num_spans, SPAN) + array_in.shape[1:])
    (final_state, last_id), outs_all = lax.scan(span_step, (start_state, prior_id), (blocks(queries), blocks(key_rows), blocks(value_rows), blocks(decays), seg_row.reshape(num_spans, SPAN)))
    return (outs_all.reshape((tok_count,) + outs_all.shape[2:]), final_state)

def silu_grad(pre_act, sig_val):
    return sig_val * (1.0 + pre_act * (1.0 - sig_val))

def sequence_pass(activ_in, seg_row, cot_rows, params):
    gain_one, query_w, key_w, value_w, outgate_w, rank_in_w, rank_out_w, bias_w, headgain_w, output_w, gain_two, gate_w, up_w, down_w = params
    f32 = jnp.float32
    bf16 = jnp.bfloat16
    activation = activ_in.astype(f32)
    tok_count = activation.shape[0]
    scale_one = rms_scale(activation)
    unit_one = activation * scale_one
    normed = (unit_one * gain_one.astype(f32)).astype(bf16)
    queries = jnp.dot(normed, query_w, preferred_element_type=f32) * DK ** (-0.5)
    keys_all = jnp.dot(normed, key_w, preferred_element_type=f32)
    values_all = jnp.dot(normed, value_w, preferred_element_type=f32)
    outgate = jnp.dot(normed, outgate_w, preferred_element_type=f32)
    low_rank = jnp.dot(normed, rank_in_w, preferred_element_type=f32)
    logits = jnp.dot(low_rank, rank_out_w.astype(f32), precision=top_prec) + bias_w.astype(f32)
    decays = jax.nn.log_sigmoid(logits) / 16.0

    def attention_core(queries_h, keys_h, values_h, decays_h):
        outs_all, final_state = gla_run(queries_h, keys_h, values_h, decays_h, seg_row, jnp.zeros((HEADS, DK, DV), f32), jnp.int32(-1))
        return outs_all
    attn_raw, pullback = jax.vjp(attention_core, queries.reshape(tok_count, HEADS, DK), keys_all.reshape(tok_count, HEADS, DK), values_all.reshape(tok_count, HEADS, DV), decays.reshape(tok_count, HEADS, DK))
    head_scale = head_rms(attn_raw)
    head_norm = attn_raw * head_scale
    gate_h = outgate.reshape(tok_count, HEADS, DV)
    gate_sig = jax.nn.sigmoid(gate_h)
    gate_act = gate_h * gate_sig
    head_gain32 = headgain_w.astype(f32)
    gated = (head_norm * head_gain32 * gate_act).reshape(tok_count, VALS).astype(bf16)
    resid = activation + jnp.dot(gated, output_w, preferred_element_type=f32)
    scale_two = rms_scale(resid)
    unit_two = resid * scale_two
    normed_two = (unit_two * gain_two.astype(f32)).astype(bf16)
    gate_pre = jnp.dot(normed_two, gate_w, preferred_element_type=f32)
    up_pre = jnp.dot(normed_two, up_w, preferred_element_type=f32)
    ffn_sig = jax.nn.sigmoid(gate_pre)
    hidden = (gate_pre * ffn_sig * up_pre).astype(bf16)
    output = (resid + jnp.dot(hidden, down_w, preferred_element_type=f32)).astype(bf16)
    grad_down = jnp.dot(hidden.T, cot_rows, preferred_element_type=f32)
    grad_hidden = jnp.dot(cot_rows, down_w.T, preferred_element_type=f32)
    grad_gate_pre = (grad_hidden * up_pre * silu_grad(gate_pre, ffn_sig)).astype(bf16)
    grad_up_pre = (grad_hidden * gate_pre * ffn_sig).astype(bf16)
    grad_gate = jnp.dot(normed_two.T, grad_gate_pre, preferred_element_type=f32)
    grad_up = jnp.dot(normed_two.T, grad_up_pre, preferred_element_type=f32)
    grad_normed_two = jnp.dot(grad_gate_pre, gate_w.T, preferred_element_type=f32) + jnp.dot(grad_up_pre, up_w.T, preferred_element_type=f32)
    grad_gain_two = lax.optimization_barrier(jnp.sum(grad_normed_two * unit_two, axis=0))
    scaled_two = grad_normed_two * gain_two.astype(f32)
    grad_resid = cot_rows.astype(f32) + scale_two * (scaled_two - unit_two * lax.optimization_barrier(jnp.mean(scaled_two * unit_two, axis=-1, keepdims=True)))
    resid_bf = grad_resid.astype(bf16)
    grad_output = jnp.dot(gated.T, resid_bf, preferred_element_type=f32)
    grad_gated = jnp.dot(resid_bf, output_w.T, preferred_element_type=f32).reshape(tok_count, HEADS, DV)
    grad_headgain = lax.optimization_barrier(jnp.sum(grad_gated * head_norm * gate_act, axis=(0, 1)))
    grad_gate_h = grad_gated * head_norm * head_gain32 * silu_grad(gate_h, gate_sig)
    grad_norm_h = grad_gated * head_gain32 * gate_act
    grad_attn = head_scale * (grad_norm_h - head_norm * lax.optimization_barrier(jnp.mean(grad_norm_h * head_norm, axis=-1, keepdims=True)))
    grad_q, grad_k, grad_v, grad_d = pullback(grad_attn)
    grad_logits = grad_d.reshape(tok_count, KEYS) * jax.nn.sigmoid(-logits) / 16.0
    grad_bias = lax.optimization_barrier(jnp.sum(grad_logits, axis=0))
    grad_rank_out = jnp.dot(low_rank.T, grad_logits, precision=top_prec)
    grad_low = jnp.dot(grad_logits, rank_out_w.astype(f32).T, precision=top_prec).astype(bf16)
    query_grad = (grad_q.reshape(tok_count, KEYS) * DK ** (-0.5)).astype(bf16)
    key_grad = grad_k.reshape(tok_count, KEYS).astype(bf16)
    value_grad = grad_v.reshape(tok_count, VALS).astype(bf16)
    outgate_grad = grad_gate_h.reshape(tok_count, VALS).astype(bf16)
    grad_query = jnp.dot(normed.T, query_grad, preferred_element_type=f32)
    grad_key = jnp.dot(normed.T, key_grad, preferred_element_type=f32)
    grad_value = jnp.dot(normed.T, value_grad, preferred_element_type=f32)
    grad_outgate = jnp.dot(normed.T, outgate_grad, preferred_element_type=f32)
    grad_rank_in = jnp.dot(normed.T, grad_low, preferred_element_type=f32)
    grad_normed = jnp.dot(query_grad, query_w.T, preferred_element_type=f32) + jnp.dot(key_grad, key_w.T, preferred_element_type=f32) + jnp.dot(value_grad, value_w.T, preferred_element_type=f32) + jnp.dot(outgate_grad, outgate_w.T, preferred_element_type=f32) + jnp.dot(grad_low, rank_in_w.T, preferred_element_type=f32)
    grad_gain_one = lax.optimization_barrier(jnp.sum(grad_normed * unit_one, axis=0))
    scaled_one = grad_normed * gain_one.astype(f32)
    grad_input = (grad_resid + scale_one * (scaled_one - unit_one * lax.optimization_barrier(jnp.mean(scaled_one * unit_one, axis=-1, keepdims=True)))).astype(bf16)
    grads = (grad_gain_one, grad_query, grad_key, grad_value, grad_outgate, grad_rank_in, grad_rank_out, grad_bias, grad_headgain, grad_output, grad_gain_two, grad_gate, grad_up, grad_down)
    return (output, grad_input, grads)

def reference(inputs, seg_ids, gain_attn, w_query, w_key, w_value, w_outgate, w_rank_in, w_rank_out, rank_bias, head_gain, w_output, gain_ffn, w_gate, w_up, w_down, cotangent):
    params = (gain_attn, w_query, w_key, w_value, w_outgate, w_rank_in, w_rank_out, rank_bias, head_gain, w_output, gain_ffn, w_gate, w_up, w_down)
    empty_grads = tuple((jnp.zeros(param.shape, jnp.float32) for param in params))

    def per_sequence(totals, items):
        out_rows, grad_rows, grads = sequence_pass(items[0], items[1], items[2], params)
        return (tuple((left + right for left, right in zip(totals, grads))), (out_rows, grad_rows))
    totals, outs_pair = lax.scan(per_sequence, empty_grads, (inputs, seg_ids, cotangent))
    return (outs_pair[0], outs_pair[1], totals[0], totals[1], totals[2], totals[3], totals[4], totals[5], totals[6], totals[7], totals[8], totals[9], totals[10], totals[11], totals[12], totals[13])
```

```python
import jax
import jax.numpy as jnp
from jax import lax
from jax.sharding import PartitionSpec as P

HEADS = 4
DK = 128
DV = 256
SPAN = 64
KEYS = 512
VALS = 1024


norm_eps = 1e-05
head_eps = 0.1
top_prec = lax.Precision.HIGHEST
BOTH = ("batch", "seq")
SEG_MOST = 1024
PAIR = 2


def rms_scale(values_in):
    return lax.rsqrt(jnp.mean(values_in * values_in, axis=-1, keepdims=True) + norm_eps)


def head_rms(values_in):
    return lax.rsqrt(jnp.mean(values_in * values_in, axis=-1, keepdims=True) + head_eps)


def silu_grad(pre_act, sig_val):
    return sig_val * (1.0 + pre_act * (1.0 - sig_val))


def mm(eq, a, b):
    return jnp.einsum(eq, a, b, precision=top_prec)


def to_spans(array_in, width):
    return array_in.reshape(-1, SPAN, array_in.shape[1] // width, width).transpose(0, 2, 1, 3)


def from_spans(array_in):
    spans, heads, span_len, width = array_in.shape
    return array_in.transpose(0, 2, 1, 3).reshape(spans * span_len, heads * width)


class Places:
    def __init__(self):
        self.nb = lax.axis_size("batch")
        self.ns = lax.axis_size("seq")
        self.b = lax.axis_index("batch")
        self.s = lax.axis_index("seq")
        self.c = self.s % PAIR
        self.t = self.s // PAIR
        self.chips = self.ns // PAIR
        self.ny = 2 if self.chips % 2 == 0 else 1
        self.nz = self.chips // self.ny
        self.y = self.t % self.ny
        self.z = self.t // self.ny

    def seq_hop(self, array_in, pairs):
        return lax.ppermute(array_in, "seq", pairs)

    def pair_hop(self, array_in):
        return self.seq_hop(array_in, [(i, i ^ 1) for i in range(self.ns)])

    def y_hop(self, array_in):
        return self.seq_hop(array_in, [(i, i ^ PAIR) for i in range(self.ns)])

    def chip_shift(self, array_in, by):
        step = by * PAIR
        return self.seq_hop(
            array_in, [(i, i + step) for i in range(self.ns) if 0 <= i + step < self.ns]
        )

    def from_batch(self, array_in, k):
        nb = self.nb
        return lax.ppermute(array_in, "batch", [((d + k) % nb, d) for d in range(nb)])

    def others(self, array_in):
        return [self.from_batch(array_in, k) for k in range(1, self.nb)]

    def by_core(self, mine, other, axis):
        return jnp.where(
            self.c == 0,
            jnp.concatenate([mine, other], axis),
            jnp.concatenate([other, mine], axis),
        )

    def pair_all(self, mine, axis=0):
        return self.by_core(mine, self.pair_hop(mine), axis)

    def pair_sum(self, partial):
        rows = partial.shape[0] // PAIR
        own = lax.dynamic_slice_in_dim(partial, self.c * rows, rows, 0)
        away = lax.dynamic_slice_in_dim(partial, (1 - self.c) * rows, rows, 0)
        return own + self.pair_hop(away)

    def to_rel(self, array_in, axis):
        nb = self.nb
        width = array_in.shape[axis] // nb
        if nb == 2:
            low = lax.slice_in_dim(array_in, 0, width, axis=axis)
            high = lax.slice_in_dim(array_in, width, 2 * width, axis=axis)
            return jnp.where(
                self.b == 0,
                jnp.concatenate([low, high], axis),
                jnp.concatenate([high, low], axis),
            )
        return jnp.roll(array_in, -self.b * width, axis)

    def to_abs(self, array_in, axis):
        if self.nb == 2:
            return self.to_rel(array_in, axis)
        return jnp.roll(array_in, self.b * (array_in.shape[axis] // self.nb), axis)

    def joint_hop(self, array_in, source, need):
        pairs = []
        for b in range(self.nb):
            for s in range(self.ns):
                if need(b, s):
                    sb, ss = source(b, s)
                    pairs.append((sb * self.ns + ss, b * self.ns + s))
        return lax.ppermute(array_in, BOTH, pairs)

    def weight_parts(self, piece, need=lambda b, s: True):
        if self.nb != 2 or self.ns % 8 or piece.shape[0] % 128:
            return jnp.concatenate(self.others(piece), axis=0)
        rows, cols = piece.shape
        quarter, eighth = rows // 4, rows // 8
        k = (self.s // 2) % 4
        own = lax.dynamic_slice_in_dim(piece, k * quarter, quarter, 0)
        first = self.joint_hop(own, lambda b, s: (1 - b, s), need)
        over_y = self.joint_hop(first, lambda b, s: (b, s ^ 2), need)
        over_z = self.joint_hop(first, lambda b, s: (b, s ^ 4), need)
        far_y = self.joint_hop(over_z[:eighth], lambda b, s: (b, s ^ 2), need)
        far_z = self.joint_hop(over_y[eighth:], lambda b, s: (b, s ^ 4), need)
        out = jnp.zeros((rows, cols), piece.dtype)
        for mask, part in ((0, first), (1, over_y), (2, over_z)):
            out = lax.dynamic_update_slice_in_dim(out, part, (k ^ mask) * quarter, 0)
        out = lax.dynamic_update_slice_in_dim(out, far_y, (k ^ 3) * quarter, 0)
        return lax.dynamic_update_slice_in_dim(out, far_z, (k ^ 3) * quarter + eighth, 0)

    def z_hop(self, array_in, by, keep):
        step = PAIR * self.ny
        pairs = []
        for i in range(self.ns):
            z = i // step
            if keep(z) and 0 <= z + by < self.nz:
                pairs.append((i, i + by * step))
        return self.seq_hop(array_in, pairs)

    def z_scatter(self, blocks):
        nz = self.nz
        total = lax.dynamic_index_in_dim(blocks, self.z, 0, False).astype(jnp.float32)
        for way in (1, -1):
            carry = None
            for step in range(1, nz):
                at = jnp.clip(self.z + way * (nz - step), 0, nz - 1)
                going = lax.dynamic_index_in_dim(blocks, at, 0, False)
                if carry is not None:
                    going = (going.astype(jnp.float32) + carry.astype(jnp.float32)).astype(
                        blocks.dtype
                    )
                if way == 1:
                    keep = lambda z, step=step: z <= step - 1
                else:
                    keep = lambda z, step=step: z >= nz - step
                carry = self.z_hop(going, way, keep)
            if carry is not None:
                total = total + carry.astype(jnp.float32)
        return total.astype(blocks.dtype)

    def z_gather(self, own):
        nz = self.nz
        out = jnp.zeros((2 * nz - 1,) + own.shape, own.dtype)
        parts = {0: own}
        for way in (1, -1):
            going = own
            for step in range(1, nz):
                if way == 1:
                    keep = lambda z, step=step: z >= step - 1
                else:
                    keep = lambda z, step=step: z <= nz - step
                going = self.z_hop(going, way, keep)
                parts[-way * step] = going
        rel = jnp.stack([parts[i] for i in range(1 - nz, nz)])
        return lax.dynamic_slice_in_dim(rel, nz - 1 - self.z, nz, 0)

    def y_scatter(self, blocks):
        if self.ny == 1:
            return blocks[0]
        own = lax.dynamic_index_in_dim(blocks, self.y, 0, False)
        away = lax.dynamic_index_in_dim(blocks, 1 - self.y, 0, False)
        return (own.astype(jnp.float32) + self.y_hop(away).astype(jnp.float32)).astype(
            blocks.dtype
        )

    def y_gather(self, own):
        if self.ny == 1:
            return own[None]
        other = self.y_hop(own)
        return jnp.where(self.y == 0, jnp.stack([own, other]), jnp.stack([other, own]))

    def plane_sum(self, grad, y_first):
        rows, cols = grad.shape
        if y_first:
            blocks = grad.reshape(self.ny, self.nz, -1, cols)
            own = self.z_scatter(self.y_scatter(blocks))
            return self.y_gather(self.z_gather(own)).reshape(rows, cols)
        blocks = grad.reshape(self.nz, self.ny, -1, cols)
        own = self.y_scatter(self.z_scatter(blocks))
        return self.z_gather(self.y_gather(own)).reshape(rows, cols)

    def total_sum(self, rel_rows):
        nb = self.nb
        total = rel_rows[0]
        for k in range(1, nb):
            total = total + self.from_batch(rel_rows[nb - k], k)
        step = 1
        while step < self.ns:
            total = total + self.seq_hop(total, [(i, i ^ step) for i in range(self.ns)])
            step *= 2
        return total


def core_cols(array_in, c):
    width = array_in.shape[1] // PAIR
    return lax.dynamic_slice_in_dim(array_in, c * width, width, 1)


def dot32(a, b):
    return jnp.dot(a, b, preferred_element_type=jnp.float32)


def dot_t(a, b):
    return lax.dot_general(a, b, (((1,), (1,)), ((), ())), preferred_element_type=jnp.float32)


def grad_dot(pairs_in):
    total = None
    for left, right in pairs_in:
        part = lax.dot_general(
            left, right, (((0,), (0,)), ((), ())), preferred_element_type=jnp.float32
        )
        total = part if total is None else total + part
    return total


def per_device(
    inputs,
    seg_ids,
    gain_attn,
    w_query,
    w_key,
    w_value,
    w_outgate,
    w_rank_in,
    w_rank_out,
    rank_bias,
    head_gain,
    w_output,
    gain_ffn,
    w_gate,
    w_up,
    w_down,
    cotangent,
):
    f32 = jnp.float32
    bf16 = jnp.bfloat16
    at_place = Places()
    nb, b, c, t = at_place.nb, at_place.b, at_place.c, at_place.t
    rank = w_rank_in.shape[1]
    heads = HEADS // PAIR
    keys_w, vals_w = KEYS // PAIR, VALS // PAIR
    dim = inputs.shape[2]
    dim_own = dim // nb

    in_pair = at_place.pair_all(inputs[0])
    seg_row = at_place.pair_all(seg_ids[0])
    tok_count = seg_row.shape[0]
    half_tok = tok_count // PAIR
    spans = tok_count // SPAN
    edges = jnp.stack([seg_row[0], seg_row[-1]])
    edges_wide = jnp.broadcast_to(edges[:, None], (2, 128)).astype(f32)
    prev_last = at_place.chip_shift(edges_wide, 1)[1, 0]
    next_first = at_place.chip_shift(edges_wide, -1)[0, 0]
    first_id, last_id = edges[0].astype(f32), edges[1].astype(f32)
    from_prev = jnp.logical_and(t > 0, prev_last == first_id).astype(f32)
    to_next = jnp.logical_and(t < at_place.chips - 1, next_first == last_id).astype(f32)
    whole_doc = (first_id == last_id).astype(f32)

    small = (gain_attn, gain_ffn, rank_bias, head_gain, w_rank_in, w_rank_out)
    packed = jnp.concatenate([a.reshape(-1) for a in small])
    packed = jnp.stack([packed] + at_place.others(packed))
    parts, at = [], 0
    for a in small:
        parts.append(packed[:, at : at + a.size])
        at += a.size
    gain_one = parts[0].reshape(-1).astype(f32)
    gain_two = parts[1].reshape(-1).astype(f32)
    bias_all = at_place.to_abs(parts[2], 0).reshape(-1).astype(f32)
    bias_w = lax.dynamic_slice_in_dim(bias_all, c * keys_w, keys_w)
    head_gain32 = at_place.to_abs(parts[3], 0).reshape(-1).astype(f32)
    rank_in_w = parts[4].reshape(-1, rank)
    rank_out_all = (
        at_place.to_abs(parts[5], 0).reshape((nb,) + w_rank_out.shape).transpose(1, 0, 2)
        .reshape(rank, -1)
    )
    rank_out_w = core_cols(rank_out_all, c).astype(f32)

    proj_own = jnp.concatenate(
        [core_cols(a, c) for a in (w_query, w_key, w_value, w_outgate)], axis=1
    )
    proj_far = at_place.weight_parts(proj_own)
    out_own = lax.dynamic_slice_in_dim(w_output, c * vals_w, vals_w, 0)
    out_far = at_place.weight_parts(out_own)
    gu_own = jnp.concatenate([core_cols(w_gate, c), core_cols(w_up, c)], axis=1)
    gu_far = at_place.weight_parts(gu_own)
    if nb == 2:
        down_far = at_place.weight_parts(w_down, lambda bb, ss: ss % PAIR != bb)
        down_w = jnp.where(c == b, w_down, down_far)
    else:
        down_all = at_place.to_abs(
            jnp.concatenate([w_down, at_place.weight_parts(w_down)], axis=0), 0
        )
        ff_half = down_all.shape[0] // PAIR
        down_w = lax.dynamic_slice_in_dim(down_all, c * ff_half, ff_half, 0)
    ff_c = down_w.shape[0]

    cot_own = cotangent[0]
    cot_pair = at_place.pair_all(cot_own)
    cot_far = [at_place.pair_all(a) for a in at_place.others(cot_own)]

    activation = at_place.to_rel(in_pair, 1).astype(f32)
    scale_one = rms_scale(activation)
    unit_one = activation * scale_one
    normed = (unit_one * gain_one).astype(bf16)
    normed_far = [
        at_place.from_batch(normed[:, (nb - k) * dim_own : (nb - k + 1) * dim_own], k)
        for k in range(1, nb)
    ]

    low_rank = dot32(normed, rank_in_w)
    logits = jnp.dot(low_rank, rank_out_w, precision=top_prec) + bias_w
    decays = jax.nn.log_sigmoid(logits) / 16.0

    seg_s = seg_row.reshape(spans, SPAN)
    first_s, last_s = seg_s[:, 0], seg_s[:, -1]
    row_pos = lax.broadcasted_iota(jnp.int32, (SPAN, SPAN), 0)
    col_pos = lax.broadcasted_iota(jnp.int32, (SPAN, SPAN), 1)
    lower = (col_pos <= row_pos).astype(f32)
    allowed = lower[None] * (seg_s[:, :, None] == seg_s[:, None, :]).astype(f32)
    allowed = allowed[:, None]
    prior = jnp.concatenate([seg_row[:1], last_s[:-1]])
    enters = (first_s == prior).astype(f32)
    within = ((seg_s == first_s[:, None]).astype(f32) * enters[:, None])[:, None, :, None]
    end_doc = (seg_s == last_s[:, None]).astype(f32)[:, None, :, None]

    cumul = mm("ts,nsc->ntc", lower, decays.reshape(spans, SPAN, keys_w))
    total_log = jnp.sum(cumul[:, -1], axis=0)

    proj = dot32(normed[:, :dim_own], proj_own) + dot32(normed[:, dim_own:], proj_far)
    queries = to_spans(proj[:, :keys_w] * DK ** (-0.5), DK)
    keys_s = to_spans(proj[:, keys_w : 2 * keys_w], DK)
    values_s = to_spans(proj[:, 2 * keys_w : 2 * keys_w + vals_w], DV)
    outgate = proj[:, 2 * keys_w + vals_w :]

    cumul = cumul.reshape(spans, SPAN, heads, DK).transpose(0, 2, 1, 3)
    last_cumul = cumul[:, :, -1:, :]
    grow = jnp.exp(cumul)
    shrink = jnp.exp(-cumul)
    to_end = jnp.exp(last_cumul - cumul) * end_doc
    query_dec = queries * grow
    key_dec = keys_s * shrink
    key_end = keys_s * to_end
    query_in = query_dec * within
    keep = jnp.exp(last_cumul[:, :, 0, :]) * within[:, :, -1]
    scores = mm("nhtc,nhsc->nhts", query_dec, key_dec) * allowed
    local_out = mm("nhts,nhsv->nhtv", scores, values_s)
    added = mm("nhsc,nhsv->nhcv", key_end, values_s)

    local_state = added[0]
    for i in range(1, spans):
        local_state = keep[i][:, :, None] * local_state + added[i]

    reach_chips = -(-(SEG_MOST - 1) // tok_count)

    def chip_scan(state, factor, way):
        state = state.reshape(heads * DK, DV)
        step = 1
        pad = jnp.zeros((15, heads * DK), f32)
        while step < min(reach_chips, at_place.chips):
            packed = jnp.concatenate(
                [state, jnp.concatenate([factor[None], pad]).reshape(-1, DV)]
            )
            got = at_place.chip_shift(packed.astype(bf16), way * step).astype(f32)
            state = state + factor[:, None] * got[: heads * DK]
            factor = factor * got[heads * DK :].reshape(16, -1)[0]
            step *= 2
        got = at_place.chip_shift(state.astype(bf16), way)
        return got.astype(f32).reshape(heads, DK, DV)

    block_keep = jnp.exp(total_log) * whole_doc
    carried = from_prev * chip_scan(local_state, block_keep * from_prev, 1)
    enter_list = [carried]
    for i in range(spans - 1):
        enter_list.append(keep[i][:, :, None] * enter_list[i] + added[i])
    entered = jnp.stack(enter_list)

    attn_raw = from_spans(local_out + mm("nhtc,nhcv->nhtv", query_in, entered)).reshape(
        tok_count, heads, DV
    )
    head_scale = head_rms(attn_raw)
    head_norm = attn_raw * head_scale
    gate_h = outgate.reshape(tok_count, heads, DV)
    gate_sig = jax.nn.sigmoid(gate_h)
    gate_act = gate_h * gate_sig
    gated = (head_norm * head_gain32 * gate_act).reshape(tok_count, vals_w).astype(bf16)
    gated_far = at_place.others(gated)
    out_w = jnp.concatenate(
        [out_own] + [out_far[k * vals_w : (k + 1) * vals_w] for k in range(nb - 1)], axis=1
    )
    own_rows = lambda a: lax.dynamic_slice_in_dim(a, c * half_tok, half_tok, 0)
    resid = own_rows(activation) + at_place.pair_sum(dot32(gated, out_w))
    scale_two = rms_scale(resid)
    unit_two = resid * scale_two
    normed_two = (unit_two * gain_two).astype(bf16)

    two_pair = at_place.pair_all(normed_two)
    two_far = [
        at_place.pair_all(jnp.roll(a, (k + 1) * dim_own, 1))
        for k, a in enumerate(at_place.others(normed_two))
    ]

    def feed_forward(two_rows, cot_rows):
        pre = dot32(two_rows[:, :dim_own], gu_own) + dot32(two_rows[:, dim_own:], gu_far)
        gate_pre, up_pre = pre[:, :ff_c], pre[:, ff_c:]
        sig = jax.nn.sigmoid(gate_pre)
        hidden = (gate_pre * sig * up_pre).astype(bf16)
        grad_hidden = dot_t(cot_rows, down_w)
        grad_gu = jnp.concatenate(
            [
                (grad_hidden * up_pre * silu_grad(gate_pre, sig)).astype(bf16),
                (grad_hidden * gate_pre * sig).astype(bf16),
            ],
            axis=1,
        )
        return hidden, grad_gu

    hidden, grad_gu = feed_forward(two_pair, cot_pair)
    down_sum = at_place.pair_sum(dot32(hidden, down_w))
    output = (at_place.to_abs(resid, 1) + down_sum).astype(bf16)

    two_grad = jnp.concatenate([dot_t(grad_gu, gu_own), dot_t(grad_gu, gu_far)], axis=1)
    grad_two = at_place.pair_sum(two_grad)

    hid_own = [at_place.pair_all(hidden, 1)]
    gu_pairs = [(two_pair[:, :dim_own], grad_gu)]
    down_cots = [cot_pair]
    for two_rows, cot_rows in zip(two_far, cot_far):
        far_hidden, far_grad = feed_forward(two_rows, cot_rows)
        gu_pairs.append((two_rows[:, :dim_own], far_grad))
        hid_own.append(at_place.pair_all(far_hidden, 1))
        down_cots.append(cot_rows)
    ff_own = hid_own[0].shape[1] // nb
    down_pairs = [
        (lax.dynamic_slice_in_dim(h, b * ff_own, ff_own, 1), core_cols(g, c))
        for h, g in zip(hid_own, down_cots)
    ]
    sum_gu = at_place.plane_sum(grad_dot(gu_pairs).astype(bf16), True)
    sum_down = at_place.plane_sum(grad_dot(down_pairs).astype(bf16), False)

    grad_gain_two = jnp.sum(grad_two * unit_two, axis=0)
    scaled_two = grad_two * gain_two
    grad_resid = at_place.to_rel(cot_own, 1).astype(f32) + scale_two * (
        scaled_two - unit_two * jnp.mean(scaled_two * unit_two, axis=-1, keepdims=True)
    )
    resid_pair = at_place.pair_all(grad_resid.astype(bf16))
    resid_far = [
        at_place.from_batch(resid_pair[:, (nb - k) * dim_own : (nb - k + 1) * dim_own], k)
        for k in range(1, nb)
    ]
    sum_out = at_place.plane_sum(
        grad_dot(
            [(gated, resid_pair[:, :dim_own])] + list(zip(gated_far, resid_far))
        ).astype(bf16),
        False,
    )
    grad_gated = dot_t(resid_pair, out_w).reshape(tok_count, heads, DV)
    grad_headgain = jnp.sum(grad_gated * head_norm * gate_act, axis=(0, 1))
    grad_gate_h = grad_gated * head_norm * head_gain32 * silu_grad(gate_h, gate_sig)
    grad_norm_h = grad_gated * head_gain32 * gate_act
    grad_attn = head_scale * (
        grad_norm_h - head_norm * jnp.mean(grad_norm_h * head_norm, axis=-1, keepdims=True)
    )
    grad_o = to_spans(grad_attn.reshape(tok_count, vals_w), DV)

    reach_grad = mm("nhtc,nhtv->nhcv", query_in, grad_o)
    local_grad = reach_grad[spans - 1]
    for i in range(spans - 2, -1, -1):
        local_grad = keep[i][:, :, None] * local_grad + reach_grad[i]
    grad_end = to_next * chip_scan(local_grad, block_keep * to_next, -1)

    grad_scores = mm("nhtv,nhsv->nhts", grad_o, values_s) * allowed
    grad_qd = mm("nhts,nhsc->nhtc", grad_scores, key_dec)
    grad_qd = grad_qd + within * mm("nhtv,nhcv->nhtc", grad_o, entered)
    grad_kd = mm("nhts,nhtc->nhsc", grad_scores, query_dec)
    grad_v = mm("nhts,nhtv->nhsv", scores, grad_o)

    end_list = [grad_end]
    for i in range(spans - 1, 0, -1):
        end_list.append(keep[i][:, :, None] * end_list[-1] + reach_grad[i])
    ends = jnp.stack(end_list[::-1])

    grad_v = grad_v + mm("nhsc,nhcv->nhsv", key_end, ends)
    grad_ke = mm("nhsv,nhcv->nhsc", values_s, ends)
    moved = grad_ke * key_end
    grad_last = jnp.sum(moved, axis=2) + keep * jnp.sum(ends * entered, axis=3)
    grad_cumul = grad_qd * query_dec - grad_kd * key_dec - moved
    grad_d = mm("ts,nhtc->nhsc", lower, grad_cumul) + grad_last[:, :, None, :]
    grad_q = grad_qd * grow
    grad_k = grad_kd * shrink + grad_ke * to_end

    grad_logits = from_spans(grad_d) * jax.nn.sigmoid(-logits) / 16.0
    grad_bias = jnp.sum(grad_logits, axis=0)
    grad_rank_out = jnp.dot(low_rank.T, grad_logits, precision=top_prec)
    grad_low = jnp.dot(grad_logits, rank_out_w.T, precision=top_prec).astype(bf16)
    proj_grad = jnp.concatenate(
        [
            from_spans(grad_q * DK ** (-0.5)).astype(bf16),
            from_spans(grad_k).astype(bf16),
            from_spans(grad_v).astype(bf16),
            grad_gate_h.reshape(tok_count, vals_w).astype(bf16),
        ],
        axis=1,
    )
    proj_grad_far = at_place.others(proj_grad)
    sum_proj = at_place.plane_sum(
        grad_dot(
            [(normed[:, :dim_own], proj_grad)] + list(zip(normed_far, proj_grad_far))
        ).astype(bf16),
        True,
    )
    normed_grad = jnp.concatenate(
        [dot_t(proj_grad, proj_own), dot_t(proj_grad, proj_far)], axis=1
    ) + dot_t(grad_low, rank_in_w)
    grad_normed = at_place.pair_sum(normed_grad)
    unit_own = own_rows(unit_one)
    grad_gain_one = jnp.sum(grad_normed * unit_own, axis=0)
    scaled_one = grad_normed * gain_one
    grad_input = (
        grad_resid
        + own_rows(scale_one)
        * (scaled_one - unit_own * jnp.mean(scaled_one * unit_own, axis=-1, keepdims=True))
    ).astype(bf16)
    grad_rank_in = grad_dot([(normed, grad_low)])

    def own_slot(part):
        return at_place.by_core(part, jnp.zeros_like(part), part.ndim - 1)

    by_owner = jnp.concatenate(
        [
            grad_gain_one.reshape(nb, -1),
            grad_gain_two.reshape(nb, -1),
            at_place.to_rel(own_slot(grad_bias).reshape(nb, -1), 0),
            at_place.to_rel(grad_headgain.reshape(nb, -1), 0),
            grad_rank_in.reshape(nb, -1),
            at_place.to_rel(
                own_slot(grad_rank_out).reshape(rank, nb, -1).transpose(1, 0, 2).reshape(nb, -1), 0
            ),
        ],
        axis=1,
    )
    owned = at_place.total_sum(by_owner)
    outs, at = [], 0
    for a in small:
        outs.append(owned[at : at + a.size].reshape(a.shape))
        at += a.size
    g_gain_one, g_gain_two, g_bias, g_headgain, g_rank_in, g_rank_out = outs

    def both_cores(mine, splits):
        other = at_place.pair_hop(mine)
        return [
            at_place.by_core(mine[:, lo:hi], other[:, lo:hi], 1).astype(f32) for lo, hi in splits
        ]

    g_gate, g_up = both_cores(sum_gu, ((0, ff_c), (ff_c, 2 * ff_c)))
    (g_down,) = both_cores(sum_down, ((0, sum_down.shape[1]),))
    g_query, g_key, g_value, g_outgate = both_cores(
        sum_proj,
        (
            (0, keys_w),
            (keys_w, 2 * keys_w),
            (2 * keys_w, 2 * keys_w + vals_w),
            (2 * keys_w + vals_w, 2 * keys_w + 2 * vals_w),
        ),
    )
    g_output = at_place.pair_all(sum_out, 0).astype(f32)
    return (
        output[None],
        at_place.to_abs(grad_input, 1)[None],
        g_gain_one,
        g_query,
        g_key,
        g_value,
        g_outgate,
        g_rank_in,
        g_rank_out,
        g_bias,
        g_headgain,
        g_output,
        g_gain_two,
        g_gate,
        g_up,
        g_down,
    )


def solution(mesh):
    in_specs = (
        P("batch", "seq", None),
        P("batch", "seq"),
        P("batch"),
        P("batch", None),
        P("batch", None),
        P("batch", None),
        P("batch", None),
        P("batch", None),
        P(None, "batch"),
        P("batch"),
        P("batch"),
        P(None, "batch"),
        P("batch"),
        P("batch", None),
        P("batch", None),
        P("batch", None),
        P("batch", "seq", None),
    )
    out_specs = (
        P("batch", "seq", None),
        P("batch", "seq", None),
        P("batch"),
        P("batch", None),
        P("batch", None),
        P("batch", None),
        P("batch", None),
        P("batch", None),
        P(None, "batch"),
        P("batch"),
        P("batch"),
        P(None, "batch"),
        P("batch"),
        P("batch", None),
        P("batch", None),
        P("batch", None),
    )
    return jax.shard_map(
        per_device, mesh=mesh, in_specs=in_specs, out_specs=out_specs, check_vma=False
    )
```

```python
import functools

import jax
import jax.numpy as jnp
from jax import lax
from jax.experimental import pallas as pl
from jax.experimental.pallas import tpu as pltpu
from jax.sharding import PartitionSpec as P

HEADS = 4
DK = 128
DV = 256
SPAN = 64
KEYS = 512
VALS = 1024


norm_eps = 1e-05
head_eps = 0.1
top_prec = lax.Precision.HIGHEST
BOTH = ("batch", "seq")
SEG_MOST = 1024
PAIR = 2


def rms_scale(values_in):
    return lax.rsqrt(jnp.mean(values_in * values_in, axis=-1, keepdims=True) + norm_eps)


def head_rms(values_in):
    return lax.rsqrt(jnp.mean(values_in * values_in, axis=-1, keepdims=True) + head_eps)


def silu_grad(pre_act, sig_val):
    return sig_val * (1.0 + pre_act * (1.0 - sig_val))


def mm(eq, a, b):
    return jnp.einsum(eq, a, b, precision=top_prec)


def to_spans(array_in, width):
    return array_in.reshape(-1, SPAN, array_in.shape[1] // width, width).transpose(0, 2, 1, 3)


def from_spans(array_in):
    spans, heads, span_len, width = array_in.shape
    return array_in.transpose(0, 2, 1, 3).reshape(spans * span_len, heads * width)


class Places:
    def __init__(self):
        self.nb = lax.axis_size("batch")
        self.ns = lax.axis_size("seq")
        self.b = lax.axis_index("batch")
        self.s = lax.axis_index("seq")
        self.c = self.s % PAIR
        self.t = self.s // PAIR
        self.chips = self.ns // PAIR
        self.ny = 2 if self.chips % 2 == 0 else 1
        self.nz = self.chips // self.ny
        self.y = self.t % self.ny
        self.z = self.t // self.ny

    def seq_hop(self, array_in, pairs):
        return lax.ppermute(array_in, "seq", pairs)

    def pair_hop(self, array_in):
        return self.seq_hop(array_in, [(i, i ^ 1) for i in range(self.ns)])

    def chip_shift(self, array_in, by):
        step = by * PAIR
        return self.seq_hop(
            array_in, [(i, i + step) for i in range(self.ns) if 0 <= i + step < self.ns]
        )

    def from_batch(self, array_in, k):
        nb = self.nb
        return lax.ppermute(array_in, "batch", [((d + k) % nb, d) for d in range(nb)])

    def others(self, array_in):
        return [self.from_batch(array_in, k) for k in range(1, self.nb)]

    def by_core(self, mine, other, axis):
        return jnp.where(
            self.c == 0,
            jnp.concatenate([mine, other], axis),
            jnp.concatenate([other, mine], axis),
        )

    def pair_all(self, mine, axis=0):
        return self.by_core(mine, self.pair_hop(mine), axis)

    def pair_sum(self, partial):
        rows = partial.shape[0] // PAIR
        own = lax.dynamic_slice_in_dim(partial, self.c * rows, rows, 0)
        away = lax.dynamic_slice_in_dim(partial, (1 - self.c) * rows, rows, 0)
        return own + self.pair_hop(away)

    def to_rel(self, array_in, axis):
        nb = self.nb
        width = array_in.shape[axis] // nb
        if nb == 2:
            low = lax.slice_in_dim(array_in, 0, width, axis=axis)
            high = lax.slice_in_dim(array_in, width, 2 * width, axis=axis)
            return jnp.where(
                self.b == 0,
                jnp.concatenate([low, high], axis),
                jnp.concatenate([high, low], axis),
            )
        return jnp.roll(array_in, -self.b * width, axis)

    def to_abs(self, array_in, axis):
        if self.nb == 2:
            return self.to_rel(array_in, axis)
        return jnp.roll(array_in, self.b * (array_in.shape[axis] // self.nb), axis)

    def total_sum(self, rel_rows):
        nb = self.nb
        total = rel_rows[0]
        for k in range(1, nb):
            total = total + self.from_batch(rel_rows[nb - k], k)
        step = 1
        while step < self.ns:
            total = total + self.seq_hop(total, [(i, i ^ step) for i in range(self.ns)])
            step *= 2
        return total


MESH_ID = pl.DeviceIdType.MESH


def plane_sum_kernel(ny, nz, jobs, *refs):
    nj = len(jobs)
    grads, sums, swapped = refs[:nj], refs[nj : 2 * nj], refs[2 * nj : 3 * nj]
    first_in, second_in, halfway = (refs[(3 + i) * nj : (4 + i) * nj] for i in range(3))
    send_sems, recv_sems = refs[6 * nj :]
    s = lax.axis_index("seq")
    t = s // PAIR
    y, z = lax.rem(t, ny), t // ny
    partner = s + 1 - 2 * lax.rem(s, PAIR)
    axes = {"y": (ny, y, PAIR), "z": (nz, z, PAIR * ny)}

    barrier = pltpu.get_barrier_semaphore()

    def signal(to):
        pl.semaphore_signal(barrier, inc=1, device_id={"seq": to}, device_id_type=MESH_ID)

    signal(partner)
    for n, pos, stride in axes.values():
        if n > 1:
            pl.when(pos > 0)(lambda: signal(s - stride))
            pl.when(pos < n - 1)(lambda: signal(s + stride))
    peers = 1
    for n, pos, stride in axes.values():
        peers = peers + (pos + n - 1) // n + (2 * n - 2 - pos) // n
    pl.semaphore_wait(barrier, peers)

    def add_blocks(dst, left, right):
        def one(i, carry):
            dst[i] = (left[i].astype(jnp.float32) + right[i].astype(jnp.float32)).astype(dst.dtype)
            return carry

        lax.fori_loop(0, dst.shape[0], one, 0)

    def line(job, phase, axis):
        n, pos, stride = axes[axis]
        ways = []
        for way in (0, 1):
            q = pos if way == 0 else n - 1 - pos
            to = s + stride if way == 0 else s - stride

            def real(m, way=way):
                return m if way == 0 else n - 1 - m

            def copy(src, dst, step, way=way, to=to):
                return pltpu.make_async_remote_copy(
                    src_ref=src,
                    dst_ref=dst,
                    send_sem=send_sems.at[job, phase, way, step - 1],
                    recv_sem=recv_sems.at[job, phase, way, step - 1],
                    device_id={"seq": to},
                    device_id_type=MESH_ID,
                )

            ways.append((q, real, copy, way))
        return n, pos, ways

    def scatter_stages(job, phase, axis, src, size, arrivals, finish):
        n, pos, ways = line(job, phase, axis)

        def block(i):
            return src.at[pl.ds(i * size, size)]

        def step_stage(step):
            for q, real, copy, way in ways:
                slot = arrivals.at[way, step - 1]

                @pl.when(q == 0)
                def _():
                    copy(block(real(n - step)), slot, step).start()

                if step > 1:
                    before = arrivals.at[way, step - 2]

                    @pl.when(jnp.logical_and(q >= 1, q <= min(step - 1, n - 2)))
                    def _():
                        copy(before, before, step - 1).wait_recv()
                        add_blocks(before, before, block(real(q + n - step)))
                        copy(before, slot, step).start()

        def last():
            dst = finish()
            own = block(pos)
            (q0, _, copy0, _), (q1, _, copy1, _) = ways
            last_r, last_l = arrivals.at[0, n - 2], arrivals.at[1, n - 2]

            @pl.when(q0 == 0)
            def _():
                copy1(last_l, last_l, n - 1).wait_recv()
                add_blocks(dst, own, last_l)

            @pl.when(q0 > 0)
            def _():
                copy0(last_r, last_r, n - 1).wait_recv()
                add_blocks(dst, own, last_r)

            if n > 2:

                @pl.when(jnp.logical_and(q0 > 0, q1 > 0))
                def _():
                    copy1(last_l, last_l, n - 1).wait_recv()
                    add_blocks(dst, dst, last_l)

        def drain():
            for step in range(1, n):
                for q, real, copy, way in ways:
                    slot = arrivals.at[way, step - 1]
                    pl.when(q <= min(step - 1, n - 2))(
                        lambda copy=copy, slot=slot, step=step: copy(slot, slot, step).wait_send()
                    )

        return [functools.partial(step_stage, i) for i in range(1, n)], last, drain

    def gather_stages(job, phase, axis, buf, base, size):
        n, pos, ways = line(job, phase, axis)

        def block(i):
            return buf.at[pl.ds(base + i * size, size)]

        def stage(step):
            for q, real, copy, way in ways:
                if step > 1:
                    here = block(real(q - step + 1))
                    pl.when(q >= step - 1)(
                        lambda copy=copy, here=here: copy(here, here, step - 1).wait_recv()
                    )
                if step < n:
                    here = block(real(q - step + 1))
                    pl.when(jnp.logical_and(q >= step - 1, q <= n - 2))(
                        lambda copy=copy, here=here: copy(here, here, step).start()
                    )

        def drain():
            for step in range(1, n):
                for q, real, copy, way in ways:
                    here = block(real(q - step + 1))
                    pl.when(jnp.logical_and(q >= step - 1, q <= n - 2))(
                        lambda copy=copy, here=here, step=step: copy(here, here, step).wait_send()
                    )

        return [functools.partial(stage, i) for i in range(1, n + 1)], drain

    plans, drains = [], []
    for job, (y_first, offset) in enumerate(jobs):
        one, two = ("y", "z") if y_first else ("z", "y")
        n_one, pos_one, _ = axes[one]
        n_two, pos_two, _ = axes[two]
        stages = []
        own_at = pos_one * n_two + pos_two
        source = grads[job]
        if n_one > 1:
            steps, last, drain = scatter_stages(
                job, 0, one, source, n_two, first_in[job], lambda job=job: halfway[job]
            )
            stages += steps
            drains.append(drain)
            close = last
        else:

            def close(job=job):
                def one_block(i, carry):
                    halfway[job][i] = grads[job][i]
                    return carry

                lax.fori_loop(0, halfway[job].shape[0], one_block, 0)

        if n_two > 1:
            steps, last, drain = scatter_stages(
                job,
                1,
                two,
                halfway[job],
                1,
                second_in[job],
                lambda job=job, own_at=own_at: sums[job].at[pl.ds(own_at, 1)],
            )
            drains.append(drain)
            stages.append(lambda close=close, step=steps[0]: (close(), step()))
            stages += steps[1:]
            close = last
        else:

            def close(job=job, own_at=own_at, before=close):
                before()
                sums[job][own_at] = halfway[job][0]

        gathers = []
        if n_two > 1:
            steps, drain = gather_stages(job, 2, two, sums[job], pos_one * n_two, 1)
            drains.append(drain)
            gathers += [steps]
        if n_one > 1:
            steps, drain = gather_stages(job, 3, one, sums[job], 0, n_two)
            drains.append(drain)
            gathers += [steps]
        pending = close
        for steps in gathers:
            stages.append(lambda pending=pending, step=steps[0]: (pending(), step()))
            stages += steps[1:-1]
            pending = steps[-1]

        def swap(job=job):
            return pltpu.make_async_remote_copy(
                src_ref=sums[job],
                dst_ref=swapped[job],
                send_sem=send_sems.at[job, 4, 0, 0],
                recv_sem=recv_sems.at[job, 4, 0, 0],
                device_id={"seq": partner},
                device_id_type=MESH_ID,
            )

        stages.append(lambda pending=pending, swap=swap: (pending(), swap().start()))
        drains.append(lambda swap=swap: swap().wait())
        plans.append((offset, stages))

    for tick in range(max(offset + len(stages) for offset, stages in plans)):
        for offset, stages in plans:
            if 0 <= tick - offset < len(stages):
                stages[tick - offset]()
    for drain in drains:
        drain()


def plane_sums(grads, jobs, ny, nz):
    longest = max(ny, nz) - 1
    scratch_one, scratch_two, scratch_mid = [], [], []
    for g, (y_first, _) in zip(grads, jobs):
        n_one, n_two = (ny, nz) if y_first else (nz, ny)
        tail = g.shape[1:]
        scratch_one.append(pltpu.VMEM((2, max(n_one - 1, 1), n_two) + tail, g.dtype))
        scratch_two.append(pltpu.VMEM((2, max(n_two - 1, 1), 1) + tail, g.dtype))
        scratch_mid.append(pltpu.VMEM((n_two,) + tail, g.dtype))
    sems = pltpu.SemaphoreType.DMA((len(grads), 5, 2, max(longest, 1)))
    outs = pl.pallas_call(
        functools.partial(plane_sum_kernel, ny, nz, tuple(jobs)),
        out_shape=[jax.ShapeDtypeStruct(g.shape, g.dtype) for g in grads] * 2,
        in_specs=[pl.BlockSpec(memory_space=pltpu.VMEM)] * len(grads),
        out_specs=[pl.BlockSpec(memory_space=pltpu.VMEM)] * (2 * len(grads)),
        scratch_shapes=scratch_one + scratch_two + scratch_mid + [sems, sems],
        compiler_params=pltpu.CompilerParams(
            collective_id=1, has_side_effects=True, vmem_limit_bytes=56 * 2**20
        ),
        name="plane_sums",
    )(*grads)
    return outs[: len(grads)], outs[len(grads) :]


def weight_kernel(pieces, down_at, *refs):
    n_in = 8
    ins, outs = refs[:n_in], refs[n_in : n_in + 7]
    local_sems, send_x, recv_x, send_p, recv_p = refs[n_in + 7 :]
    b, s = lax.axis_index("batch"), lax.axis_index("seq")
    c = lax.rem(s, PAIR)
    k = lax.rem(s // 2, 4)
    k_y = k + 1 - 2 * lax.rem(k, 2)
    k_z = k + 2 - 4 * (k // 2)
    k_far = 3 - k
    by_x = {"batch": 1 - b}
    by_y = {"seq": s + 2 * (k_y - k)}
    by_z = {"seq": s + 2 * (k_z - k)}

    barrier = pltpu.get_barrier_semaphore()
    for to in (by_x, by_y, by_z):
        pl.semaphore_signal(barrier, inc=1, device_id=to, device_id_type=MESH_ID)
    pl.semaphore_wait(barrier, 3)

    def source(arg, row_step, col_step, width, start, count):
        rows = pl.ds(pl.multiple_of(c * row_step + start, 16), count)
        if col_step:
            return ins[arg].at[rows, pl.ds(pl.multiple_of(c * col_step, 128), width)]
        return ins[arg].at[rows]

    def remote(src, dst, send, recv, to):
        return pltpu.make_async_remote_copy(
            src_ref=src, dst_ref=dst, send_sem=send, recv_sem=recv, device_id=to, device_id_type=MESH_ID
        )

    far_refs = [outs[1], outs[3], outs[5], outs[6]]
    groups = len(pieces)
    x_copies = []
    for g, group in enumerate(pieces):
        far = far_refs[g]
        quarter = far.shape[0] // 4
        mine = []
        for i, (arg, row_step, col_step, width, place) in enumerate(group):
            src = source(arg, row_step, col_step, width, k * quarter, quarter)
            rows = pl.ds(pl.multiple_of(k * quarter, 16), quarter)
            dst = far.at[rows, pl.ds(place, width)]
            mine.append(remote(src, dst, send_x.at[g, i], recv_x.at[g, i], by_x))
        x_copies.append(mine)

    is_sender, is_taker = c == b, c != b

    def guarded(g, taker, body):
        if g == down_at:
            pl.when(is_taker if taker else is_sender)(body)
        else:
            body()

    def start_x(g):
        for copy in x_copies[g]:
            copy.start()

    for g in range(groups):
        guarded(g, False, functools.partial(start_x, g))

    locals_ = []
    for g, group in enumerate(pieces):
        if g == down_at:
            continue
        own = outs[2 * g]
        for i, (arg, row_step, col_step, width, place) in enumerate(group):
            src = source(arg, row_step, col_step, width, 0, own.shape[0])
            locals_.append(
                pltpu.make_async_copy(src, own.at[:, pl.ds(place, width)], local_sems.at[g, i])
            )
    down_copy = pltpu.make_async_copy(ins[7], outs[6], local_sems.at[down_at, 0])
    for copy in locals_:
        copy.start()
    pl.when(is_sender)(down_copy.start)

    def rows_of(g, q, part):
        far = far_refs[g]
        quarter = far.shape[0] // 4
        if part is None:
            return far.at[pl.ds(pl.multiple_of(q * quarter, 16), quarter)]
        eighth = quarter // 2
        return far.at[pl.ds(pl.multiple_of(q * quarter + part * eighth, 16), eighth)]

    def hop(g, kind):
        at, to, q, part = (
            (0, by_y, k, None),
            (1, by_z, k, None),
            (2, by_y, k_z, 0),
            (3, by_z, k_y, 1),
        )[kind]
        ref = rows_of(g, q, part)
        return remote(ref, ref, send_p.at[g, at], recv_p.at[g, at], to)

    def arrived(g, kind):
        at, to, q, part = (
            (0, by_y, k_y, None),
            (1, by_z, k_z, None),
            (2, by_y, k_far, 0),
            (3, by_z, k_far, 1),
        )[kind]
        ref = rows_of(g, q, part)
        return remote(ref, ref, send_p.at[g, at], recv_p.at[g, at], to)

    def second(g):
        for copy in x_copies[g]:
            copy.wait_recv()
        hop(g, 0).start()
        hop(g, 1).start()

    def third(g):
        arrived(g, 1).wait_recv()
        hop(g, 2).start()
        arrived(g, 0).wait_recv()
        hop(g, 3).start()

    def final(g):
        arrived(g, 2).wait_recv()
        arrived(g, 3).wait_recv()
        for kind in range(4):
            hop(g, kind).wait_send()

    def x_sent(g):
        for copy in x_copies[g]:
            copy.wait_send()

    for g in range(groups + 1):
        if g < groups:
            guarded(g, True, functools.partial(second, g))
        if g > 0:
            guarded(g - 1, True, functools.partial(third, g - 1))
    for g in range(groups):
        guarded(g, True, functools.partial(final, g))
        guarded(g, False, functools.partial(x_sent, g))
    for copy in locals_:
        copy.wait()
    pl.when(is_sender)(down_copy.wait)


def fetch_weights(w_query, w_key, w_value, w_outgate, w_output, w_gate, w_up, w_down):
    half = lambda a: a.shape[1] // PAIR
    proj, place = [], 0
    for arg, a in enumerate((w_query, w_key, w_value, w_outgate)):
        proj.append((arg, 0, half(a), half(a), place))
        place += half(a)
    proj_shape = (w_query.shape[0], place)
    out_rows = w_output.shape[0] // PAIR
    out_piece = [(4, out_rows, 0, w_output.shape[1], 0)]
    gu = [(5, 0, half(w_gate), half(w_gate), 0), (6, 0, half(w_up), half(w_up), half(w_gate))]
    gu_shape = (w_gate.shape[0], 2 * half(w_gate))
    down = [(7, 0, 0, w_down.shape[1], 0)]
    shapes = [proj_shape] * 2 + [(out_rows, w_output.shape[1])] * 2 + [gu_shape] * 2 + [w_down.shape]
    any_spec = pl.BlockSpec(memory_space=pl.ANY)
    sem = pltpu.SemaphoreType.DMA((4, 4))
    return pl.pallas_call(
        functools.partial(weight_kernel, (proj, out_piece, gu, down), 3),
        out_shape=[jax.ShapeDtypeStruct(shape, w_query.dtype) for shape in shapes],
        in_specs=[any_spec] * 8,
        out_specs=[pl.BlockSpec(memory_space=pltpu.VMEM)] * 7,
        scratch_shapes=[sem] * 5,
        compiler_params=pltpu.CompilerParams(
            collective_id=0, has_side_effects=True, vmem_limit_bytes=40 * 2**20
        ),
        name="fetch_weights",
    )(w_query, w_key, w_value, w_outgate, w_output, w_gate, w_up, w_down)


def core_cols(array_in, c):
    width = array_in.shape[1] // PAIR
    return lax.dynamic_slice_in_dim(array_in, c * width, width, 1)


def dot32(a, b):
    return jnp.dot(a, b, preferred_element_type=jnp.float32)


def dot_t(a, b):
    return lax.dot_general(a, b, (((1,), (1,)), ((), ())), preferred_element_type=jnp.float32)


def grad_dot(pairs_in):
    total = None
    for left, right in pairs_in:
        part = lax.dot_general(
            left, right, (((0,), (0,)), ((), ())), preferred_element_type=jnp.float32
        )
        total = part if total is None else total + part
    return total


def per_device(
    inputs,
    seg_ids,
    gain_attn,
    w_query,
    w_key,
    w_value,
    w_outgate,
    w_rank_in,
    w_rank_out,
    rank_bias,
    head_gain,
    w_output,
    gain_ffn,
    w_gate,
    w_up,
    w_down,
    cotangent,
):
    f32 = jnp.float32
    bf16 = jnp.bfloat16
    at_place = Places()
    nb, b, c, t = at_place.nb, at_place.b, at_place.c, at_place.t
    rank = w_rank_in.shape[1]
    heads = HEADS // PAIR
    keys_w, vals_w = KEYS // PAIR, VALS // PAIR
    dim = inputs.shape[2]
    dim_own = dim // nb

    in_pair = at_place.pair_all(inputs[0])
    seg_row = at_place.pair_all(seg_ids[0])
    tok_count = seg_row.shape[0]
    half_tok = tok_count // PAIR
    spans = tok_count // SPAN
    edges = jnp.stack([seg_row[0], seg_row[-1]])
    edges_wide = jnp.broadcast_to(edges[:, None], (2, 128)).astype(f32)
    prev_last = at_place.chip_shift(edges_wide, 1)[1, 0]
    next_first = at_place.chip_shift(edges_wide, -1)[0, 0]
    first_id, last_id = edges[0].astype(f32), edges[1].astype(f32)
    from_prev = jnp.logical_and(t > 0, prev_last == first_id).astype(f32)
    to_next = jnp.logical_and(t < at_place.chips - 1, next_first == last_id).astype(f32)
    whole_doc = (first_id == last_id).astype(f32)

    small = (gain_attn, gain_ffn, rank_bias, head_gain, w_rank_in, w_rank_out)
    packed = jnp.concatenate([a.reshape(-1) for a in small])
    packed = jnp.stack([packed] + at_place.others(packed))
    parts, at = [], 0
    for a in small:
        parts.append(packed[:, at : at + a.size])
        at += a.size
    gain_one = parts[0].reshape(-1).astype(f32)
    gain_two = parts[1].reshape(-1).astype(f32)
    bias_all = at_place.to_abs(parts[2], 0).reshape(-1).astype(f32)
    bias_w = lax.dynamic_slice_in_dim(bias_all, c * keys_w, keys_w)
    head_gain32 = at_place.to_abs(parts[3], 0).reshape(-1).astype(f32)
    rank_in_w = parts[4].reshape(-1, rank)
    rank_out_all = (
        at_place.to_abs(parts[5], 0).reshape((nb,) + w_rank_out.shape).transpose(1, 0, 2)
        .reshape(rank, -1)
    )
    rank_out_w = core_cols(rank_out_all, c).astype(f32)

    weights = (w_query, w_key, w_value, w_outgate, w_output, w_gate, w_up, w_down)
    if nb == 2 and at_place.ns % 8 == 0:
        proj_own, proj_far, out_own, out_far, gu_own, gu_far, down_w = fetch_weights(*weights)
    else:
        proj_own = jnp.concatenate(
            [core_cols(a, c) for a in (w_query, w_key, w_value, w_outgate)], axis=1
        )
        out_own = lax.dynamic_slice_in_dim(w_output, c * vals_w, vals_w, 0)
        gu_own = jnp.concatenate([core_cols(w_gate, c), core_cols(w_up, c)], axis=1)
        proj_far, out_far, gu_far, down_far = (
            jnp.concatenate(at_place.others(a), axis=0) for a in (proj_own, out_own, gu_own, w_down)
        )
        down_all = at_place.to_abs(jnp.concatenate([w_down, down_far], axis=0), 0)
        ff_half = down_all.shape[0] // PAIR
        down_w = lax.dynamic_slice_in_dim(down_all, c * ff_half, ff_half, 0)
    ff_c = down_w.shape[0]

    cot_own = cotangent[0]
    cot_pair = at_place.pair_all(cot_own)
    cot_far = [at_place.pair_all(a) for a in at_place.others(cot_own)]

    activation = at_place.to_rel(in_pair, 1).astype(f32)
    scale_one = rms_scale(activation)
    unit_one = activation * scale_one
    normed = (unit_one * gain_one).astype(bf16)
    normed_far = [
        at_place.from_batch(normed[:, (nb - k) * dim_own : (nb - k + 1) * dim_own], k)
        for k in range(1, nb)
    ]

    low_rank = dot32(normed, rank_in_w)
    logits = jnp.dot(low_rank, rank_out_w, precision=top_prec) + bias_w
    decays = jax.nn.log_sigmoid(logits) / 16.0

    seg_s = seg_row.reshape(spans, SPAN)
    first_s, last_s = seg_s[:, 0], seg_s[:, -1]
    row_pos = lax.broadcasted_iota(jnp.int32, (SPAN, SPAN), 0)
    col_pos = lax.broadcasted_iota(jnp.int32, (SPAN, SPAN), 1)
    lower = (col_pos <= row_pos).astype(f32)
    allowed = lower[None] * (seg_s[:, :, None] == seg_s[:, None, :]).astype(f32)
    allowed = allowed[:, None]
    prior = jnp.concatenate([seg_row[:1], last_s[:-1]])
    enters = (first_s == prior).astype(f32)
    within = ((seg_s == first_s[:, None]).astype(f32) * enters[:, None])[:, None, :, None]
    end_doc = (seg_s == last_s[:, None]).astype(f32)[:, None, :, None]

    cumul = mm("ts,nsc->ntc", lower, decays.reshape(spans, SPAN, keys_w))
    total_log = jnp.sum(cumul[:, -1], axis=0)

    proj = dot32(normed[:, :dim_own], proj_own) + dot32(normed[:, dim_own:], proj_far)
    queries = to_spans(proj[:, :keys_w] * DK ** (-0.5), DK)
    keys_s = to_spans(proj[:, keys_w : 2 * keys_w], DK)
    values_s = to_spans(proj[:, 2 * keys_w : 2 * keys_w + vals_w], DV)
    outgate = proj[:, 2 * keys_w + vals_w :]

    cumul = cumul.reshape(spans, SPAN, heads, DK).transpose(0, 2, 1, 3)
    last_cumul = cumul[:, :, -1:, :]
    grow = jnp.exp(cumul)
    shrink = jnp.exp(-cumul)
    to_end = jnp.exp(last_cumul - cumul) * end_doc
    query_dec = queries * grow
    key_dec = keys_s * shrink
    key_end = keys_s * to_end
    query_in = query_dec * within
    keep = jnp.exp(last_cumul[:, :, 0, :]) * within[:, :, -1]
    scores = mm("nhtc,nhsc->nhts", query_dec, key_dec) * allowed
    local_out = mm("nhts,nhsv->nhtv", scores, values_s)
    added = mm("nhsc,nhsv->nhcv", key_end, values_s)

    local_state = added[0]
    for i in range(1, spans):
        local_state = keep[i][:, :, None] * local_state + added[i]

    reach_chips = -(-(SEG_MOST - 1) // tok_count)

    def chip_scan(state, factor, way):
        state = state.reshape(heads * DK, DV)
        step = 1
        pad = jnp.zeros((15, heads * DK), f32)
        while step < min(reach_chips, at_place.chips):
            packed = jnp.concatenate(
                [state, jnp.concatenate([factor[None], pad]).reshape(-1, DV)]
            )
            got = at_place.chip_shift(packed.astype(bf16), way * step).astype(f32)
            state = state + factor[:, None] * got[: heads * DK]
            factor = factor * got[heads * DK :].reshape(16, -1)[0]
            step *= 2
        got = at_place.chip_shift(state.astype(bf16), way)
        return got.astype(f32).reshape(heads, DK, DV)

    block_keep = jnp.exp(total_log) * whole_doc
    carried = from_prev * chip_scan(local_state, block_keep * from_prev, 1)
    enter_list = [carried]
    for i in range(spans - 1):
        enter_list.append(keep[i][:, :, None] * enter_list[i] + added[i])
    entered = jnp.stack(enter_list)

    attn_raw = from_spans(local_out + mm("nhtc,nhcv->nhtv", query_in, entered)).reshape(
        tok_count, heads, DV
    )
    head_scale = head_rms(attn_raw)
    head_norm = attn_raw * head_scale
    gate_h = outgate.reshape(tok_count, heads, DV)
    gate_sig = jax.nn.sigmoid(gate_h)
    gate_act = gate_h * gate_sig
    gated = (head_norm * head_gain32 * gate_act).reshape(tok_count, vals_w).astype(bf16)
    gated_far = at_place.others(gated)
    out_w = jnp.concatenate(
        [out_own] + [out_far[k * vals_w : (k + 1) * vals_w] for k in range(nb - 1)], axis=1
    )
    own_rows = lambda a: lax.dynamic_slice_in_dim(a, c * half_tok, half_tok, 0)
    resid = own_rows(activation) + at_place.pair_sum(dot32(gated, out_w))
    scale_two = rms_scale(resid)
    unit_two = resid * scale_two
    normed_two = (unit_two * gain_two).astype(bf16)

    two_pair = at_place.pair_all(normed_two)
    two_far = [
        at_place.pair_all(jnp.roll(a, (k + 1) * dim_own, 1))
        for k, a in enumerate(at_place.others(normed_two))
    ]

    def feed_forward(two_rows, cot_rows):
        pre = dot32(two_rows[:, :dim_own], gu_own) + dot32(two_rows[:, dim_own:], gu_far)
        gate_pre, up_pre = pre[:, :ff_c], pre[:, ff_c:]
        sig = jax.nn.sigmoid(gate_pre)
        hidden = (gate_pre * sig * up_pre).astype(bf16)
        grad_hidden = dot_t(cot_rows, down_w)
        grad_gu = jnp.concatenate(
            [
                (grad_hidden * up_pre * silu_grad(gate_pre, sig)).astype(bf16),
                (grad_hidden * gate_pre * sig).astype(bf16),
            ],
            axis=1,
        )
        return hidden, grad_gu

    hidden, grad_gu = feed_forward(two_pair, cot_pair)
    down_sum = at_place.pair_sum(dot32(hidden, down_w))
    output = (at_place.to_abs(resid, 1) + down_sum).astype(bf16)

    two_grad = jnp.concatenate([dot_t(grad_gu, gu_own), dot_t(grad_gu, gu_far)], axis=1)
    grad_two = at_place.pair_sum(two_grad)

    hid_own = [at_place.pair_all(hidden, 1)]
    gu_pairs = [(two_pair[:, :dim_own], grad_gu)]
    down_cots = [cot_pair]
    for two_rows, cot_rows in zip(two_far, cot_far):
        far_hidden, far_grad = feed_forward(two_rows, cot_rows)
        gu_pairs.append((two_rows[:, :dim_own], far_grad))
        hid_own.append(at_place.pair_all(far_hidden, 1))
        down_cots.append(cot_rows)
    ff_own = hid_own[0].shape[1] // nb
    down_pairs = [
        (lax.dynamic_slice_in_dim(h, b * ff_own, ff_own, 1), core_cols(g, c))
        for h, g in zip(hid_own, down_cots)
    ]
    part_gate = grad_dot([(left, right[:, :ff_c]) for left, right in gu_pairs]).astype(bf16)
    part_up = grad_dot([(left, right[:, ff_c:]) for left, right in gu_pairs]).astype(bf16)
    part_down = grad_dot(down_pairs).astype(bf16)

    grad_gain_two = jnp.sum(grad_two * unit_two, axis=0)
    scaled_two = grad_two * gain_two
    grad_resid = at_place.to_rel(cot_own, 1).astype(f32) + scale_two * (
        scaled_two - unit_two * jnp.mean(scaled_two * unit_two, axis=-1, keepdims=True)
    )
    resid_pair = at_place.pair_all(grad_resid.astype(bf16))
    resid_far = [
        at_place.from_batch(resid_pair[:, (nb - k) * dim_own : (nb - k + 1) * dim_own], k)
        for k in range(1, nb)
    ]
    part_out = grad_dot(
        [(gated, resid_pair[:, :dim_own])] + list(zip(gated_far, resid_far))
    ).astype(bf16)
    grad_gated = dot_t(resid_pair, out_w).reshape(tok_count, heads, DV)
    grad_headgain = jnp.sum(grad_gated * head_norm * gate_act, axis=(0, 1))
    grad_gate_h = grad_gated * head_norm * head_gain32 * silu_grad(gate_h, gate_sig)
    grad_norm_h = grad_gated * head_gain32 * gate_act
    grad_attn = head_scale * (
        grad_norm_h - head_norm * jnp.mean(grad_norm_h * head_norm, axis=-1, keepdims=True)
    )
    grad_o = to_spans(grad_attn.reshape(tok_count, vals_w), DV)

    reach_grad = mm("nhtc,nhtv->nhcv", query_in, grad_o)
    local_grad = reach_grad[spans - 1]
    for i in range(spans - 2, -1, -1):
        local_grad = keep[i][:, :, None] * local_grad + reach_grad[i]
    grad_end = to_next * chip_scan(local_grad, block_keep * to_next, -1)

    grad_scores = mm("nhtv,nhsv->nhts", grad_o, values_s) * allowed
    grad_qd = mm("nhts,nhsc->nhtc", grad_scores, key_dec)
    grad_qd = grad_qd + within * mm("nhtv,nhcv->nhtc", grad_o, entered)
    grad_kd = mm("nhts,nhtc->nhsc", grad_scores, query_dec)
    grad_v = mm("nhts,nhtv->nhsv", scores, grad_o)

    end_list = [grad_end]
    for i in range(spans - 1, 0, -1):
        end_list.append(keep[i][:, :, None] * end_list[-1] + reach_grad[i])
    ends = jnp.stack(end_list[::-1])

    grad_v = grad_v + mm("nhsc,nhcv->nhsv", key_end, ends)
    grad_ke = mm("nhsv,nhcv->nhsc", values_s, ends)
    moved = grad_ke * key_end
    grad_last = jnp.sum(moved, axis=2) + keep * jnp.sum(ends * entered, axis=3)
    grad_cumul = grad_qd * query_dec - grad_kd * key_dec - moved
    grad_d = mm("ts,nhtc->nhsc", lower, grad_cumul) + grad_last[:, :, None, :]
    grad_q = grad_qd * grow
    grad_k = grad_kd * shrink + grad_ke * to_end

    grad_logits = from_spans(grad_d) * jax.nn.sigmoid(-logits) / 16.0
    grad_bias = jnp.sum(grad_logits, axis=0)
    grad_rank_out = jnp.dot(low_rank.T, grad_logits, precision=top_prec)
    grad_low = jnp.dot(grad_logits, rank_out_w.T, precision=top_prec).astype(bf16)
    proj_grad = jnp.concatenate(
        [
            from_spans(grad_q * DK ** (-0.5)).astype(bf16),
            from_spans(grad_k).astype(bf16),
            from_spans(grad_v).astype(bf16),
            grad_gate_h.reshape(tok_count, vals_w).astype(bf16),
        ],
        axis=1,
    )
    proj_grad_far = at_place.others(proj_grad)
    part_proj = grad_dot(
        [(normed[:, :dim_own], proj_grad)] + list(zip(normed_far, proj_grad_far))
    ).astype(bf16)
    normed_grad = jnp.concatenate(
        [dot_t(proj_grad, proj_own), dot_t(proj_grad, proj_far)], axis=1
    ) + dot_t(grad_low, rank_in_w)
    grad_normed = at_place.pair_sum(normed_grad)
    unit_own = own_rows(unit_one)
    grad_gain_one = jnp.sum(grad_normed * unit_own, axis=0)
    scaled_one = grad_normed * gain_one
    grad_input = (
        grad_resid
        + own_rows(scale_one)
        * (scaled_one - unit_own * jnp.mean(scaled_one * unit_own, axis=-1, keepdims=True))
    ).astype(bf16)
    grad_rank_in = grad_dot([(normed, grad_low)])

    def own_slot(part):
        return at_place.by_core(part, jnp.zeros_like(part), part.ndim - 1)

    by_owner = jnp.concatenate(
        [
            grad_gain_one.reshape(nb, -1),
            grad_gain_two.reshape(nb, -1),
            at_place.to_rel(own_slot(grad_bias).reshape(nb, -1), 0),
            at_place.to_rel(grad_headgain.reshape(nb, -1), 0),
            grad_rank_in.reshape(nb, -1),
            at_place.to_rel(
                own_slot(grad_rank_out).reshape(rank, nb, -1).transpose(1, 0, 2).reshape(nb, -1), 0
            ),
        ],
        axis=1,
    )
    owned = at_place.total_sum(by_owner)
    outs, at = [], 0
    for a in small:
        outs.append(owned[at : at + a.size].reshape(a.shape))
        at += a.size
    g_gain_one, g_gain_two, g_bias, g_headgain, g_rank_in, g_rank_out = outs

    chunks = at_place.chips
    parts = [part_gate, part_down, part_up, part_out, part_proj]
    jobs = ((True, 0), (False, 0), (True, 1), (False, 2), (True, 2))
    mine, theirs = plane_sums(
        [a.reshape(chunks, -1, a.shape[1]) for a in parts], jobs, at_place.ny, at_place.nz
    )
    mine = [a.reshape(-1, a.shape[2]) for a in mine]
    theirs = [a.reshape(-1, a.shape[2]) for a in theirs]

    def both(i, lo, hi, axis=1):
        return at_place.by_core(mine[i][:, lo:hi], theirs[i][:, lo:hi], axis).astype(f32)

    g_gate = both(0, 0, ff_c)
    g_down = both(1, 0, part_down.shape[1])
    g_up = both(2, 0, ff_c)
    g_output = both(3, 0, part_out.shape[1], 0)
    g_query = both(4, 0, keys_w)
    g_key = both(4, keys_w, 2 * keys_w)
    g_value = both(4, 2 * keys_w, 2 * keys_w + vals_w)
    g_outgate = both(4, 2 * keys_w + vals_w, 2 * keys_w + 2 * vals_w)
    return (
        output[None],
        at_place.to_abs(grad_input, 1)[None],
        g_gain_one,
        g_query,
        g_key,
        g_value,
        g_outgate,
        g_rank_in,
        g_rank_out,
        g_bias,
        g_headgain,
        g_output,
        g_gain_two,
        g_gate,
        g_up,
        g_down,
    )


def solution(mesh):
    in_specs = (
        P("batch", "seq", None),
        P("batch", "seq"),
        P("batch"),
        P("batch", None),
        P("batch", None),
        P("batch", None),
        P("batch", None),
        P("batch", None),
        P(None, "batch"),
        P("batch"),
        P("batch"),
        P(None, "batch"),
        P("batch"),
        P("batch", None),
        P("batch", None),
        P("batch", None),
        P("batch", "seq", None),
    )
    out_specs = (
        P("batch", "seq", None),
        P("batch", "seq", None),
        P("batch"),
        P("batch", None),
        P("batch", None),
        P("batch", None),
        P("batch", None),
        P("batch", None),
        P(None, "batch"),
        P("batch"),
        P("batch"),
        P(None, "batch"),
        P("batch"),
        P("batch", None),
        P("batch", None),
        P("batch", None),
    )
    return jax.shard_map(
        per_device, mesh=mesh, in_specs=in_specs, out_specs=out_specs, check_vma=False
    )
```

```python
import functools

import jax
import jax.numpy as jnp
from jax import lax
from jax.experimental import pallas as pl
from jax.experimental.pallas import tpu as pltpu
from jax.sharding import PartitionSpec as P

HEADS = 4
DK = 128
DV = 256
SPAN = 64
KEYS = 512
VALS = 1024


norm_eps = 1e-05
head_eps = 0.1
top_prec = lax.Precision.HIGHEST
BOTH = ("batch", "seq")
SEG_MOST = 1024
PAIR = 2


def rms_scale(values_in):
    return lax.rsqrt(jnp.mean(values_in * values_in, axis=-1, keepdims=True) + norm_eps)


def head_rms(values_in):
    return lax.rsqrt(jnp.mean(values_in * values_in, axis=-1, keepdims=True) + head_eps)


def silu_grad(pre_act, sig_val):
    return sig_val * (1.0 + pre_act * (1.0 - sig_val))


def mm(eq, a, b):
    return jnp.einsum(eq, a, b, precision=top_prec)


def to_spans(array_in, width):
    return array_in.reshape(-1, SPAN, array_in.shape[1] // width, width).transpose(0, 2, 1, 3)


def from_spans(array_in):
    spans, heads, span_len, width = array_in.shape
    return array_in.transpose(0, 2, 1, 3).reshape(spans * span_len, heads * width)


class Places:
    def __init__(self):
        self.nb = lax.axis_size("batch")
        self.ns = lax.axis_size("seq")
        self.b = lax.axis_index("batch")
        self.s = lax.axis_index("seq")
        self.c = self.s % PAIR
        self.t = self.s // PAIR
        self.chips = self.ns // PAIR
        self.ny = 2 if self.chips % 2 == 0 else 1
        self.nz = self.chips // self.ny
        self.y = self.t % self.ny
        self.z = self.t // self.ny

    def seq_hop(self, array_in, pairs):
        return lax.ppermute(array_in, "seq", pairs)

    def pair_hop(self, array_in):
        return self.seq_hop(array_in, [(i, i ^ 1) for i in range(self.ns)])

    def chip_shift(self, array_in, by):
        step = by * PAIR
        return self.seq_hop(
            array_in, [(i, i + step) for i in range(self.ns) if 0 <= i + step < self.ns]
        )

    def from_batch(self, array_in, k):
        nb = self.nb
        return lax.ppermute(array_in, "batch", [((d + k) % nb, d) for d in range(nb)])

    def others(self, array_in):
        return [self.from_batch(array_in, k) for k in range(1, self.nb)]

    def by_core(self, mine, other, axis):
        return jnp.where(
            self.c == 0,
            jnp.concatenate([mine, other], axis),
            jnp.concatenate([other, mine], axis),
        )

    def pair_all(self, mine, axis=0):
        return self.by_core(mine, self.pair_hop(mine), axis)

    def pair_sum(self, partial):
        rows = partial.shape[0] // PAIR
        own = lax.dynamic_slice_in_dim(partial, self.c * rows, rows, 0)
        away = lax.dynamic_slice_in_dim(partial, (1 - self.c) * rows, rows, 0)
        return own + self.pair_hop(away)

    def to_rel(self, array_in, axis):
        nb = self.nb
        width = array_in.shape[axis] // nb
        if nb == 2:
            low = lax.slice_in_dim(array_in, 0, width, axis=axis)
            high = lax.slice_in_dim(array_in, width, 2 * width, axis=axis)
            return jnp.where(
                self.b == 0,
                jnp.concatenate([low, high], axis),
                jnp.concatenate([high, low], axis),
            )
        return jnp.roll(array_in, -self.b * width, axis)

    def to_abs(self, array_in, axis):
        if self.nb == 2:
            return self.to_rel(array_in, axis)
        return jnp.roll(array_in, self.b * (array_in.shape[axis] // self.nb), axis)

    def total_sum(self, rel_rows):
        nb = self.nb
        total = rel_rows[0]
        for k in range(1, nb):
            total = total + self.from_batch(rel_rows[nb - k], k)
        step = 1
        while step < self.ns:
            total = total + self.seq_hop(total, [(i, i ^ step) for i in range(self.ns)])
            step *= 2
        return total


MESH_ID = pl.DeviceIdType.MESH


def plane_plans(ny, nz, jobs, grads, sums, swapped, first_in, second_in, halfway, sems, greet):
    send_sems, recv_sems = sems
    s = lax.axis_index("seq")
    t = s // PAIR
    y, z = lax.rem(t, ny), t // ny
    partner = s + 1 - 2 * lax.rem(s, PAIR)
    axes = {"y": (ny, y, PAIR), "z": (nz, z, PAIR * ny)}

    barrier = pltpu.get_barrier_semaphore()

    def signal(to, axis="seq"):
        pl.semaphore_signal(barrier, inc=1, device_id={axis: to}, device_id_type=MESH_ID)

    signal(partner)
    distances, nb = greet
    chips = ny * nz
    b = lax.axis_index("batch")
    for k in range(1, nb):
        signal(lax.rem(b + k, nb), "batch")
    for d in distances:
        pl.when(t >= d)(lambda: signal(s - PAIR * d))
        pl.when(t < chips - d)(lambda: signal(s + PAIR * d))
    for n, pos, stride in axes.values():
        if n > 1:
            pl.when(pos > 0)(lambda: signal(s - stride))
            pl.when(pos < n - 1)(lambda: signal(s + stride))
    peers = nb
    for n, pos, stride in axes.values():
        peers = peers + (pos + n - 1) // n + (2 * n - 2 - pos) // n
    for d in distances:
        peers = peers + (t + chips - d) // chips + (2 * chips - 1 - d - t) // chips
    pl.semaphore_wait(barrier, peers)

    def add_blocks(dst, left, right):
        def one(i, carry):
            dst[i] = (left[i].astype(jnp.float32) + right[i].astype(jnp.float32)).astype(dst.dtype)
            return carry

        lax.fori_loop(0, dst.shape[0], one, 0)

    def line(job, phase, axis):
        n, pos, stride = axes[axis]
        ways = []
        for way in (0, 1):
            q = pos if way == 0 else n - 1 - pos
            to = s + stride if way == 0 else s - stride

            def real(m, way=way):
                return m if way == 0 else n - 1 - m

            def copy(src, dst, step, way=way, to=to):
                return pltpu.make_async_remote_copy(
                    src_ref=src,
                    dst_ref=dst,
                    send_sem=send_sems.at[job, phase, way, step - 1],
                    recv_sem=recv_sems.at[job, phase, way, step - 1],
                    device_id={"seq": to},
                    device_id_type=MESH_ID,
                )

            ways.append((q, real, copy, way))
        return n, pos, ways

    def scatter_stages(job, phase, axis, src, size, arrivals, finish):
        n, pos, ways = line(job, phase, axis)

        def block(i):
            return src.at[pl.ds(i * size, size)]

        def step_stage(step):
            for q, real, copy, way in ways:
                slot = arrivals.at[way, step - 1]

                @pl.when(q == 0)
                def _():
                    copy(block(real(n - step)), slot, step).start()

                if step > 1:
                    before = arrivals.at[way, step - 2]

                    @pl.when(jnp.logical_and(q >= 1, q <= min(step - 1, n - 2)))
                    def _():
                        copy(before, before, step - 1).wait_recv()
                        add_blocks(before, before, block(real(q + n - step)))
                        copy(before, slot, step).start()

        def last():
            dst = finish()
            own = block(pos)
            (q0, _, copy0, _), (q1, _, copy1, _) = ways
            last_r, last_l = arrivals.at[0, n - 2], arrivals.at[1, n - 2]

            @pl.when(q0 == 0)
            def _():
                copy1(last_l, last_l, n - 1).wait_recv()
                add_blocks(dst, own, last_l)

            @pl.when(q0 > 0)
            def _():
                copy0(last_r, last_r, n - 1).wait_recv()
                add_blocks(dst, own, last_r)

            if n > 2:

                @pl.when(jnp.logical_and(q0 > 0, q1 > 0))
                def _():
                    copy1(last_l, last_l, n - 1).wait_recv()
                    add_blocks(dst, dst, last_l)

        def drain():
            for step in range(1, n):
                for q, real, copy, way in ways:
                    slot = arrivals.at[way, step - 1]
                    pl.when(q <= min(step - 1, n - 2))(
                        lambda copy=copy, slot=slot, step=step: copy(slot, slot, step).wait_send()
                    )

        return [functools.partial(step_stage, i) for i in range(1, n)], last, drain

    def gather_stages(job, phase, axis, buf, base, size):
        n, pos, ways = line(job, phase, axis)

        def block(i):
            return buf.at[pl.ds(base + i * size, size)]

        def stage(step):
            for q, real, copy, way in ways:
                if step > 1:
                    here = block(real(q - step + 1))
                    pl.when(q >= step - 1)(
                        lambda copy=copy, here=here: copy(here, here, step - 1).wait_recv()
                    )
                if step < n:
                    here = block(real(q - step + 1))
                    pl.when(jnp.logical_and(q >= step - 1, q <= n - 2))(
                        lambda copy=copy, here=here: copy(here, here, step).start()
                    )

        def drain():
            for step in range(1, n):
                for q, real, copy, way in ways:
                    here = block(real(q - step + 1))
                    pl.when(jnp.logical_and(q >= step - 1, q <= n - 2))(
                        lambda copy=copy, here=here, step=step: copy(here, here, step).wait_send()
                    )

        return [functools.partial(stage, i) for i in range(1, n + 1)], drain

    plans, drains = [], []
    for job, (y_first, offset) in enumerate(jobs):
        one, two = ("y", "z") if y_first else ("z", "y")
        n_one, pos_one, _ = axes[one]
        n_two, pos_two, _ = axes[two]
        stages = []
        own_at = pos_one * n_two + pos_two
        source = grads[job]
        if n_one > 1:
            steps, last, drain = scatter_stages(
                job, 0, one, source, n_two, first_in[job], lambda job=job: halfway[job]
            )
            stages += steps
            drains.append(drain)
            close = last
        else:

            def close(job=job):
                def one_block(i, carry):
                    halfway[job][i] = grads[job][i]
                    return carry

                lax.fori_loop(0, halfway[job].shape[0], one_block, 0)

        if n_two > 1:
            steps, last, drain = scatter_stages(
                job,
                1,
                two,
                halfway[job],
                1,
                second_in[job],
                lambda job=job, own_at=own_at: sums[job].at[pl.ds(own_at, 1)],
            )
            drains.append(drain)
            stages.append(lambda close=close, step=steps[0]: (close(), step()))
            stages += steps[1:]
            close = last
        else:

            def close(job=job, own_at=own_at, before=close):
                before()
                sums[job][own_at] = halfway[job][0]

        gathers = []
        if n_two > 1:
            steps, drain = gather_stages(job, 2, two, sums[job], pos_one * n_two, 1)
            drains.append(drain)
            gathers += [steps]
        if n_one > 1:
            steps, drain = gather_stages(job, 3, one, sums[job], 0, n_two)
            drains.append(drain)
            gathers += [steps]
        pending = close
        for steps in gathers:
            stages.append(lambda pending=pending, step=steps[0]: (pending(), step()))
            stages += steps[1:-1]
            pending = steps[-1]

        def swap(job=job):
            return pltpu.make_async_remote_copy(
                src_ref=sums[job],
                dst_ref=swapped[job],
                send_sem=send_sems.at[job, 4, 0, 0],
                recv_sem=recv_sems.at[job, 4, 0, 0],
                device_id={"seq": partner},
                device_id_type=MESH_ID,
            )

        stages.append(lambda pending=pending, swap=swap: (pending(), swap().start()))
        drains.append(lambda swap=swap: swap().wait())
        plans.append((offset, stages))

    return plans, drains


def high(a, b, dims=((1,), (0,))):
    return lax.dot_general(
        a, b, (dims, ((), ())), precision=top_prec, preferred_element_type=jnp.float32
    )


ROWS_OF = ((1,), (1,))
COLS_OF = ((0,), (0,))
BACK_IN = (
    ("gate_part", "down_part", "up_part", "resid_pair")
    + ("resid_far", "gated", "gated_far", "out_w")
    + ("attn", "outgate", "head_gain", "queries")
    + ("keys", "values", "cumul", "entered")
    + ("mask", "within", "end_doc", "keep")
    + ("factors", "to_next", "logits", "normed")
    + ("normed_far", "proj_own", "proj_far")
)
BACK_OUT = (
    ("normed_grad", "grad_logits", "grad_headgain")
)
BACK_TMP = (
    ("out_part", "proj_part", "grad_o", "reach")
    + ("grad_qd", "grad_kd", "grad_v", "proj_grad")
    + ("proj_grad_far", "proj_acc")
)


def back_kernel(ny, nz, nb, steps, jobs, at_tick, *refs):
    f32, bf16 = jnp.float32, jnp.bfloat16
    nj = len(jobs)
    refs = list(refs)

    def take(n):
        out = refs[:n]
        del refs[:n]
        return out

    r = dict(zip(BACK_IN, take(len(BACK_IN))))
    sums, swapped = take(nj), take(nj)
    r.update(zip(BACK_OUT, take(len(BACK_OUT))))
    first_in, second_in, halfway = take(nj), take(nj), take(nj)
    r.update(zip(BACK_TMP, take(len(BACK_TMP))))
    going, coming = take(2)
    sems, scan_sems, batch_sems = take(2), take(2), take(2)
    grads = [r["gate_part"], r["down_part"], r["up_part"], r["out_part"], r["proj_part"]]
    plans, drains = plane_plans(
        ny, nz, jobs, grads, sums, swapped, first_in, second_in, halfway, sems, (steps, nb)
    )
    s, b = lax.axis_index("seq"), lax.axis_index("batch")
    t = s // PAIR
    chips = ny * nz
    spans = r["entered"].shape[0]
    heads = r["queries"].shape[1] // DK
    keys_w, vals_w = heads * DK, heads * DV
    dim_own = r["resid_far"].shape[2]

    def put_chunks(ref, value):
        rows = ref.shape[1]
        for i in range(ref.shape[0]):
            ref[i] = value[i * rows : (i + 1) * rows].astype(ref.dtype)

    def out_grad():
        total = lax.dot_general(
            r["gated"][...], r["resid_pair"][:, :dim_own], (COLS_OF, ((), ())),
            preferred_element_type=f32,
        )
        for k in range(nb - 1):
            total = total + lax.dot_general(
                r["gated_far"][k], r["resid_far"][k], (COLS_OF, ((), ())),
                preferred_element_type=f32,
            )
        put_chunks(r["out_part"], total)

    def head_back():
        gains = r["head_gain"][...]
        total = jnp.zeros_like(gains)
        for h in range(heads):
            cols = pl.ds(h * DV, DV)
            grad_gated = dot_t(r["resid_pair"][...], r["out_w"][cols, :])
            raw = r["attn"][:, cols]
            scale = head_rms(raw)
            norm = raw * scale
            gate = r["outgate"][:, cols]
            sig = jax.nn.sigmoid(gate)
            act = gate * sig
            total = total + jnp.sum(grad_gated * norm * act, axis=0, keepdims=True)
            r["proj_grad"][:, pl.ds(2 * keys_w + vals_w + h * DV, DV)] = (
                grad_gated * norm * gains * silu_grad(gate, sig)
            ).astype(bf16)
            weighted = grad_gated * gains * act
            r["grad_o"][:, cols] = scale * (
                weighted - norm * jnp.mean(weighted * norm, axis=-1, keepdims=True)
            )
        r["grad_headgain"][...] = total

    def span_parts(n, h):
        rows, kc, vc = pl.ds(n * SPAN, SPAN), pl.ds(h * DK, DK), pl.ds(h * DV, DV)
        cum = r["cumul"][rows, kc]
        last = cum[SPAN - 1 : SPAN]
        to_end = jnp.exp(last - cum) * r["end_doc"][rows]
        keys = r["keys"][rows, kc]
        grow, shrink = jnp.exp(cum), jnp.exp(-cum)
        return dict(
            rows=rows, kc=kc, vc=vc, last=last, grow=grow, shrink=shrink, to_end=to_end,
            query_dec=r["queries"][rows, kc] * grow,
            key_dec=keys * shrink,
            key_end=keys * to_end,
            values=r["values"][rows, vc],
            grad_o=r["grad_o"][rows, vc],
            within=r["within"][rows],
        )

    def keep_of(n, h):
        return r["keep"][n, pl.ds(h * DK, DK)]

    def scan_copy(step, by):
        return pltpu.make_async_remote_copy(
            src_ref=going.at[step],
            dst_ref=coming.at[step],
            send_sem=scan_sems[0].at[step],
            recv_sem=scan_sems[1].at[step],
            device_id={"seq": s - PAIR * by},
            device_id_type=MESH_ID,
        )

    hops = list(steps) + [1]

    def reach_local():
        for h in range(heads):
            local = None
            for n in reversed(range(spans)):
                p = span_parts(n, h)
                reach = high(p["query_dec"] * p["within"], p["grad_o"], COLS_OF)
                r["reach"][n, pl.ds(h * DK, DK)] = reach
                local = reach if local is None else keep_of(n, h) * local + reach
            going[0, pl.ds(h * DK, DK)] = local.astype(bf16)
            r["reach"][spans, pl.ds(h * DK, DK)] = local

    def scan_start(i):
        pl.when(t >= hops[i])(lambda: scan_copy(i, hops[i]).start())

    def scan_join(i):
        @pl.when(t < chips - hops[i])
        def _():
            scan_copy(i, hops[i]).wait_recv()
            r["reach"][spans] += r["factors"][i] * coming[i].astype(f32)

        going[i + 1] = r["reach"][spans].astype(bf16)
        scan_start(i + 1)

    def scan_end():
        i = len(hops) - 1

        @pl.when(t < chips - 1)
        def _():
            scan_copy(i, 1).wait_recv()
            r["reach"][spans] = r["to_next"][...] * coming[i].astype(f32)

        @pl.when(t == chips - 1)
        def _():
            r["reach"][spans] = jnp.zeros_like(r["reach"][spans])

    def local_back():
        seen = r["mask"][...] > 0.0
        for h in range(heads):
            kc, vc = pl.ds(h * DK, DK), pl.ds(h * DV, DV)
            cum = r["cumul"][:, kc]
            query_dec = r["queries"][:, kc] * jnp.exp(cum)
            key_dec = r["keys"][:, kc] * jnp.exp(-cum)
            grad_o = r["grad_o"][:, vc]
            scores = jnp.where(seen, high(query_dec, key_dec, ROWS_OF), 0.0)
            r["grad_v"][:, vc] = high(scores, grad_o, COLS_OF)
            grad_scores = jnp.where(seen, high(grad_o, r["values"][:, vc], ROWS_OF), 0.0)
            r["grad_qd"][:, kc] = high(grad_scores, key_dec)
            r["grad_kd"][:, kc] = high(grad_scores, query_dec, COLS_OF)
            for n in range(spans):
                rows = pl.ds(n * SPAN, SPAN)
                r["grad_qd"][rows, kc] += r["within"][rows] * high(
                    r["grad_o"][rows, vc], r["entered"][n, kc], ROWS_OF
                )

    def state_back():
        row_pos = lax.broadcasted_iota(jnp.int32, (SPAN, SPAN), 0)
        col_pos = lax.broadcasted_iota(jnp.int32, (SPAN, SPAN), 1)
        lower = (col_pos <= row_pos).astype(f32)
        ones = jnp.ones((8, DV), f32)
        for h in range(heads):
            hk = pl.ds(h * DK, DK)
            ends = r["reach"][spans, hk]
            for n in reversed(range(spans)):
                p = span_parts(n, h)
                rows, kc, vc = p["rows"], p["kc"], p["vc"]
                r["proj_grad"][rows, pl.ds(2 * keys_w + h * DV, DV)] = (
                    r["grad_v"][rows, vc] + high(p["key_end"], ends)
                ).astype(bf16)
                grad_ke = high(p["values"], ends, ROWS_OF)
                moved = grad_ke * p["key_end"]
                kept = jnp.exp(p["last"]) * p["within"][SPAN - 1 : SPAN]
                across = high(ones, ends * r["entered"][n, hk], ROWS_OF)[:1]
                grad_last = jnp.sum(moved, axis=0, keepdims=True) + kept * across
                grad_qd, grad_kd = r["grad_qd"][rows, kc], r["grad_kd"][rows, kc]
                grad_cumul = grad_qd * p["query_dec"] - grad_kd * p["key_dec"] - moved
                grad_d = high(lower, grad_cumul, COLS_OF) + grad_last
                r["grad_logits"][rows, kc] = grad_d * jax.nn.sigmoid(-r["logits"][rows, kc]) / 16.0
                r["proj_grad"][rows, kc] = (grad_qd * p["grow"] * DK ** (-0.5)).astype(bf16)
                r["proj_grad"][rows, pl.ds(keys_w + h * DK, DK)] = (
                    grad_kd * p["shrink"] + grad_ke * p["to_end"]
                ).astype(bf16)
                ends = keep_of(n, h) * ends + r["reach"][n, hk]
        for copy in batch_copies:
            copy.start()

    batch_copies = [
        pltpu.make_async_remote_copy(
            src_ref=r["proj_grad"],
            dst_ref=r["proj_grad_far"].at[nb - 1 - k],
            send_sem=batch_sems[0].at[k - 1],
            recv_sem=batch_sems[1].at[nb - 1 - k],
            device_id={"batch": lax.rem(b + k, nb)},
            device_id_type=MESH_ID,
        )
        for k in range(1, nb)
    ]

    wide = 512

    def proj_back():
        total = r["proj_grad"].shape[1]
        for at in range(0, total, wide):
            cols = pl.ds(at, wide)
            r["proj_acc"][:, cols] = lax.dot_general(
                r["normed"][:, :dim_own], r["proj_grad"][:, cols], (COLS_OF, ((), ())),
                preferred_element_type=f32,
            )
        r["normed_grad"][:, :dim_own] = dot_t(r["proj_grad"][...], r["proj_own"][...])
        far = r["proj_far"].shape[0]
        for at in range(0, far, dim_own):
            r["normed_grad"][:, pl.ds(dim_own + at, dim_own)] = dot_t(
                r["proj_grad"][...], r["proj_far"][pl.ds(at, dim_own)]
            )

    def proj_far_back():
        for k in range(1, nb):
            pltpu.make_async_remote_copy(
                src_ref=r["proj_grad"],
                dst_ref=r["proj_grad_far"].at[k - 1],
                send_sem=batch_sems[0].at[k - 1],
                recv_sem=batch_sems[1].at[k - 1],
                device_id={"batch": lax.rem(b + k, nb)},
                device_id_type=MESH_ID,
            ).wait_recv()
        total = r["proj_grad"].shape[1]
        for at in range(0, total, wide):
            cols = pl.ds(at, wide)
            acc = r["proj_acc"][:, cols]
            for k in range(nb - 1):
                acc = acc + lax.dot_general(
                    r["normed_far"][k], r["proj_grad_far"][k, :, cols], (COLS_OF, ((), ())),
                    preferred_element_type=f32,
                )
            rows = r["proj_part"].shape[1]
            for i in range(r["proj_part"].shape[0]):
                r["proj_part"][i, :, cols] = acc[i * rows : (i + 1) * rows].astype(bf16)

    def last_wait():
        for i, by in enumerate(hops):
            pl.when(t >= by)(lambda: scan_copy(i, by).wait_send())
        for copy in batch_copies:
            copy.wait_send()

    work = {
        "out": out_grad,
        "head": head_back,
        "reach": lambda: (reach_local(), scan_start(0)),
        "local": local_back,
        "end": scan_end,
        "state": state_back,
        "proj": proj_back,
        "far": proj_far_back,
    }
    for i in range(len(hops) - 1):
        work["join%d" % i] = functools.partial(scan_join, i)
    order = dict(at_tick)
    for tick in range(max(offset + len(stages) for offset, stages in plans)):
        for name in order.get(tick, ()):
            if name in work:
                work[name]()
        for offset, stages in plans:
            if 0 <= tick - offset < len(stages):
                stages[tick - offset]()
    for drain in drains:
        drain()
    last_wait()


def attention_back(inputs, jobs, at_tick, ny, nz, nb, steps):
    f32, bf16 = jnp.float32, jnp.bfloat16
    chips = ny * nz
    arrays = [inputs[name] for name in BACK_IN]
    tok, keys_w = inputs["queries"].shape
    vals_w = inputs["values"].shape[1]
    spans = inputs["entered"].shape[0]
    dim_own = inputs["proj_own"].shape[0]
    proj_w = inputs["proj_own"].shape[1]
    shapes = [inputs[name].shape for name in ("gate_part", "down_part", "up_part")]
    shapes.append((chips, vals_w // chips, dim_own))
    shapes.append((chips, dim_own // chips, proj_w))
    scratch_one, scratch_two, scratch_mid = [], [], []
    for (_, rows, cols), (y_first, _) in zip(shapes, jobs):
        n_one, n_two = (ny, nz) if y_first else (nz, ny)
        scratch_one.append(pltpu.VMEM((2, max(n_one - 1, 1), n_two, rows, cols), bf16))
        scratch_two.append(pltpu.VMEM((2, max(n_two - 1, 1), 1, rows, cols), bf16))
        scratch_mid.append(pltpu.VMEM((n_two, rows, cols), bf16))
    tmp = [
        pltpu.VMEM(shapes[3], bf16),
        pltpu.VMEM(shapes[4], bf16),
        pltpu.VMEM((tok, vals_w), f32),
        pltpu.VMEM((spans + 1, keys_w, DV), f32),
        pltpu.VMEM((tok, keys_w), f32),
        pltpu.VMEM((tok, keys_w), f32),
        pltpu.VMEM((tok, vals_w), f32),
        pltpu.VMEM((tok, proj_w), bf16),
        pltpu.VMEM((max(nb - 1, 1), tok, proj_w), bf16),
        pltpu.VMEM((dim_own, proj_w), f32),
    ]
    hops = len(steps) + 1
    tmp += [pltpu.VMEM((hops, keys_w, DV), bf16)] * 2
    dma = pltpu.SemaphoreType.DMA
    sems = [dma((len(jobs), 5, 2, max(ny, nz, 2) - 1))] * 2
    sems += [dma((hops,))] * 2 + [dma((max(nb - 1, 1),))] * 2
    vmem = pl.BlockSpec(memory_space=pltpu.VMEM)
    out_shape = [jax.ShapeDtypeStruct(shape, bf16) for shape in shapes] * 2 + [
        jax.ShapeDtypeStruct((tok, dim_own * nb), f32),
        jax.ShapeDtypeStruct((tok, keys_w), f32),
        jax.ShapeDtypeStruct((1, DV), f32),
    ]
    outs = pl.pallas_call(
        functools.partial(back_kernel, ny, nz, nb, tuple(steps), tuple(jobs), tuple(at_tick)),
        out_shape=out_shape,
        in_specs=[vmem] * len(arrays),
        out_specs=[vmem] * len(out_shape),
        scratch_shapes=scratch_one + scratch_two + scratch_mid + tmp + sems,
        compiler_params=pltpu.CompilerParams(
            collective_id=1, has_side_effects=True, vmem_limit_bytes=60 * 2**20
        ),
        name="attention_back",
    )(*arrays)
    nj = len(jobs)
    return outs[:nj], outs[nj : 2 * nj], outs[2 * nj :]


FRONT_IN = ("tokens", "seg", "gain_one", "gain_two", "bias", "head_gain", "rank_in", "rank_out")
FRONT_OUT = (
    ("normed", "normed_far", "low_rank", "logits", "cumul", "queries", "keys", "values", "outgate")
    + ("mask", "within", "end_doc", "keep", "factors", "to_next", "entered", "attn", "gated")
    + ("gated_far", "resid", "normed_two", "gain_one_rel", "gain_two_rel", "head_gain_all")
    + ("rank_in_far", "rank_out_core")
)


def front_kernel(pieces, down_at, steps, *refs):
    f32, bf16 = jnp.float32, jnp.bfloat16
    refs = list(refs)

    def take(n):
        out = refs[:n]
        del refs[:n]
        return out

    ins = take(8)
    r = dict(zip(FRONT_IN, take(len(FRONT_IN))))
    outs = take(7)
    r.update(zip(FRONT_OUT, take(len(FRONT_OUT))))
    tokens_far, seg_slots, factor_rows, gain_one_far, gain_two_far, bias_far, head_far, rank_out_far = take(8)
    proj, local_out, state, going, coming, out_away, out_come, local_sems = take(8)
    send_x, recv_x, send_p, recv_p, send_s, recv_s, send_c, recv_c = take(8)
    b, s = lax.axis_index("batch"), lax.axis_index("seq")
    ns = lax.axis_size("seq")
    chips = ns // PAIR
    c = lax.rem(s, PAIR)
    t = s // PAIR
    k = lax.rem(s // 2, 4)
    k_y = k + 1 - 2 * lax.rem(k, 2)
    k_z = k + 2 - 4 * (k // 2)
    k_far = 3 - k
    by_x = {"batch": 1 - b}
    by_y = {"seq": s + 2 * (k_y - k)}
    by_z = {"seq": s + 2 * (k_z - k)}
    by_c = {"seq": s + 1 - 2 * c}

    seg_slots[...] = jnp.zeros_like(seg_slots)
    factor_rows[...] = jnp.zeros_like(factor_rows)
    barrier = pltpu.get_barrier_semaphore()

    def signal(to):
        pl.semaphore_signal(barrier, inc=1, device_id=to, device_id_type=MESH_ID)

    signal(by_x)
    peers = 1
    for d in sorted({1, 2, 4} | {PAIR * d for d in steps}):
        pl.when(s >= d)(lambda: signal({"seq": s - d}))
        pl.when(s < ns - d)(lambda: signal({"seq": s + d}))
        peers = peers + (s + ns - d) // ns + (2 * ns - 1 - d - s) // ns
    pl.semaphore_wait(barrier, peers)

    def remote(src, dst, send, recv, to):
        return pltpu.make_async_remote_copy(
            src_ref=src, dst_ref=dst, send_sem=send, recv_sem=recv, device_id=to, device_id_type=MESH_ID
        )

    def source(arg, row_step, col_step, width, start, count):
        rows = pl.ds(pl.multiple_of(c * row_step + start, 16), count)
        if col_step:
            return ins[arg].at[rows, pl.ds(pl.multiple_of(c * col_step, 128), width)]
        return ins[arg].at[rows]

    far_refs = [outs[1], outs[3], outs[5], outs[6]]
    groups = len(pieces)
    x_copies = []
    for g, group in enumerate(pieces):
        far = far_refs[g]
        quarter = far.shape[0] // 4
        mine = []
        for i, (arg, row_step, col_step, width, place) in enumerate(group):
            src = source(arg, row_step, col_step, width, k * quarter, quarter)
            rows = pl.ds(pl.multiple_of(k * quarter, 16), quarter)
            dst = far.at[rows, pl.ds(place, width)]
            mine.append(remote(src, dst, send_x.at[g, i], recv_x.at[g, i], by_x))
        x_copies.append(mine)

    is_sender, is_taker = c == b, c != b

    def guarded(g, taker, body):
        if g == down_at:
            pl.when(is_taker if taker else is_sender)(body)
        else:
            body()

    def start_x(g):
        def body():
            for copy in x_copies[g]:
                copy.start()

        guarded(g, False, body)

    local_copies = []
    for g, group in enumerate(pieces):
        mine = []
        if g != down_at:
            own = outs[2 * g]
            for i, (arg, row_step, col_step, width, place) in enumerate(group):
                src = source(arg, row_step, col_step, width, 0, own.shape[0])
                mine.append(
                    pltpu.make_async_copy(src, own.at[:, pl.ds(place, width)], local_sems.at[g, i])
                )
        local_copies.append(mine)
    down_copy = pltpu.make_async_copy(ins[7], outs[6], local_sems.at[down_at, 0])

    def rows_of(g, q, part):
        far = far_refs[g]
        quarter = far.shape[0] // 4
        if part is None:
            return far.at[pl.ds(pl.multiple_of(q * quarter, 16), quarter)]
        eighth = quarter // 2
        return far.at[pl.ds(pl.multiple_of(q * quarter + part * eighth, 16), eighth)]

    def plane_copy(g, kind, coming_in):
        to, q, part = (
            (by_y, k_y if coming_in else k, None),
            (by_z, k_z if coming_in else k, None),
            (by_y, k_far if coming_in else k_z, 0),
            (by_z, k_far if coming_in else k_y, 1),
        )[kind]
        ref = rows_of(g, q, part)
        return remote(ref, ref, send_p.at[g, kind], recv_p.at[g, kind], to)

    def second(g):
        def body():
            for copy in x_copies[g]:
                copy.wait_recv()
            plane_copy(g, 0, False).start()
            plane_copy(g, 1, False).start()

        guarded(g, True, body)

    def third(g):
        def body():
            plane_copy(g, 1, True).wait_recv()
            plane_copy(g, 2, False).start()
            plane_copy(g, 0, True).wait_recv()
            plane_copy(g, 3, False).start()

        guarded(g, True, body)

    def final(g):
        def body():
            plane_copy(g, 2, True).wait_recv()
            plane_copy(g, 3, True).wait_recv()

        guarded(g, True, body)

    small = [
        remote(src, dst, send_s.at[i], recv_s.at[i], by_x)
        for i, (src, dst) in enumerate(
            (
                (r["gain_one"], gain_one_far),
                (r["gain_two"], gain_two_far),
                (r["bias"], bias_far),
                (r["head_gain"], head_far),
                (r["rank_in"], r["rank_in_far"]),
                (r["rank_out"], rank_out_far),
            )
        )
    ]
    at = len(small)
    token_copy = remote(r["tokens"], tokens_far, send_s.at[at], recv_s.at[at], by_c)
    out_copy = remote(out_away, out_come, send_s.at[at + 1], recv_s.at[at + 1], by_c)
    dim_own = outs[0].shape[0]
    normed_copy = remote(
        r["normed"].at[:, pl.ds(dim_own, dim_own)], r["normed_far"].at[0],
        send_s.at[at + 2], recv_s.at[at + 2], by_x,
    )
    gated_copy = remote(
        r["gated"], r["gated_far"].at[0], send_s.at[at + 3], recv_s.at[at + 3], by_x
    )
    seg_moves = []
    for i, d in enumerate((2, 1, -1, -2)):
        there = s < ns - d if d > 0 else s >= -d
        here = s >= d if d > 0 else s < ns + d
        move = remote(
            r["seg"], seg_slots.at[i], send_c.at[0, i], recv_c.at[0, i], {"seq": s + d}
        )
        seg_moves.append((there, here, move))
    factor_moves = []
    for i, d in enumerate((1, -1)):
        there = t < chips - d if d > 0 else t >= -d
        here = t >= d if d > 0 else t < chips + d
        move = remote(
            factor_rows.at[2 + i], factor_rows.at[i], send_c.at[1, i], recv_c.at[1, i],
            {"seq": s + PAIR * d},
        )
        factor_moves.append((there, here, move))
    hops = list(steps) + [1]

    def scan_move(i):
        return remote(
            going.at[i], coming.at[i], send_c.at[2, i], recv_c.at[2, i], {"seq": s + PAIR * hops[i]}
        )

    start_x(0)
    token_copy.start()
    for there, _, move in seg_moves:
        pl.when(there)(move.start)
    for copy in small:
        copy.start()
    start_x(1)
    for mine in local_copies:
        for copy in mine:
            copy.start()
    pl.when(is_sender)(down_copy.start)

    tok = r["normed"].shape[0]
    spans = tok // SPAN
    keys_w, vals_w = r["queries"].shape[1], r["values"].shape[1]
    heads = keys_w // DK

    def iotas(n):
        return (
            lax.broadcasted_iota(jnp.int32, (n, n), 0),
            lax.broadcasted_iota(jnp.int32, (n, n), 1),
        )

    def to_col(row):
        i, j = iotas(row.shape[1])
        return jnp.sum(jnp.where(i == j, row, 0.0), axis=1, keepdims=True)

    def by_core(mine, other, axis):
        return jnp.where(
            c == 0, jnp.concatenate([mine, other], axis), jnp.concatenate([other, mine], axis)
        )

    for _, here, move in seg_moves:
        pl.when(here)(move.wait_recv)
    seg_own = r["seg"][...]
    seg_row = by_core(seg_own, jnp.where(c == 0, seg_slots[2], seg_slots[1]), 1)
    prev_last = jnp.where(c == 0, seg_slots[1], seg_slots[0])[:, -1:]
    next_first = jnp.where(c == 0, seg_slots[3], seg_slots[2])[:, :1]
    first_id, last_id = seg_row[:, :1], seg_row[:, -1:]
    has_prev = jnp.where(t > 0, 1.0, 0.0)
    has_next = jnp.where(t < chips - 1, 1.0, 0.0)
    from_prev = has_prev * (prev_last == first_id).astype(f32)
    to_next = has_next * (next_first == last_id).astype(f32)
    whole_doc = (first_id == last_id).astype(f32)
    r["to_next"][...] = to_next
    seg_col = to_col(seg_row)
    i_pos, j_pos = iotas(tok)

    def span_of(pos):
        return sum((pos >= n * SPAN).astype(jnp.int32) for n in range(1, spans))

    mask = jnp.where(
        jnp.logical_and(
            jnp.logical_and(span_of(i_pos) == span_of(j_pos), j_pos <= i_pos), seg_col == seg_row
        ),
        1.0,
        0.0,
    )
    r["mask"][...] = mask
    before = seg_col[:1]
    for n in range(spans):
        rows = pl.ds(n * SPAN, SPAN)
        mine = seg_col[n * SPAN : (n + 1) * SPAN]
        first, last = mine[:1], mine[-1:]
        r["within"][rows] = (mine == first).astype(f32) * (first == before).astype(f32)
        r["end_doc"][rows] = (mine == last).astype(f32)
        before = last

    for copy in small:
        copy.wait_recv()
    gain_one = jnp.concatenate([r["gain_one"][...], gain_one_far[...]], axis=1)
    r["gain_one_rel"][...] = gain_one
    gain_two = jnp.concatenate([r["gain_two"][...], gain_two_far[...]], axis=1)
    r["gain_two_rel"][...] = gain_two
    head_gain = jnp.where(
        b == 0,
        jnp.concatenate([r["head_gain"][...], head_far[...]], axis=1),
        jnp.concatenate([head_far[...], r["head_gain"][...]], axis=1),
    )
    r["head_gain_all"][...] = head_gain
    same = jnp.where(is_sender, 1.0, 0.0)
    bias = same * r["bias"][...] + (1.0 - same) * bias_far[...]
    rank_out = same * r["rank_out"][...].astype(f32) + (1.0 - same) * rank_out_far[...].astype(f32)
    r["rank_out_core"][...] = rank_out
    token_copy.wait_recv()
    both = by_core(r["tokens"][...].astype(f32), tokens_far[...].astype(f32), 0)
    half = both.shape[1] // 2
    activation = jnp.where(
        b == 0, both, jnp.concatenate([both[:, half:], both[:, :half]], axis=1)
    )
    r["normed"][...] = (activation * rms_scale(activation) * gain_one).astype(bf16)
    normed_copy.start()
    low_rank = dot32(r["normed"][:, :half], r["rank_in"][...]) + dot32(
        r["normed"][:, half:], r["rank_in_far"][...]
    )
    r["low_rank"][...] = low_rank
    logits = high(low_rank, rank_out) + bias
    r["logits"][...] = logits
    decays = (jnp.minimum(logits, 0.0) - jnp.log1p(jnp.exp(-jnp.abs(logits)))) / 16.0
    i_span, j_span = iotas(SPAN)
    lower = (j_span <= i_span).astype(f32)
    total = jnp.zeros((1, keys_w), f32)
    for n in range(spans):
        rows = pl.ds(n * SPAN, SPAN)
        part = high(lower, decays[n * SPAN : (n + 1) * SPAN])
        r["cumul"][rows] = part
        last = part[SPAN - 1 :]
        total = total + last
        r["keep"][n] = to_col(jnp.exp(last)) * r["within"][pl.ds((n + 1) * SPAN - 1, 1)]
    block_keep = jnp.exp(total) * whole_doc
    factor_rows[2] = block_keep * from_prev
    factor_rows[3] = block_keep * to_next
    for there, _, move in factor_moves:
        pl.when(there)(move.start)

    second(0)
    start_x(2)
    second(1)
    start_x(3)
    for copy in local_copies[0]:
        copy.wait()
    wide = 512

    def columns(body):
        for at in range(0, proj.shape[1], wide):
            body(pl.ds(at, wide))

    def own_proj(cols):
        proj[:, cols] = dot32(r["normed"][:, :half], outs[0][:, cols])

    def far_proj(cols):
        proj[:, cols] += dot32(r["normed"][:, half:], outs[1][:, cols])

    columns(own_proj)
    third(0)
    third(1)
    final(0)
    columns(far_proj)
    r["queries"][...] = proj[:, :keys_w] * DK ** (-0.5)
    r["keys"][...] = proj[:, pl.ds(keys_w, keys_w)]
    r["values"][...] = proj[:, pl.ds(2 * keys_w, vals_w)]
    r["outgate"][...] = proj[:, pl.ds(2 * keys_w + vals_w, vals_w)]

    for h in range(heads):
        kc, vc = pl.ds(h * DK, DK), pl.ds(h * DV, DV)
        local = None
        for n in range(spans):
            rows = pl.ds(n * SPAN, SPAN)
            cum = r["cumul"][rows, kc]
            key_end = r["keys"][rows, kc] * jnp.exp(cum[SPAN - 1 :] - cum) * r["end_doc"][rows]
            added = high(key_end, r["values"][rows, vc], COLS_OF)
            r["entered"][n, kc] = added
            local = added if local is None else r["keep"][n, kc] * local + added
        state[kc] = local
    going[0] = state[...].astype(bf16)
    pl.when(t < chips - hops[0])(scan_move(0).start)
    second(2)

    for _, here, move in factor_moves:
        pl.when(here)(move.wait_recv)
    front, back = to_col(factor_rows[2]), to_col(factor_rows[3])
    r["factors"][0] = back
    front_factors = [front]
    if len(steps) > 1:
        r["factors"][1] = back * to_col(factor_rows[1])
        front_factors.append(front * to_col(factor_rows[0]))

    for h in range(heads):
        kc, vc = pl.ds(h * DK, DK), pl.ds(h * DV, DV)
        cum = r["cumul"][:, kc]
        scores = jnp.where(
            r["mask"][...] > 0.0,
            high(r["queries"][:, kc] * jnp.exp(cum), r["keys"][:, kc] * jnp.exp(-cum), ROWS_OF),
            0.0,
        )
        local_out[:, vc] = high(scores, r["values"][:, vc])

    for i in range(len(steps)):

        @pl.when(t >= hops[i])
        def _():
            scan_move(i).wait_recv()
            state[...] += front_factors[i] * coming[i].astype(f32)

        going[i + 1] = state[...].astype(bf16)
        pl.when(t < chips - hops[i + 1])(scan_move(i + 1).start)
    third(2)
    second(3)
    i = len(steps)

    @pl.when(t >= 1)
    def _():
        scan_move(i).wait_recv()
        state[...] = from_prev * coming[i].astype(f32)

    @pl.when(t < 1)
    def _():
        state[...] = jnp.zeros_like(state)

    for h in range(heads):
        kc, vc = pl.ds(h * DK, DK), pl.ds(h * DV, DV)
        inside = state[kc]
        for n in range(spans):
            rows = pl.ds(n * SPAN, SPAN)
            added = r["entered"][n, kc]
            r["entered"][n, kc] = inside
            query_in = r["queries"][rows, kc] * jnp.exp(r["cumul"][rows, kc]) * r["within"][rows]
            r["attn"][rows, vc] = local_out[rows, vc] + high(query_in, inside)
            inside = r["keep"][n, kc] * inside + added
        raw = r["attn"][:, vc]
        gate = r["outgate"][:, vc]
        r["gated"][:, vc] = (
            raw * head_rms(raw) * head_gain * (gate * jax.nn.sigmoid(gate))
        ).astype(bf16)
    gated_copy.start()
    third(3)

    final(1)
    for copy in local_copies[1]:
        copy.wait()
    rows = tok // PAIR
    mine, away = pl.ds(pl.multiple_of(c * rows, 16), rows), pl.ds(pl.multiple_of((1 - c) * rows, 16), rows)
    for j, ref in ((0, outs[2]), (1, outs[3])):
        cols = pl.ds(j * half, half)
        out_away[:, cols] = dot32(r["gated"][away], ref[...])
        r["resid"][:, cols] = dot32(r["gated"][mine], ref[...])
    out_copy.start()
    tokens = r["tokens"][...].astype(f32)
    own_act = jnp.where(
        b == 0, tokens, jnp.concatenate([tokens[:, half:], tokens[:, :half]], axis=1)
    )
    out_copy.wait_recv()
    resid = own_act + r["resid"][...] + out_come[...]
    r["resid"][...] = resid
    r["normed_two"][...] = (resid * rms_scale(resid) * gain_two).astype(bf16)

    final(2)
    final(3)
    for g in range(groups):

        def plane_sent(g=g):
            for kind in range(4):
                plane_copy(g, kind, False).wait_send()

        def x_sent(g=g):
            for copy in x_copies[g]:
                copy.wait_send()

        guarded(g, True, plane_sent)
        guarded(g, False, x_sent)
        if g > 1:
            for copy in local_copies[g]:
                copy.wait()
    pl.when(is_sender)(down_copy.wait)
    for copy in small + [token_copy, out_copy, normed_copy, gated_copy]:
        copy.wait_send()
    normed_copy.wait_recv()
    gated_copy.wait_recv()
    for there, _, move in seg_moves + factor_moves:
        pl.when(there)(move.wait_send)
    for i in range(len(hops)):
        pl.when(t < chips - hops[i])(scan_move(i).wait_send)


def attention_front(weights, tokens, seg_row, small, steps):
    f32, bf16 = jnp.float32, jnp.bfloat16
    w_query, w_key, w_value, w_outgate, w_output, w_gate, w_up, w_down = weights
    half = lambda a: a.shape[1] // PAIR
    proj, place = [], 0
    for arg, a in enumerate((w_query, w_key, w_value, w_outgate)):
        proj.append((arg, 0, half(a), half(a), place))
        place += half(a)
    dim_own, proj_w = w_query.shape[0], place
    out_rows = w_output.shape[0] // PAIR
    out_piece = [(4, out_rows, 0, w_output.shape[1], 0)]
    gu = [(5, 0, half(w_gate), half(w_gate), 0), (6, 0, half(w_up), half(w_up), half(w_gate))]
    gu_shape = (w_gate.shape[0], 2 * half(w_gate))
    down = [(7, 0, 0, w_down.shape[1], 0)]
    w_shapes = [(dim_own, proj_w)] * 2 + [(out_rows, w_output.shape[1])] * 2 + [gu_shape] * 2
    w_shapes.append(w_down.shape)
    own_tok, dim = tokens.shape
    tok = PAIR * own_tok
    spans, keys_w, vals_w = tok // SPAN, half(w_query), half(w_value)
    rank = small[4].shape[1]
    shape_of = dict(
        normed=((tok, dim), bf16), normed_far=((1, tok, dim_own), bf16),
        low_rank=((tok, rank), f32), logits=((tok, keys_w), f32), cumul=((tok, keys_w), f32),
        queries=((tok, keys_w), f32), keys=((tok, keys_w), f32), values=((tok, vals_w), f32),
        outgate=((tok, vals_w), f32), mask=((tok, tok), f32), within=((tok, 1), f32),
        end_doc=((tok, 1), f32), keep=((spans, keys_w, 1), f32),
        factors=((len(steps), keys_w, 1), f32), to_next=((1, 1), f32),
        entered=((spans, keys_w, DV), f32), attn=((tok, vals_w), f32), gated=((tok, vals_w), bf16),
        gated_far=((1, tok, vals_w), bf16), resid=((own_tok, dim), f32),
        normed_two=((own_tok, dim), bf16), gain_one_rel=((1, dim), f32),
        gain_two_rel=((1, dim), f32), head_gain_all=((1, DV), f32),
        rank_in_far=(small[4].shape, bf16), rank_out_core=((rank, keys_w), f32),
    )
    hops = len(steps) + 1
    vm, dma = pltpu.VMEM, pltpu.SemaphoreType.DMA
    scratch = [
        vm(tokens.shape, bf16), vm((4,) + seg_row.shape, f32), vm((4, 1, keys_w), f32),
        vm(small[0].shape, f32), vm(small[1].shape, f32), vm(small[2].shape, f32),
        vm(small[3].shape, f32), vm(small[5].shape, bf16),
        vm((tok, proj_w), f32), vm((tok, vals_w), f32), vm((keys_w, DV), f32),
        vm((hops, keys_w, DV), bf16), vm((hops, keys_w, DV), bf16),
        vm((own_tok, dim), f32), vm((own_tok, dim), f32),
        dma((4, 4)), dma((4, 4)), dma((4, 4)), dma((4, 4)), dma((4, 4)),
        dma((10,)), dma((10,)), dma((3, 4)), dma((3, 4)),
    ]
    any_spec, vmem = pl.BlockSpec(memory_space=pl.ANY), pl.BlockSpec(memory_space=pltpu.VMEM)
    out_shape = [jax.ShapeDtypeStruct(shape, bf16) for shape in w_shapes]
    out_shape += [jax.ShapeDtypeStruct(*shape_of[name]) for name in FRONT_OUT]
    got = pl.pallas_call(
        functools.partial(front_kernel, (proj, out_piece, gu, down), 3, tuple(steps)),
        out_shape=out_shape,
        in_specs=[any_spec] * 8 + [vmem] * len(FRONT_IN),
        out_specs=[vmem] * len(out_shape),
        scratch_shapes=scratch,
        compiler_params=pltpu.CompilerParams(
            collective_id=0, has_side_effects=True, vmem_limit_bytes=48 * 2**20
        ),
        name="attention_front",
    )(*weights, tokens, seg_row, *small)
    return got[:7], dict(zip(FRONT_OUT, got[7:]))


def core_cols(array_in, c):
    width = array_in.shape[1] // PAIR
    return lax.dynamic_slice_in_dim(array_in, c * width, width, 1)


def dot32(a, b):
    return jnp.dot(a, b, preferred_element_type=jnp.float32)


def dot_t(a, b):
    return lax.dot_general(a, b, (((1,), (1,)), ((), ())), preferred_element_type=jnp.float32)


def grad_dot(pairs_in):
    total = None
    for left, right in pairs_in:
        part = lax.dot_general(
            left, right, (((0,), (0,)), ((), ())), preferred_element_type=jnp.float32
        )
        total = part if total is None else total + part
    return total


def plain_front(at_place, weights, inputs, seg_ids, small, steps):
    f32, bf16 = jnp.float32, jnp.bfloat16
    nb, b, c, t = at_place.nb, at_place.b, at_place.c, at_place.t
    w_query, w_key, w_value, w_outgate, w_output, w_gate, w_up, w_down = weights
    w_rank_in, w_rank_out = small[4], small[5]
    rank = w_rank_in.shape[1]
    heads = HEADS // PAIR
    keys_w, vals_w = KEYS // PAIR, VALS // PAIR
    dim_own = inputs.shape[2] // nb

    in_pair = at_place.pair_all(inputs[0])
    seg_row = at_place.pair_all(seg_ids[0])
    tok_count = seg_row.shape[0]
    half_tok = tok_count // PAIR
    spans = tok_count // SPAN
    edges = jnp.stack([seg_row[0], seg_row[-1]])
    edges_wide = jnp.broadcast_to(edges[:, None], (2, 128)).astype(f32)
    prev_last = at_place.chip_shift(edges_wide, 1)[1, 0]
    next_first = at_place.chip_shift(edges_wide, -1)[0, 0]
    first_id, last_id = edges[0].astype(f32), edges[1].astype(f32)
    from_prev = jnp.logical_and(t > 0, prev_last == first_id).astype(f32)
    to_next = jnp.logical_and(t < at_place.chips - 1, next_first == last_id).astype(f32)
    whole_doc = (first_id == last_id).astype(f32)

    packed = jnp.concatenate([a.reshape(-1) for a in small])
    packed = jnp.stack([packed] + at_place.others(packed))
    parts, at = [], 0
    for a in small:
        parts.append(packed[:, at : at + a.size])
        at += a.size
    gain_one = parts[0].reshape(-1).astype(f32)
    gain_two = parts[1].reshape(-1).astype(f32)
    bias_all = at_place.to_abs(parts[2], 0).reshape(-1).astype(f32)
    bias_w = lax.dynamic_slice_in_dim(bias_all, c * keys_w, keys_w)
    head_gain32 = at_place.to_abs(parts[3], 0).reshape(-1).astype(f32)
    rank_in_w = parts[4].reshape(-1, rank)
    rank_out_all = (
        at_place.to_abs(parts[5], 0).reshape((nb,) + w_rank_out.shape).transpose(1, 0, 2)
        .reshape(rank, -1)
    )
    rank_out_w = core_cols(rank_out_all, c).astype(f32)

    proj_own = jnp.concatenate(
        [core_cols(a, c) for a in (w_query, w_key, w_value, w_outgate)], axis=1
    )
    out_own = lax.dynamic_slice_in_dim(w_output, c * vals_w, vals_w, 0)
    gu_own = jnp.concatenate([core_cols(w_gate, c), core_cols(w_up, c)], axis=1)
    proj_far, out_far, gu_far, down_far = (
        jnp.concatenate(at_place.others(a), axis=0) for a in (proj_own, out_own, gu_own, w_down)
    )
    down_all = at_place.to_abs(jnp.concatenate([w_down, down_far], axis=0), 0)
    ff_half = down_all.shape[0] // PAIR
    down_w = lax.dynamic_slice_in_dim(down_all, c * ff_half, ff_half, 0)
    activation = at_place.to_rel(in_pair, 1).astype(f32)
    scale_one = rms_scale(activation)
    unit_one = activation * scale_one
    normed = (unit_one * gain_one).astype(bf16)
    normed_far = [
        at_place.from_batch(normed[:, (nb - k) * dim_own : (nb - k + 1) * dim_own], k)
        for k in range(1, nb)
    ]

    low_rank = dot32(normed, rank_in_w)
    logits = jnp.dot(low_rank, rank_out_w, precision=top_prec) + bias_w
    decays = jax.nn.log_sigmoid(logits) / 16.0

    seg_s = seg_row.reshape(spans, SPAN)
    first_s, last_s = seg_s[:, 0], seg_s[:, -1]
    row_pos = lax.broadcasted_iota(jnp.int32, (SPAN, SPAN), 0)
    col_pos = lax.broadcasted_iota(jnp.int32, (SPAN, SPAN), 1)
    lower = (col_pos <= row_pos).astype(f32)
    allowed = lower[None] * (seg_s[:, :, None] == seg_s[:, None, :]).astype(f32)
    allowed = allowed[:, None]
    prior = jnp.concatenate([seg_row[:1], last_s[:-1]])
    enters = (first_s == prior).astype(f32)
    within = ((seg_s == first_s[:, None]).astype(f32) * enters[:, None])[:, None, :, None]
    end_doc = (seg_s == last_s[:, None]).astype(f32)[:, None, :, None]

    cumul = mm("ts,nsc->ntc", lower, decays.reshape(spans, SPAN, keys_w))
    total_log = jnp.sum(cumul[:, -1], axis=0)

    proj = dot32(normed[:, :dim_own], proj_own) + dot32(normed[:, dim_own:], proj_far)
    queries = to_spans(proj[:, :keys_w] * DK ** (-0.5), DK)
    keys_s = to_spans(proj[:, keys_w : 2 * keys_w], DK)
    values_s = to_spans(proj[:, 2 * keys_w : 2 * keys_w + vals_w], DV)
    outgate = proj[:, 2 * keys_w + vals_w :]

    cumul = cumul.reshape(spans, SPAN, heads, DK).transpose(0, 2, 1, 3)
    last_cumul = cumul[:, :, -1:, :]
    grow = jnp.exp(cumul)
    shrink = jnp.exp(-cumul)
    to_end = jnp.exp(last_cumul - cumul) * end_doc
    query_dec = queries * grow
    key_dec = keys_s * shrink
    key_end = keys_s * to_end
    query_in = query_dec * within
    keep = jnp.exp(last_cumul[:, :, 0, :]) * within[:, :, -1]
    scores = mm("nhtc,nhsc->nhts", query_dec, key_dec) * allowed
    local_out = mm("nhts,nhsv->nhtv", scores, values_s)
    added = mm("nhsc,nhsv->nhcv", key_end, values_s)

    local_state = added[0]
    for i in range(1, spans):
        local_state = keep[i][:, :, None] * local_state + added[i]

    reach_chips = -(-(SEG_MOST - 1) // tok_count)

    def chip_scan(state, factor, way):
        state = state.reshape(heads * DK, DV)
        step = 1
        pad = jnp.zeros((15, heads * DK), f32)
        while step < min(reach_chips, at_place.chips):
            packed = jnp.concatenate(
                [state, jnp.concatenate([factor[None], pad]).reshape(-1, DV)]
            )
            got = at_place.chip_shift(packed.astype(bf16), way * step).astype(f32)
            state = state + factor[:, None] * got[: heads * DK]
            factor = factor * got[heads * DK :].reshape(16, -1)[0]
            step *= 2
        got = at_place.chip_shift(state.astype(bf16), way)
        return got.astype(f32).reshape(heads, DK, DV)

    block_keep = jnp.exp(total_log) * whole_doc
    carried = from_prev * chip_scan(local_state, block_keep * from_prev, 1)
    enter_list = [carried]
    for i in range(spans - 1):
        enter_list.append(keep[i][:, :, None] * enter_list[i] + added[i])
    entered = jnp.stack(enter_list)

    attn_raw = from_spans(local_out + mm("nhtc,nhcv->nhtv", query_in, entered)).reshape(
        tok_count, heads, DV
    )
    head_scale = head_rms(attn_raw)
    head_norm = attn_raw * head_scale
    gate_h = outgate.reshape(tok_count, heads, DV)
    gate_sig = jax.nn.sigmoid(gate_h)
    gate_act = gate_h * gate_sig
    gated = (head_norm * head_gain32 * gate_act).reshape(tok_count, vals_w).astype(bf16)
    gated_far = at_place.others(gated)
    out_w = jnp.concatenate(
        [out_own] + [out_far[k * vals_w : (k + 1) * vals_w] for k in range(nb - 1)], axis=1
    )
    own_rows = lambda a: lax.dynamic_slice_in_dim(a, c * half_tok, half_tok, 0)
    resid = own_rows(activation) + at_place.pair_sum(dot32(gated, out_w))
    normed_two = (resid * rms_scale(resid) * gain_two).astype(bf16)
    col = lambda a: a.reshape(-1, 1)
    factor = block_keep * to_next
    factors = []
    for step in steps or [1]:
        factors.append(col(factor))
        if step != steps[-1]:
            factor = factor * at_place.chip_shift(factor, -step)
    in_span = jnp.arange(tok_count) // SPAN
    mask = jnp.logical_and(
        jnp.logical_and(in_span[:, None] == in_span, seg_row[:, None] == seg_row),
        jnp.tril(jnp.ones((tok_count, tok_count), bool)),
    )
    front = dict(
        normed=normed, normed_far=jnp.stack(normed_far), low_rank=low_rank, logits=logits,
        cumul=from_spans(cumul), queries=from_spans(queries), keys=from_spans(keys_s),
        values=from_spans(values_s), outgate=outgate, mask=mask.astype(f32), within=col(within),
        end_doc=col(end_doc), keep=keep.reshape(spans, keys_w, 1), factors=jnp.stack(factors),
        to_next=to_next.reshape(1, 1), entered=entered.reshape(spans, keys_w, DV),
        attn=attn_raw.reshape(tok_count, vals_w), gated=gated, gated_far=jnp.stack(gated_far),
        resid=resid, normed_two=normed_two, gain_one_rel=gain_one[None],
        gain_two_rel=gain_two[None], head_gain_all=head_gain32[None],
        rank_in_far=rank_in_w[dim_own:], rank_out_core=rank_out_w,
    )
    return (proj_own, proj_far, out_own, out_far, gu_own, gu_far, down_w), front


def per_device(
    inputs,
    seg_ids,
    gain_attn,
    w_query,
    w_key,
    w_value,
    w_outgate,
    w_rank_in,
    w_rank_out,
    rank_bias,
    head_gain,
    w_output,
    gain_ffn,
    w_gate,
    w_up,
    w_down,
    cotangent,
):
    f32 = jnp.float32
    bf16 = jnp.bfloat16
    at_place = Places()
    nb, b, c, t = at_place.nb, at_place.b, at_place.c, at_place.t
    rank = w_rank_in.shape[1]
    heads = HEADS // PAIR
    keys_w, vals_w = KEYS // PAIR, VALS // PAIR
    dim = inputs.shape[2]
    dim_own = dim // nb

    weights = (w_query, w_key, w_value, w_outgate, w_output, w_gate, w_up, w_down)
    small = (gain_attn, gain_ffn, rank_bias, head_gain, w_rank_in, w_rank_out)
    tok_count = PAIR * inputs.shape[1]
    half_tok = inputs.shape[1]
    reach_chips = -(-(SEG_MOST - 1) // tok_count)
    steps, step = [], 1
    while step < min(reach_chips, at_place.chips):
        steps.append(step)
        step *= 2
    if nb == 2 and at_place.ns % 8 == 0 and len(steps) in (1, 2):
        rows = [a.reshape(1, -1).astype(f32) for a in small[:4]]
        moved, front = attention_front(
            weights, inputs[0], seg_ids.astype(f32), rows + [w_rank_in, w_rank_out], steps
        )
    else:
        moved, front = plain_front(at_place, weights, inputs, seg_ids, small, steps)
    proj_own, proj_far, out_own, out_far, gu_own, gu_far, down_w = moved
    gain_one, gain_two = front["gain_one_rel"][0], front["gain_two_rel"][0]
    normed, low_rank, resid = front["normed"], front["low_rank"], front["resid"]
    normed_two, rank_out_w = front["normed_two"], front["rank_out_core"]
    rank_in_w = jnp.concatenate([w_rank_in, front["rank_in_far"]], axis=0)
    out_w = jnp.concatenate(
        [out_own] + [out_far[k * vals_w : (k + 1) * vals_w] for k in range(nb - 1)], axis=1
    )
    ff_c = down_w.shape[0]

    cot_own = cotangent[0]
    cot_pair = at_place.pair_all(cot_own)
    cot_far = [at_place.pair_all(a) for a in at_place.others(cot_own)]

    scale_two = rms_scale(resid)
    unit_two = resid * scale_two

    two_pair = at_place.pair_all(normed_two)
    two_far = [
        at_place.pair_all(jnp.roll(a, (k + 1) * dim_own, 1))
        for k, a in enumerate(at_place.others(normed_two))
    ]

    def feed_forward(two_rows, cot_rows):
        pre = dot32(two_rows[:, :dim_own], gu_own) + dot32(two_rows[:, dim_own:], gu_far)
        gate_pre, up_pre = pre[:, :ff_c], pre[:, ff_c:]
        sig = jax.nn.sigmoid(gate_pre)
        hidden = (gate_pre * sig * up_pre).astype(bf16)
        grad_hidden = dot_t(cot_rows, down_w)
        grad_gu = jnp.concatenate(
            [
                (grad_hidden * up_pre * silu_grad(gate_pre, sig)).astype(bf16),
                (grad_hidden * gate_pre * sig).astype(bf16),
            ],
            axis=1,
        )
        return hidden, grad_gu

    hidden, grad_gu = feed_forward(two_pair, cot_pair)
    down_sum = at_place.pair_sum(dot32(hidden, down_w))
    output = (at_place.to_abs(resid, 1) + down_sum).astype(bf16)

    two_grad = jnp.concatenate([dot_t(grad_gu, gu_own), dot_t(grad_gu, gu_far)], axis=1)
    grad_two = at_place.pair_sum(two_grad)

    hid_own = [at_place.pair_all(hidden, 1)]
    gu_pairs = [(two_pair[:, :dim_own], grad_gu)]
    down_cots = [cot_pair]
    for two_rows, cot_rows in zip(two_far, cot_far):
        far_hidden, far_grad = feed_forward(two_rows, cot_rows)
        gu_pairs.append((two_rows[:, :dim_own], far_grad))
        hid_own.append(at_place.pair_all(far_hidden, 1))
        down_cots.append(cot_rows)
    ff_own = hid_own[0].shape[1] // nb
    down_pairs = [
        (lax.dynamic_slice_in_dim(h, b * ff_own, ff_own, 1), core_cols(g, c))
        for h, g in zip(hid_own, down_cots)
    ]
    part_gate = grad_dot([(left, right[:, :ff_c]) for left, right in gu_pairs]).astype(bf16)
    part_up = grad_dot([(left, right[:, ff_c:]) for left, right in gu_pairs]).astype(bf16)
    part_down = grad_dot(down_pairs).astype(bf16)

    grad_gain_two = jnp.sum(grad_two * unit_two, axis=0)
    scaled_two = grad_two * gain_two
    grad_resid = at_place.to_rel(cot_own, 1).astype(f32) + scale_two * (
        scaled_two - unit_two * jnp.mean(scaled_two * unit_two, axis=-1, keepdims=True)
    )
    resid_pair = at_place.pair_all(grad_resid.astype(bf16))
    resid_far = [
        at_place.from_batch(resid_pair[:, (nb - k) * dim_own : (nb - k + 1) * dim_own], k)
        for k in range(1, nb)
    ]
    chunks = at_place.chips
    cut = lambda a: a.reshape(chunks, -1, a.shape[1])
    jobs = ((True, 0), (False, 0), (True, 0), (False, 2), (True, 3))
    at_tick = (
        (1, ("out", "head", "reach", "local")),
        (2, ("join0", "join1", "join2", "end", "state", "proj")),
        (3, ("far",)),
    )
    mine, theirs, (normed_grad, grad_logits, headgain_row) = attention_back(
        dict(
            front, gate_part=cut(part_gate), down_part=cut(part_down), up_part=cut(part_up),
            resid_pair=resid_pair, resid_far=jnp.stack(resid_far), out_w=out_w,
            head_gain=front["head_gain_all"], proj_own=proj_own, proj_far=proj_far,
        ),
        jobs, at_tick, at_place.ny, at_place.nz, nb, steps,
    )
    grad_headgain = headgain_row[0]

    grad_bias = jnp.sum(grad_logits, axis=0)
    grad_rank_out = jnp.dot(low_rank.T, grad_logits, precision=top_prec)
    grad_low = jnp.dot(grad_logits, rank_out_w.T, precision=top_prec).astype(bf16)
    normed_grad = normed_grad + dot_t(grad_low, rank_in_w)
    grad_normed = at_place.pair_sum(normed_grad)
    own_in = at_place.to_rel(inputs[0], 1).astype(f32)
    scale_one = rms_scale(own_in)
    unit_own = own_in * scale_one
    grad_gain_one = jnp.sum(grad_normed * unit_own, axis=0)
    scaled_one = grad_normed * gain_one
    grad_input = (
        grad_resid
        + scale_one
        * (scaled_one - unit_own * jnp.mean(scaled_one * unit_own, axis=-1, keepdims=True))
    ).astype(bf16)
    grad_rank_in = grad_dot([(normed, grad_low)])

    def own_slot(part):
        return at_place.by_core(part, jnp.zeros_like(part), part.ndim - 1)

    by_owner = jnp.concatenate(
        [
            grad_gain_one.reshape(nb, -1),
            grad_gain_two.reshape(nb, -1),
            at_place.to_rel(own_slot(grad_bias).reshape(nb, -1), 0),
            at_place.to_rel(grad_headgain.reshape(nb, -1), 0),
            grad_rank_in.reshape(nb, -1),
            at_place.to_rel(
                own_slot(grad_rank_out).reshape(rank, nb, -1).transpose(1, 0, 2).reshape(nb, -1), 0
            ),
        ],
        axis=1,
    )
    owned = at_place.total_sum(by_owner)
    outs, at = [], 0
    for a in small:
        outs.append(owned[at : at + a.size].reshape(a.shape))
        at += a.size
    g_gain_one, g_gain_two, g_bias, g_headgain, g_rank_in, g_rank_out = outs

    mine = [a.reshape(-1, a.shape[2]) for a in mine]
    theirs = [a.reshape(-1, a.shape[2]) for a in theirs]

    def both(i, lo, hi, axis=1):
        return at_place.by_core(mine[i][:, lo:hi], theirs[i][:, lo:hi], axis).astype(f32)

    g_gate = both(0, 0, ff_c)
    g_down = both(1, 0, part_down.shape[1])
    g_up = both(2, 0, ff_c)
    g_output = both(3, 0, dim_own, 0)
    g_query = both(4, 0, keys_w)
    g_key = both(4, keys_w, 2 * keys_w)
    g_value = both(4, 2 * keys_w, 2 * keys_w + vals_w)
    g_outgate = both(4, 2 * keys_w + vals_w, 2 * keys_w + 2 * vals_w)
    return (
        output[None],
        at_place.to_abs(grad_input, 1)[None],
        g_gain_one,
        g_query,
        g_key,
        g_value,
        g_outgate,
        g_rank_in,
        g_rank_out,
        g_bias,
        g_headgain,
        g_output,
        g_gain_two,
        g_gate,
        g_up,
        g_down,
    )


def solution(mesh):
    in_specs = (
        P("batch", "seq", None),
        P("batch", "seq"),
        P("batch"),
        P("batch", None),
        P("batch", None),
        P("batch", None),
        P("batch", None),
        P("batch", None),
        P(None, "batch"),
        P("batch"),
        P("batch"),
        P(None, "batch"),
        P("batch"),
        P("batch", None),
        P("batch", None),
        P("batch", None),
        P("batch", "seq", None),
    )
    out_specs = (
        P("batch", "seq", None),
        P("batch", "seq", None),
        P("batch"),
        P("batch", None),
        P("batch", None),
        P("batch", None),
        P("batch", None),
        P("batch", None),
        P(None, "batch"),
        P("batch"),
        P("batch"),
        P(None, "batch"),
        P("batch"),
        P("batch", None),
        P("batch", None),
        P("batch", None),
    )
    return jax.shard_map(
        per_device, mesh=mesh, in_specs=in_specs, out_specs=out_specs, check_vma=False
    )
```

```python
import functools
from types import SimpleNamespace
from typing import Any, NamedTuple

import jax
import jax.numpy as jnp
from jax import lax
from jax.experimental import pallas as pl
from jax.experimental.pallas import tpu as pltpu
from jax.sharding import PartitionSpec as P

HEADS = 4
DK = 128
DV = 256
SPAN = 64
KEYS = 512
VALS = 1024


norm_eps = 1e-05
head_eps = 0.1
top_prec = lax.Precision.HIGHEST
BOTH = ("batch", "seq")
SEG_MOST = 1024
PAIR = 2


def rms_scale(values_in):
    return lax.rsqrt(jnp.mean(values_in * values_in, axis=-1, keepdims=True) + norm_eps)


def head_rms(values_in):
    return lax.rsqrt(jnp.mean(values_in * values_in, axis=-1, keepdims=True) + head_eps)


def silu_grad(pre_act, sig_val):
    return sig_val * (1.0 + pre_act * (1.0 - sig_val))


def mm(eq, a, b):
    return jnp.einsum(eq, a, b, precision=top_prec)


def to_spans(array_in, width):
    return array_in.reshape(-1, SPAN, array_in.shape[1] // width, width).transpose(0, 2, 1, 3)


def from_spans(array_in):
    spans, heads, span_len, width = array_in.shape
    return array_in.transpose(0, 2, 1, 3).reshape(spans * span_len, heads * width)


class Places:
    def __init__(self):
        self.nb = lax.axis_size("batch")
        self.ns = lax.axis_size("seq")
        self.b = lax.axis_index("batch")
        self.s = lax.axis_index("seq")
        self.c = self.s % PAIR
        self.t = self.s // PAIR
        self.chips = self.ns // PAIR
        self.ny = 2 if self.chips % 2 == 0 else 1
        self.nz = self.chips // self.ny
        self.y = self.t % self.ny
        self.z = self.t // self.ny

    def seq_hop(self, array_in, pairs):
        return lax.ppermute(array_in, "seq", pairs)

    def pair_hop(self, array_in):
        return self.seq_hop(array_in, [(i, i ^ 1) for i in range(self.ns)])

    def chip_shift(self, array_in, by):
        step = by * PAIR
        return self.seq_hop(
            array_in, [(i, i + step) for i in range(self.ns) if 0 <= i + step < self.ns]
        )

    def from_batch(self, array_in, k):
        nb = self.nb
        return lax.ppermute(array_in, "batch", [((d + k) % nb, d) for d in range(nb)])

    def others(self, array_in):
        return [self.from_batch(array_in, k) for k in range(1, self.nb)]

    def by_core(self, mine, other, axis):
        return jnp.where(
            self.c == 0,
            jnp.concatenate([mine, other], axis),
            jnp.concatenate([other, mine], axis),
        )

    def pair_all(self, mine, axis=0):
        return self.by_core(mine, self.pair_hop(mine), axis)

    def pair_sum(self, partial):
        rows = partial.shape[0] // PAIR
        own = lax.dynamic_slice_in_dim(partial, self.c * rows, rows, 0)
        away = lax.dynamic_slice_in_dim(partial, (1 - self.c) * rows, rows, 0)
        return own + self.pair_hop(away)

    def to_rel(self, array_in, axis):
        nb = self.nb
        width = array_in.shape[axis] // nb
        if nb == 2:
            low = lax.slice_in_dim(array_in, 0, width, axis=axis)
            high = lax.slice_in_dim(array_in, width, 2 * width, axis=axis)
            return jnp.where(
                self.b == 0,
                jnp.concatenate([low, high], axis),
                jnp.concatenate([high, low], axis),
            )
        return jnp.roll(array_in, -self.b * width, axis)

    def to_abs(self, array_in, axis):
        if self.nb == 2:
            return self.to_rel(array_in, axis)
        return jnp.roll(array_in, self.b * (array_in.shape[axis] // self.nb), axis)

    def total_sum(self, rel_rows):
        nb = self.nb
        total = rel_rows[0]
        for k in range(1, nb):
            total = total + self.from_batch(rel_rows[nb - k], k)
        step = 1
        while step < self.ns:
            total = total + self.seq_hop(total, [(i, i ^ step) for i in range(self.ns)])
            step *= 2
        return total


MESH_ID = pl.DeviceIdType.MESH


def plane_plans(ny, nz, jobs, grads, sums, swapped, first_in, second_in, halfway, sems, greet):
    send_sems, recv_sems = sems
    s = lax.axis_index("seq")
    t = s // PAIR
    y, z = lax.rem(t, ny), t // ny
    partner = s + 1 - 2 * lax.rem(s, PAIR)
    axes = {"y": (ny, y, PAIR), "z": (nz, z, PAIR * ny)}

    barrier = pltpu.get_barrier_semaphore()

    def signal(to, axis="seq"):
        pl.semaphore_signal(barrier, inc=1, device_id={axis: to}, device_id_type=MESH_ID)

    signal(partner)
    distances, nb = greet
    chips = ny * nz
    b = lax.axis_index("batch")
    for k in range(1, nb):
        signal(lax.rem(b + k, nb), "batch")
    for d in distances:
        pl.when(t >= d)(lambda: signal(s - PAIR * d))
        pl.when(t < chips - d)(lambda: signal(s + PAIR * d))
    for n, pos, stride in axes.values():
        if n > 1:
            pl.when(pos > 0)(lambda: signal(s - stride))
            pl.when(pos < n - 1)(lambda: signal(s + stride))
    peers = nb
    for n, pos, stride in axes.values():
        peers = peers + (pos + n - 1) // n + (2 * n - 2 - pos) // n
    for d in distances:
        peers = peers + (t + chips - d) // chips + (2 * chips - 1 - d - t) // chips
    pl.semaphore_wait(barrier, peers)

    def add_blocks(dst, left, right):
        def one(i, carry):
            dst[i] = (left[i].astype(jnp.float32) + right[i].astype(jnp.float32)).astype(dst.dtype)
            return carry

        lax.fori_loop(0, dst.shape[0], one, 0)

    def line(job, phase, axis):
        n, pos, stride = axes[axis]
        ways = []
        for way in (0, 1):
            q = pos if way == 0 else n - 1 - pos
            to = s + stride if way == 0 else s - stride

            def real(m, way=way):
                return m if way == 0 else n - 1 - m

            def copy(src, dst, step, way=way, to=to):
                return pltpu.make_async_remote_copy(
                    src_ref=src,
                    dst_ref=dst,
                    send_sem=send_sems.at[job, phase, way, step - 1],
                    recv_sem=recv_sems.at[job, phase, way, step - 1],
                    device_id={"seq": to},
                    device_id_type=MESH_ID,
                )

            ways.append((q, real, copy, way))
        return n, pos, ways

    def scatter_stages(job, phase, axis, src, size, arrivals, finish):
        n, pos, ways = line(job, phase, axis)

        def block(i):
            return src.at[pl.ds(i * size, size)]

        def step_stage(step):
            for q, real, copy, way in ways:
                slot = arrivals.at[way, step - 1]

                @pl.when(q == 0)
                def _():
                    copy(block(real(n - step)), slot, step).start()

                if step > 1:
                    before = arrivals.at[way, step - 2]

                    @pl.when(jnp.logical_and(q >= 1, q <= min(step - 1, n - 2)))
                    def _():
                        copy(before, before, step - 1).wait_recv()
                        add_blocks(before, before, block(real(q + n - step)))
                        copy(before, slot, step).start()

        def last():
            dst = finish()
            own = block(pos)
            (q0, _, copy0, _), (q1, _, copy1, _) = ways
            last_r, last_l = arrivals.at[0, n - 2], arrivals.at[1, n - 2]

            @pl.when(q0 == 0)
            def _():
                copy1(last_l, last_l, n - 1).wait_recv()
                add_blocks(dst, own, last_l)

            @pl.when(q0 > 0)
            def _():
                copy0(last_r, last_r, n - 1).wait_recv()
                add_blocks(dst, own, last_r)

            if n > 2:

                @pl.when(jnp.logical_and(q0 > 0, q1 > 0))
                def _():
                    copy1(last_l, last_l, n - 1).wait_recv()
                    add_blocks(dst, dst, last_l)

        def drain():
            for step in range(1, n):
                for q, real, copy, way in ways:
                    slot = arrivals.at[way, step - 1]
                    pl.when(q <= min(step - 1, n - 2))(
                        lambda copy=copy, slot=slot, step=step: copy(slot, slot, step).wait_send()
                    )

        return [functools.partial(step_stage, i) for i in range(1, n)], last, drain

    def gather_stages(job, phase, axis, buf, base, size):
        n, pos, ways = line(job, phase, axis)

        def block(i):
            return buf.at[pl.ds(base + i * size, size)]

        def stage(step):
            for q, real, copy, way in ways:
                if step > 1:
                    here = block(real(q - step + 1))
                    pl.when(q >= step - 1)(
                        lambda copy=copy, here=here: copy(here, here, step - 1).wait_recv()
                    )
                if step < n:
                    here = block(real(q - step + 1))
                    pl.when(jnp.logical_and(q >= step - 1, q <= n - 2))(
                        lambda copy=copy, here=here: copy(here, here, step).start()
                    )

        def drain():
            for step in range(1, n):
                for q, real, copy, way in ways:
                    here = block(real(q - step + 1))
                    pl.when(jnp.logical_and(q >= step - 1, q <= n - 2))(
                        lambda copy=copy, here=here, step=step: copy(here, here, step).wait_send()
                    )

        return [functools.partial(stage, i) for i in range(1, n + 1)], drain

    plans, drains = [], []
    for job, (y_first, swaps) in enumerate(jobs):
        one, two = ("y", "z") if y_first else ("z", "y")
        n_one, pos_one, _ = axes[one]
        n_two, pos_two, _ = axes[two]
        stages = []
        own_at = pos_one * n_two + pos_two
        source = grads[job]
        if n_one > 1:
            steps, last, drain = scatter_stages(
                job, 0, one, source, n_two, first_in[job], lambda job=job: halfway[job]
            )
            stages += steps
            drains.append(drain)
            close = last
        else:

            def close(job=job):
                def one_block(i, carry):
                    halfway[job][i] = grads[job][i]
                    return carry

                lax.fori_loop(0, halfway[job].shape[0], one_block, 0)

        if n_two > 1:
            steps, last, drain = scatter_stages(
                job,
                1,
                two,
                halfway[job],
                1,
                second_in[job],
                lambda job=job, own_at=own_at: sums[job].at[pl.ds(own_at, 1)],
            )
            drains.append(drain)
            stages.append(lambda close=close, step=steps[0]: (close(), step()))
            stages += steps[1:]
            close = last
        else:

            def close(job=job, own_at=own_at, before=close):
                before()
                sums[job][own_at] = halfway[job][0]

        gathers = []
        if n_two > 1:
            steps, drain = gather_stages(job, 2, two, sums[job], pos_one * n_two, 1)
            drains.append(drain)
            gathers += [steps]
        if n_one > 1:
            steps, drain = gather_stages(job, 3, one, sums[job], 0, n_two)
            drains.append(drain)
            gathers += [steps]
        pending = close
        for steps in gathers:
            stages.append(lambda pending=pending, step=steps[0]: (pending(), step()))
            stages += steps[1:-1]
            pending = steps[-1]

        if not swaps:
            stages.append(pending)
            plans.append(stages)
            continue

        def swap(job=job):
            return pltpu.make_async_remote_copy(
                src_ref=sums[job],
                dst_ref=swapped[job],
                send_sem=send_sems.at[job, 4, 0, 0],
                recv_sem=recv_sems.at[job, 4, 0, 0],
                device_id={"seq": partner},
                device_id_type=MESH_ID,
            )

        stages.append(lambda pending=pending, swap=swap: (pending(), swap().start()))
        drains.append(lambda swap=swap: swap().wait())
        plans.append(stages)

    return plans, drains


def high(a, b, dims=((1,), (0,))):
    return lax.dot_general(
        a, b, (dims, ((), ())), precision=top_prec, preferred_element_type=jnp.float32
    )


def low(a, b, dims=((1,), (0,))):
    a, b = a.astype(jnp.bfloat16), b.astype(jnp.bfloat16)
    return lax.dot_general(a, b, (dims, ((), ())), preferred_element_type=jnp.float32)


def split(a):
    top = a.astype(jnp.bfloat16)
    return top, (a - top.astype(jnp.float32)).astype(jnp.bfloat16)


def mid(a, b, dims=((1,), (0,))):
    (a_top, a_rest), (b_top, b_rest) = split(a), split(b)
    return low(a_top, b_top, dims) + (low(a_top, b_rest, dims) + low(a_rest, b_top, dims))


def counted(ones, b, dims=((1,), (0,))):
    top, rest = split(b)
    return low(ones, top, dims) + low(ones, rest, dims)


ROWS_OF = ((1,), (1,))
COLS_OF = ((0,), (0,))
class BackIn(NamedTuple):
    gate_part: Any = None
    down_part: Any = None
    up_part: Any = None
    resid_pair: Any = None
    resid_far: Any = None
    gated: Any = None
    gated_far: Any = None
    out_w: Any = None
    attn: Any = None
    outgate: Any = None
    head_gain: Any = None
    queries: Any = None
    keys: Any = None
    values: Any = None
    cumul: Any = None
    entered: Any = None
    mask: Any = None
    within: Any = None
    end_doc: Any = None
    keep: Any = None
    factors: Any = None
    to_next: Any = None
    logits: Any = None
    normed: Any = None
    normed_far: Any = None
    proj_own: Any = None
    proj_far: Any = None
    rank_in: Any = None
    rank_out_core: Any = None
    low_rank: Any = None
    tokens: Any = None
    grad_resid: Any = None
    gain_one_rel: Any = None
    grad_gain_two: Any = None


class BackOut(NamedTuple):
    normed_grad: Any = None
    grad_logits: Any = None
    grad_headgain: Any = None
    grad_input: Any = None


class BackTmp(NamedTuple):
    out_part: Any = None
    proj_part: Any = None
    grad_o: Any = None
    reach: Any = None
    grad_qd: Any = None
    grad_kd: Any = None
    grad_v: Any = None
    proj_grad: Any = None
    proj_grad_far: Any = None
    proj_acc: Any = None
    grad_rows: Any = None
    rows_away: Any = None
    rows_come: Any = None
    small_own: Any = None
    small_other: Any = None
    small_come: Any = None
    small_part: Any = None


def back_kernel(ny, nz, nb, steps, jobs, order, *refs):
    f32, bf16 = jnp.float32, jnp.bfloat16
    nj = len(jobs)
    refs = list(refs)

    def take(n):
        out = refs[:n]
        del refs[:n]
        return out

    r = SimpleNamespace(**dict(zip(BackIn._fields, take(len(BackIn._fields)))))
    sums = take(nj)
    swapped = take(5)
    vars(r).update(zip(BackOut._fields, take(len(BackOut._fields))))
    first_in, second_in, halfway = take(nj), take(nj), take(nj)
    vars(r).update(zip(BackTmp._fields, take(len(BackTmp._fields))))
    going, coming = take(2)
    sems, scan_sems, batch_sems, small_sems = take(2), take(2), take(2), take(2)
    grads = [r.gate_part, r.down_part, r.up_part, r.out_part, r.proj_part, r.small_part][:nj]
    ends_here = nj > 5
    plans, drains = plane_plans(
        ny, nz, jobs, grads, sums, swapped, first_in, second_in, halfway, sems, (steps, nb)
    )
    s, b = lax.axis_index("seq"), lax.axis_index("batch")
    t = s // PAIR
    chips = ny * nz
    spans = r.entered.shape[0]
    heads = r.queries.shape[1] // DK
    keys_w, vals_w = heads * DK, heads * DV
    dim_own = r.resid_far.shape[2]

    def put_chunks(ref, value):
        rows = ref.shape[1]
        for i in range(ref.shape[0]):
            ref[i] = value[i * rows : (i + 1) * rows].astype(ref.dtype)

    if ends_here:
        r.normed_grad[...] = jnp.zeros_like(r.normed_grad)
    else:
        r.grad_input[...] = jnp.zeros_like(r.grad_input)

    def out_grad():
        total = lax.dot_general(
            r.gated[...], r.resid_pair[:, :dim_own], (COLS_OF, ((), ())),
            preferred_element_type=f32,
        )
        for k in range(nb - 1):
            total = total + lax.dot_general(
                r.gated_far[k], r.resid_far[k], (COLS_OF, ((), ())),
                preferred_element_type=f32,
            )
        put_chunks(r.out_part, total)

    def head_back(h):
        gains = r.head_gain[...]
        total = jnp.zeros_like(gains) if h == 0 else r.grad_headgain[...]
        for h in (h,):
            cols = pl.ds(h * DV, DV)
            grad_gated = dot_t(r.resid_pair[...], r.out_w[cols, :])
            raw = r.attn[:, cols]
            scale = head_rms(raw)
            norm = raw * scale
            gate = r.outgate[:, cols]
            sig = jax.nn.sigmoid(gate)
            act = gate * sig
            total = total + jnp.sum(grad_gated * norm * act, axis=0, keepdims=True)
            r.proj_grad[:, pl.ds(2 * keys_w + vals_w + h * DV, DV)] = (
                grad_gated * norm * gains * silu_grad(gate, sig)
            ).astype(bf16)
            weighted = grad_gated * gains * act
            r.grad_o[:, cols] = scale * (
                weighted - norm * jnp.mean(weighted * norm, axis=-1, keepdims=True)
            )
        r.grad_headgain[...] = total

    def span_parts(n, h):
        rows, kc, vc = pl.ds(n * SPAN, SPAN), pl.ds(h * DK, DK), pl.ds(h * DV, DV)
        cum = r.cumul[rows, kc]
        last = cum[SPAN - 1 : SPAN]
        to_end = jnp.exp(last - cum) * r.end_doc[rows]
        keys = r.keys[rows, kc]
        grow, shrink = jnp.exp(cum), jnp.exp(-cum)
        return dict(
            rows=rows, kc=kc, vc=vc, last=last, grow=grow, shrink=shrink, to_end=to_end,
            query_dec=r.queries[rows, kc] * grow,
            key_dec=keys * shrink,
            key_end=keys * to_end,
            values=r.values[rows, vc],
            grad_o=r.grad_o[rows, vc],
            within=r.within[rows],
        )

    def keep_of(n, h):
        return r.keep[n, pl.ds(h * DK, DK)]

    def scan_copy(step, by):
        return pltpu.make_async_remote_copy(
            src_ref=going.at[step],
            dst_ref=coming.at[step],
            send_sem=scan_sems[0].at[step],
            recv_sem=scan_sems[1].at[step],
            device_id={"seq": s - PAIR * by},
            device_id_type=MESH_ID,
        )

    hops = list(steps) + [1]

    def reach_local(h):
        for h in (h,):
            local = None
            for n in reversed(range(spans)):
                p = span_parts(n, h)
                reach = low(p["query_dec"] * p["within"], p["grad_o"], COLS_OF)
                r.reach[n, pl.ds(h * DK, DK)] = reach
                local = reach if local is None else keep_of(n, h) * local + reach
            going[0, pl.ds(h * DK, DK)] = local.astype(bf16)
            r.reach[spans, pl.ds(h * DK, DK)] = local

    def scan_start(i):
        pl.when(t >= hops[i])(lambda: scan_copy(i, hops[i]).start())

    def scan_join(i):
        @pl.when(t < chips - hops[i])
        def _():
            scan_copy(i, hops[i]).wait_recv()
            r.reach[spans] += r.factors[i] * coming[i].astype(f32)

        going[i + 1] = r.reach[spans].astype(bf16)
        scan_start(i + 1)

    def scan_end():
        i = len(hops) - 1

        @pl.when(t < chips - 1)
        def _():
            scan_copy(i, 1).wait_recv()
            r.reach[spans] = r.to_next[...] * coming[i].astype(f32)

        @pl.when(t == chips - 1)
        def _():
            r.reach[spans] = jnp.zeros_like(r.reach[spans])

    def local_back(h):
        seen = r.mask[...] > 0.0
        for h in (h,):
            kc, vc = pl.ds(h * DK, DK), pl.ds(h * DV, DV)
            cum = r.cumul[:, kc]
            query_dec = r.queries[:, kc] * jnp.exp(cum)
            key_dec = r.keys[:, kc] * jnp.exp(-cum)
            grad_o = r.grad_o[:, vc]
            scores = jnp.where(seen, low(query_dec, key_dec, ROWS_OF), 0.0)
            r.grad_v[:, vc] = low(scores, grad_o, COLS_OF)
            grad_scores = jnp.where(seen, mid(grad_o, r.values[:, vc], ROWS_OF), 0.0)
            r.grad_qd[:, kc] = mid(grad_scores, key_dec)
            r.grad_kd[:, kc] = mid(grad_scores, query_dec, COLS_OF)
            for n in range(spans):
                rows = pl.ds(n * SPAN, SPAN)
                r.grad_qd[rows, kc] += r.within[rows] * mid(
                    r.grad_o[rows, vc], r.entered[n, kc], ROWS_OF
                )

    def state_back(h):
        row_pos = lax.broadcasted_iota(jnp.int32, (SPAN, SPAN), 0)
        col_pos = lax.broadcasted_iota(jnp.int32, (SPAN, SPAN), 1)
        lower = (col_pos <= row_pos).astype(f32)
        ones = jnp.ones((8, DV), f32)
        for h in (h,):
            hk = pl.ds(h * DK, DK)
            ends = r.reach[spans, hk]
            for n in reversed(range(spans)):
                p = span_parts(n, h)
                rows, kc, vc = p["rows"], p["kc"], p["vc"]
                r.proj_grad[rows, pl.ds(2 * keys_w + h * DV, DV)] = (
                    r.grad_v[rows, vc] + low(p["key_end"], ends)
                ).astype(bf16)
                grad_ke = mid(p["values"], ends, ROWS_OF)
                moved = grad_ke * p["key_end"]
                kept = jnp.exp(p["last"]) * p["within"][SPAN - 1 : SPAN]
                across = counted(ones, ends * r.entered[n, hk], ROWS_OF)[:1]
                grad_last = jnp.sum(moved, axis=0, keepdims=True) + kept * across
                grad_qd, grad_kd = r.grad_qd[rows, kc], r.grad_kd[rows, kc]
                grad_cumul = grad_qd * p["query_dec"] - grad_kd * p["key_dec"] - moved
                grad_d = counted(lower, grad_cumul, COLS_OF) + grad_last
                r.grad_logits[rows, kc] = grad_d * jax.nn.sigmoid(-r.logits[rows, kc]) / 16.0
                r.proj_grad[rows, kc] = (grad_qd * p["grow"] * DK ** (-0.5)).astype(bf16)
                r.proj_grad[rows, pl.ds(keys_w + h * DK, DK)] = (
                    grad_kd * p["shrink"] + grad_ke * p["to_end"]
                ).astype(bf16)
                ends = keep_of(n, h) * ends + r.reach[n, hk]

    def send_batch():
        for copy in batch_copies:
            copy.start()

    batch_copies = [
        pltpu.make_async_remote_copy(
            src_ref=r.proj_grad,
            dst_ref=r.proj_grad_far.at[nb - 1 - k],
            send_sem=batch_sems[0].at[k - 1],
            recv_sem=batch_sems[1].at[nb - 1 - k],
            device_id={"batch": lax.rem(b + k, nb)},
            device_id_type=MESH_ID,
        )
        for k in range(1, nb)
    ]

    wide = 512

    def proj_back(at):
        cols = pl.ds(at, wide)
        r.proj_acc[:, cols] = lax.dot_general(
            r.normed[:, :dim_own], r.proj_grad[:, cols], (COLS_OF, ((), ())),
            preferred_element_type=f32,
        )

    def rows_back():
        target = r.grad_rows if ends_here else r.normed_grad
        target[:, :dim_own] = dot_t(r.proj_grad[...], r.proj_own[...])
        far = r.proj_far.shape[0]
        for at in range(0, far, dim_own):
            target[:, pl.ds(dim_own + at, dim_own)] = dot_t(
                r.proj_grad[...], r.proj_far[pl.ds(at, dim_own)]
            )

    def far_arrived():
        for k in range(1, nb):
            pltpu.make_async_remote_copy(
                src_ref=r.proj_grad,
                dst_ref=r.proj_grad_far.at[k - 1],
                send_sem=batch_sems[0].at[k - 1],
                recv_sem=batch_sems[1].at[k - 1],
                device_id={"batch": lax.rem(b + k, nb)},
                device_id_type=MESH_ID,
            ).wait_recv()

    def proj_far_back(at):
        cols = pl.ds(at, wide)
        acc = r.proj_acc[:, cols]
        for k in range(nb - 1):
            acc = acc + lax.dot_general(
                r.normed_far[k], r.proj_grad_far[k, :, cols], (COLS_OF, ((), ())),
                preferred_element_type=f32,
            )
        rows = r.proj_part.shape[1]
        for i in range(r.proj_part.shape[0]):
            r.proj_part[i, :, cols] = acc[i * rows : (i + 1) * rows].astype(bf16)

    def last_wait():
        for i, by in enumerate(hops):
            pl.when(t >= by)(lambda: scan_copy(i, by).wait_send())
        for copy in batch_copies:
            copy.wait_send()

    c = lax.rem(s, PAIR)
    own_tok = r.tokens.shape[0]
    same = jnp.where(c == b, 1.0, 0.0)

    def small_move(i, src, dst, to):
        return pltpu.make_async_remote_copy(
            src_ref=src,
            dst_ref=dst,
            send_sem=small_sems[0].at[i],
            recv_sem=small_sems[1].at[i],
            device_id=to,
            device_id_type=MESH_ID,
        )

    by_pair, by_batch = {"seq": s + 1 - 2 * c}, {"batch": 1 - b}
    row_moves = small_move(0, r.rows_away, r.rows_come, by_pair)
    small_moves = [
        small_move(1, r.small_other, r.small_come.at[0], by_batch),
        small_move(2, r.small_own, r.small_come.at[1], by_pair),
    ]

    def rank_back():
        grad_low = mid(r.grad_logits[...], r.rank_out_core[...], ROWS_OF).astype(bf16)
        r.grad_rows[...] += dot_t(grad_low, r.rank_in[...])
        start = pl.multiple_of((1 - c) * own_tok, 8)
        r.rows_away[...] = r.grad_rows[pl.ds(start, own_tok)]
        row_moves.start()
        bias = jnp.sum(r.grad_logits[...], axis=0, keepdims=True)
        out_rows = mid(r.low_rank[...], r.grad_logits[...], COLS_OF)
        in_rows = lax.dot_general(
            grad_low, r.normed[...], (COLS_OF, ((), ())), preferred_element_type=f32
        )
        gains = r.grad_headgain[...]
        width = gains.shape[1] // 2
        low, upper = gains[:, :width], gains[:, width:]
        rank = out_rows.shape[0]
        for i, ref in enumerate((r.small_own, r.small_other)):
            mine = same if i == 0 else 1.0 - same
            ref[...] = jnp.zeros_like(ref)
            for j in range(dim_own // DV):
                at = i * dim_own + j * DV
                ref[2 + j : 3 + j] = r.grad_gain_two[:, at : at + DV]
                ref[(2 + j) * rank : (3 + j) * rank] = in_rows[:, at : at + DV]
            ref[4:5] = bias * mine
            ref[5:6, :width] = jnp.where(b == i, low, upper)
            ref[rank : 2 * rank] = out_rows * mine

    def end_back():
        row_moves.wait_recv()
        start = pl.multiple_of(c * own_tok, 8)
        grad_normed = r.grad_rows[pl.ds(start, own_tok)] + r.rows_come[...]
        tokens = r.tokens[...].astype(f32)
        rel = jnp.where(
            b == 0, tokens, jnp.concatenate([tokens[:, dim_own:], tokens[:, :dim_own]], axis=1)
        )
        scale = rms_scale(rel)
        unit = rel * scale
        gain_grad = jnp.sum(grad_normed * unit, axis=0, keepdims=True)
        for i, ref in enumerate((r.small_own, r.small_other)):
            for j in range(dim_own // DV):
                at = i * dim_own + j * DV
                ref[j : j + 1] = gain_grad[:, at : at + DV]
        small_moves[0].start()
        scaled = grad_normed * r.gain_one_rel[...]
        grad = r.grad_resid[...] + scale * (
            scaled - unit * jnp.mean(scaled * unit, axis=-1, keepdims=True)
        )
        grad = jnp.where(
            b == 0, grad, jnp.concatenate([grad[:, dim_own:], grad[:, :dim_own]], axis=1)
        )
        r.grad_input[...] = grad.astype(bf16)

    def batch_small():
        small_moves[0].wait_recv()
        r.small_own[...] += r.small_come[0]
        small_moves[1].start()

    def pair_small():
        small_moves[1].wait_recv()
        rows = r.small_part.shape[1]
        for i in range(r.small_part.shape[0]):
            at = pl.ds(i * rows, rows)
            r.small_part[i] = r.small_own[at] + r.small_come[1, at]

    cuts = range(0, r.proj_grad.shape[1], wide)
    each = lambda body, over: [functools.partial(body, i) for i in over]
    work = [out_grad] + each(head_back, range(heads)) + each(reach_local, range(heads))
    work += [lambda: scan_start(0)] + each(local_back, range(heads))
    work += each(scan_join, range(len(hops) - 1)) + [scan_end] + each(state_back, range(heads))
    work += [send_batch, rows_back]
    if ends_here:
        work += [rank_back, end_back]
    work += each(proj_back, cuts) + [far_arrived] + each(proj_far_back, cuts)
    if ends_here:
        work += [batch_small, pair_small]
    work, plans = iter(work), [iter(stages) for stages in plans]

    def advance(what):
        body = next(what, None)
        if body is not None:
            body()
        return body is not None

    for job in order:
        if job < nj:
            advance(work if job < 0 else plans[job])
    while advance(work):
        pass
    while any([advance(stages) for stages in plans]):
        pass
    for drain in drains:
        drain()
    last_wait()
    if ends_here:
        for move in [row_moves] + small_moves:
            move.wait_send()


def attention_back(inputs, jobs, order, ny, nz, nb, steps):
    f32, bf16 = jnp.float32, jnp.bfloat16
    chips = ny * nz
    arrays = list(inputs)
    tok, keys_w = inputs.queries.shape
    vals_w = inputs.values.shape[1]
    spans = inputs.entered.shape[0]
    dim_own = inputs.proj_own.shape[0]
    proj_w = inputs.proj_own.shape[1]
    shapes = [inputs.gate_part.shape, inputs.down_part.shape, inputs.up_part.shape]
    shapes.append((chips, vals_w // chips, dim_own))
    shapes.append((chips, dim_own // chips, proj_w))
    kinds = [bf16] * 5
    ends_here = len(jobs) > 5
    rank, own_tok = inputs.rank_in.shape[1], inputs.tokens.shape[0]
    small_rows = rank * (2 + dim_own // DV) if ends_here else chips
    if ends_here:
        shapes.append((chips, small_rows // chips, DV))
        kinds.append(f32)
    scratch_one, scratch_two, scratch_mid = [], [], []
    for (_, rows, cols), (y_first, _), kind in zip(shapes, jobs, kinds):
        n_one, n_two = (ny, nz) if y_first else (nz, ny)
        scratch_one.append(pltpu.VMEM((2, max(n_one - 1, 1), n_two, rows, cols), kind))
        scratch_two.append(pltpu.VMEM((2, max(n_two - 1, 1), 1, rows, cols), kind))
        scratch_mid.append(pltpu.VMEM((n_two, rows, cols), kind))
    tmp = [
        pltpu.VMEM(shapes[3], bf16),
        pltpu.VMEM(shapes[4], bf16),
        pltpu.VMEM((tok, vals_w), f32),
        pltpu.VMEM((spans + 1, keys_w, DV), f32),
        pltpu.VMEM((tok, keys_w), f32),
        pltpu.VMEM((tok, keys_w), f32),
        pltpu.VMEM((tok, vals_w), f32),
        pltpu.VMEM((tok, proj_w), bf16),
        pltpu.VMEM((max(nb - 1, 1), tok, proj_w), bf16),
        pltpu.VMEM((dim_own, proj_w), f32),
        pltpu.VMEM((tok, dim_own * nb), f32),
        pltpu.VMEM((own_tok, dim_own * nb), f32),
        pltpu.VMEM((own_tok, dim_own * nb), f32),
        pltpu.VMEM((small_rows, DV), f32),
        pltpu.VMEM((small_rows, DV), f32),
        pltpu.VMEM((2, small_rows, DV), f32),
        pltpu.VMEM((chips, small_rows // chips, DV), f32),
    ]
    hops = len(steps) + 1
    tmp += [pltpu.VMEM((hops, keys_w, DV), bf16)] * 2
    dma = pltpu.SemaphoreType.DMA
    sems = [dma((len(jobs), 5, 2, max(ny, nz, 2) - 1))] * 2
    sems += [dma((hops,))] * 2 + [dma((max(nb - 1, 1),))] * 2 + [dma((3,))] * 2
    vmem = pl.BlockSpec(memory_space=pltpu.VMEM)
    out_shape = [jax.ShapeDtypeStruct(shape, kind) for shape, kind in zip(shapes, kinds)]
    out_shape += out_shape[:5]
    out_shape += [
        jax.ShapeDtypeStruct((8, 128) if ends_here else (tok, dim_own * nb), f32),
        jax.ShapeDtypeStruct((tok, keys_w), f32),
        jax.ShapeDtypeStruct((1, DV), f32),
        jax.ShapeDtypeStruct((own_tok, dim_own * nb), bf16),
    ]
    outs = pl.pallas_call(
        functools.partial(back_kernel, ny, nz, nb, tuple(steps), tuple(jobs), tuple(order)),
        out_shape=out_shape,
        in_specs=[vmem] * len(arrays),
        out_specs=[vmem] * len(out_shape),
        scratch_shapes=scratch_one + scratch_two + scratch_mid + tmp + sems,
        compiler_params=pltpu.CompilerParams(
            collective_id=1, has_side_effects=True, vmem_limit_bytes=60 * 2**20
        ),
        name="attention_back",
    )(*arrays)
    nj = len(jobs)
    return outs[:nj], outs[nj : nj + 5], outs[nj + 5 :]


class FrontIn(NamedTuple):
    tokens: Any = None
    seg: Any = None
    gain_one: Any = None
    gain_two: Any = None
    bias: Any = None
    head_gain: Any = None
    rank_in: Any = None
    rank_out: Any = None


class FrontOut(NamedTuple):
    normed: Any = None
    normed_far: Any = None
    low_rank: Any = None
    logits: Any = None
    cumul: Any = None
    queries: Any = None
    keys: Any = None
    values: Any = None
    outgate: Any = None
    mask: Any = None
    within: Any = None
    end_doc: Any = None
    keep: Any = None
    factors: Any = None
    to_next: Any = None
    entered: Any = None
    attn: Any = None
    gated: Any = None
    gated_far: Any = None
    resid: Any = None
    normed_two: Any = None
    gain_one_rel: Any = None
    gain_two_rel: Any = None
    head_gain_all: Any = None
    rank_in_far: Any = None
    rank_out_core: Any = None


def front_kernel(pieces, down_at, steps, *refs):
    f32, bf16 = jnp.float32, jnp.bfloat16
    refs = list(refs)

    def take(n):
        out = refs[:n]
        del refs[:n]
        return out

    ins = take(8)
    r = SimpleNamespace(**dict(zip(FrontIn._fields, take(len(FrontIn._fields)))))
    outs = take(7)
    vars(r).update(zip(FrontOut._fields, take(len(FrontOut._fields))))
    tokens_far, seg_slots, factor_rows, gain_one_far, gain_two_far, bias_far, head_far, rank_out_far = take(8)
    proj, local_out, state, going, coming, out_away, out_come, local_sems = take(8)
    send_x, recv_x, send_p, recv_p, send_s, recv_s, send_c, recv_c = take(8)
    b, s = lax.axis_index("batch"), lax.axis_index("seq")
    ns = lax.axis_size("seq")
    chips = ns // PAIR
    c = lax.rem(s, PAIR)
    t = s // PAIR
    k = lax.rem(s // 2, 4)
    k_y = k + 1 - 2 * lax.rem(k, 2)
    k_z = k + 2 - 4 * (k // 2)
    k_far = 3 - k
    by_x = {"batch": 1 - b}
    by_y = {"seq": s + 2 * (k_y - k)}
    by_z = {"seq": s + 2 * (k_z - k)}
    by_c = {"seq": s + 1 - 2 * c}

    seg_slots[...] = jnp.zeros_like(seg_slots)
    factor_rows[...] = jnp.zeros_like(factor_rows)
    barrier = pltpu.get_barrier_semaphore()

    def signal(to):
        pl.semaphore_signal(barrier, inc=1, device_id=to, device_id_type=MESH_ID)

    signal(by_x)
    peers = 1
    for d in sorted({1, 2, 4} | {PAIR * d for d in steps}):
        pl.when(s >= d)(lambda: signal({"seq": s - d}))
        pl.when(s < ns - d)(lambda: signal({"seq": s + d}))
        peers = peers + (s + ns - d) // ns + (2 * ns - 1 - d - s) // ns
    pl.semaphore_wait(barrier, peers)

    def remote(src, dst, send, recv, to):
        return pltpu.make_async_remote_copy(
            src_ref=src, dst_ref=dst, send_sem=send, recv_sem=recv, device_id=to, device_id_type=MESH_ID
        )

    def source(arg, row_step, col_step, width, start, count):
        rows = pl.ds(pl.multiple_of(c * row_step + start, 16), count)
        if col_step:
            return ins[arg].at[rows, pl.ds(pl.multiple_of(c * col_step, 128), width)]
        return ins[arg].at[rows]

    far_refs = [outs[1], outs[3], outs[5], outs[6]]
    groups = len(pieces)
    x_copies = []
    for g, group in enumerate(pieces):
        far = far_refs[g]
        quarter = far.shape[0] // 4
        mine = []
        for i, (arg, row_step, col_step, width, place) in enumerate(group):
            src = source(arg, row_step, col_step, width, k * quarter, quarter)
            rows = pl.ds(pl.multiple_of(k * quarter, 16), quarter)
            dst = far.at[rows, pl.ds(place, width)]
            mine.append(remote(src, dst, send_x.at[g, i], recv_x.at[g, i], by_x))
        x_copies.append(mine)

    is_sender, is_taker = c == b, c != b

    def guarded(g, taker, body):
        if g == down_at:
            pl.when(is_taker if taker else is_sender)(body)
        else:
            body()

    def start_x(g):
        def body():
            for copy in x_copies[g]:
                copy.start()

        guarded(g, False, body)

    local_copies = []
    for g, group in enumerate(pieces):
        mine = []
        if g != down_at:
            own = outs[2 * g]
            for i, (arg, row_step, col_step, width, place) in enumerate(group):
                src = source(arg, row_step, col_step, width, 0, own.shape[0])
                mine.append(
                    pltpu.make_async_copy(src, own.at[:, pl.ds(place, width)], local_sems.at[g, i])
                )
        local_copies.append(mine)
    down_copy = pltpu.make_async_copy(ins[7], outs[6], local_sems.at[down_at, 0])

    def rows_of(g, q, part):
        far = far_refs[g]
        quarter = far.shape[0] // 4
        if part is None:
            return far.at[pl.ds(pl.multiple_of(q * quarter, 16), quarter)]
        eighth = quarter // 2
        return far.at[pl.ds(pl.multiple_of(q * quarter + part * eighth, 16), eighth)]

    def plane_copy(g, kind, coming_in):
        to, q, part = (
            (by_y, k_y if coming_in else k, None),
            (by_z, k_z if coming_in else k, None),
            (by_y, k_far if coming_in else k_z, 0),
            (by_z, k_far if coming_in else k_y, 1),
        )[kind]
        ref = rows_of(g, q, part)
        return remote(ref, ref, send_p.at[g, kind], recv_p.at[g, kind], to)

    def second(g):
        def body():
            for copy in x_copies[g]:
                copy.wait_recv()
            plane_copy(g, 0, False).start()
            plane_copy(g, 1, False).start()

        guarded(g, True, body)

    def third(g):
        def body():
            plane_copy(g, 1, True).wait_recv()
            plane_copy(g, 2, False).start()
            plane_copy(g, 0, True).wait_recv()
            plane_copy(g, 3, False).start()

        guarded(g, True, body)

    def final(g):
        def body():
            plane_copy(g, 2, True).wait_recv()
            plane_copy(g, 3, True).wait_recv()

        guarded(g, True, body)

    small = [
        remote(src, dst, send_s.at[i], recv_s.at[i], by_x)
        for i, (src, dst) in enumerate(
            (
                (r.gain_one, gain_one_far),
                (r.gain_two, gain_two_far),
                (r.bias, bias_far),
                (r.head_gain, head_far),
                (r.rank_in, r.rank_in_far),
                (r.rank_out, rank_out_far),
            )
        )
    ]
    at = len(small)
    token_copy = remote(r.tokens, tokens_far, send_s.at[at], recv_s.at[at], by_c)
    out_copy = remote(out_away, out_come, send_s.at[at + 1], recv_s.at[at + 1], by_c)
    dim_own = outs[0].shape[0]
    normed_copy = remote(
        r.normed.at[:, pl.ds(dim_own, dim_own)], r.normed_far.at[0],
        send_s.at[at + 2], recv_s.at[at + 2], by_x,
    )
    gated_copy = remote(
        r.gated, r.gated_far.at[0], send_s.at[at + 3], recv_s.at[at + 3], by_x
    )
    seg_moves = []
    for i, d in enumerate((2, 1, -1, -2)):
        there = s < ns - d if d > 0 else s >= -d
        here = s >= d if d > 0 else s < ns + d
        move = remote(
            r.seg, seg_slots.at[i], send_c.at[0, i], recv_c.at[0, i], {"seq": s + d}
        )
        seg_moves.append((there, here, move))
    factor_moves = []
    for i, d in enumerate((1, -1)):
        there = t < chips - d if d > 0 else t >= -d
        here = t >= d if d > 0 else t < chips + d
        move = remote(
            factor_rows.at[2 + i], factor_rows.at[i], send_c.at[1, i], recv_c.at[1, i],
            {"seq": s + PAIR * d},
        )
        factor_moves.append((there, here, move))
    hops = list(steps) + [1]

    def scan_move(i):
        return remote(
            going.at[i], coming.at[i], send_c.at[2, i], recv_c.at[2, i], {"seq": s + PAIR * hops[i]}
        )

    start_x(0)
    token_copy.start()
    for there, _, move in seg_moves:
        pl.when(there)(move.start)
    for copy in small:
        copy.start()
    start_x(1)
    for mine in local_copies:
        for copy in mine:
            copy.start()
    pl.when(is_sender)(down_copy.start)

    tok = r.normed.shape[0]
    spans = tok // SPAN
    keys_w, vals_w = r.queries.shape[1], r.values.shape[1]
    heads = keys_w // DK

    def iotas(n):
        return (
            lax.broadcasted_iota(jnp.int32, (n, n), 0),
            lax.broadcasted_iota(jnp.int32, (n, n), 1),
        )

    def to_col(row):
        i, j = iotas(row.shape[1])
        return jnp.sum(jnp.where(i == j, row, 0.0), axis=1, keepdims=True)

    def by_core(mine, other, axis):
        return jnp.where(
            c == 0, jnp.concatenate([mine, other], axis), jnp.concatenate([other, mine], axis)
        )

    for _, here, move in seg_moves:
        pl.when(here)(move.wait_recv)
    seg_own = r.seg[...]
    seg_row = by_core(seg_own, jnp.where(c == 0, seg_slots[2], seg_slots[1]), 1)
    prev_last = jnp.where(c == 0, seg_slots[1], seg_slots[0])[:, -1:]
    next_first = jnp.where(c == 0, seg_slots[3], seg_slots[2])[:, :1]
    first_id, last_id = seg_row[:, :1], seg_row[:, -1:]
    has_prev = jnp.where(t > 0, 1.0, 0.0)
    has_next = jnp.where(t < chips - 1, 1.0, 0.0)
    from_prev = has_prev * (prev_last == first_id).astype(f32)
    to_next = has_next * (next_first == last_id).astype(f32)
    whole_doc = (first_id == last_id).astype(f32)
    r.to_next[...] = to_next
    seg_col = to_col(seg_row)
    i_pos, j_pos = iotas(tok)

    def span_of(pos):
        return sum((pos >= n * SPAN).astype(jnp.int32) for n in range(1, spans))

    mask = jnp.where(
        jnp.logical_and(
            jnp.logical_and(span_of(i_pos) == span_of(j_pos), j_pos <= i_pos), seg_col == seg_row
        ),
        1.0,
        0.0,
    )
    r.mask[...] = mask
    before = seg_col[:1]
    for n in range(spans):
        rows = pl.ds(n * SPAN, SPAN)
        mine = seg_col[n * SPAN : (n + 1) * SPAN]
        first, last = mine[:1], mine[-1:]
        r.within[rows] = (mine == first).astype(f32) * (first == before).astype(f32)
        r.end_doc[rows] = (mine == last).astype(f32)
        before = last

    for copy in small:
        copy.wait_recv()
    gain_one = jnp.concatenate([r.gain_one[...], gain_one_far[...]], axis=1)
    r.gain_one_rel[...] = gain_one
    gain_two = jnp.concatenate([r.gain_two[...], gain_two_far[...]], axis=1)
    r.gain_two_rel[...] = gain_two
    head_gain = jnp.where(
        b == 0,
        jnp.concatenate([r.head_gain[...], head_far[...]], axis=1),
        jnp.concatenate([head_far[...], r.head_gain[...]], axis=1),
    )
    r.head_gain_all[...] = head_gain
    same = jnp.where(is_sender, 1.0, 0.0)
    bias = same * r.bias[...] + (1.0 - same) * bias_far[...]
    rank_out = same * r.rank_out[...].astype(f32) + (1.0 - same) * rank_out_far[...].astype(f32)
    r.rank_out_core[...] = rank_out
    token_copy.wait_recv()
    both = by_core(r.tokens[...].astype(f32), tokens_far[...].astype(f32), 0)
    half = both.shape[1] // 2
    activation = jnp.where(
        b == 0, both, jnp.concatenate([both[:, half:], both[:, :half]], axis=1)
    )
    r.normed[...] = (activation * rms_scale(activation) * gain_one).astype(bf16)
    normed_copy.start()
    low_rank = dot32(r.normed[:, :half], r.rank_in[...]) + dot32(
        r.normed[:, half:], r.rank_in_far[...]
    )
    r.low_rank[...] = low_rank
    logits = high(low_rank, rank_out) + bias
    r.logits[...] = logits
    decays = (jnp.minimum(logits, 0.0) - jnp.log1p(jnp.exp(-jnp.abs(logits)))) / 16.0
    i_span, j_span = iotas(SPAN)
    lower = (j_span <= i_span).astype(f32)
    total = jnp.zeros((1, keys_w), f32)
    for n in range(spans):
        rows = pl.ds(n * SPAN, SPAN)
        part = high(lower, decays[n * SPAN : (n + 1) * SPAN])
        r.cumul[rows] = part
        last = part[SPAN - 1 :]
        total = total + last
        r.keep[n] = to_col(jnp.exp(last)) * r.within[pl.ds((n + 1) * SPAN - 1, 1)]
    block_keep = jnp.exp(total) * whole_doc
    factor_rows[2] = block_keep * from_prev
    factor_rows[3] = block_keep * to_next
    for there, _, move in factor_moves:
        pl.when(there)(move.start)

    second(0)
    start_x(2)
    second(1)
    start_x(3)
    for copy in local_copies[0]:
        copy.wait()
    wide = 512

    def columns(body):
        for at in range(0, proj.shape[1], wide):
            body(pl.ds(at, wide))

    def own_proj(cols):
        proj[:, cols] = dot32(r.normed[:, :half], outs[0][:, cols])

    def far_proj(cols):
        proj[:, cols] += dot32(r.normed[:, half:], outs[1][:, cols])

    columns(own_proj)
    third(0)
    third(1)
    final(0)
    columns(far_proj)
    r.queries[...] = proj[:, :keys_w] * DK ** (-0.5)
    r.keys[...] = proj[:, pl.ds(keys_w, keys_w)]
    r.values[...] = proj[:, pl.ds(2 * keys_w, vals_w)]
    r.outgate[...] = proj[:, pl.ds(2 * keys_w + vals_w, vals_w)]

    for h in range(heads):
        kc, vc = pl.ds(h * DK, DK), pl.ds(h * DV, DV)
        local = None
        for n in range(spans):
            rows = pl.ds(n * SPAN, SPAN)
            cum = r.cumul[rows, kc]
            key_end = r.keys[rows, kc] * jnp.exp(cum[SPAN - 1 :] - cum) * r.end_doc[rows]
            added = low(key_end, r.values[rows, vc], COLS_OF)
            r.entered[n, kc] = added
            local = added if local is None else r.keep[n, kc] * local + added
        state[kc] = local
    going[0] = state[...].astype(bf16)
    pl.when(t < chips - hops[0])(scan_move(0).start)
    second(2)

    for _, here, move in factor_moves:
        pl.when(here)(move.wait_recv)
    front, back = to_col(factor_rows[2]), to_col(factor_rows[3])
    r.factors[0] = back
    front_factors = [front]
    if len(steps) > 1:
        r.factors[1] = back * to_col(factor_rows[1])
        front_factors.append(front * to_col(factor_rows[0]))

    for h in range(heads):
        kc, vc = pl.ds(h * DK, DK), pl.ds(h * DV, DV)
        cum = r.cumul[:, kc]
        scores = jnp.where(
            r.mask[...] > 0.0,
            low(r.queries[:, kc] * jnp.exp(cum), r.keys[:, kc] * jnp.exp(-cum), ROWS_OF),
            0.0,
        )
        local_out[:, vc] = low(scores, r.values[:, vc])

    for i in range(len(steps)):

        @pl.when(t >= hops[i])
        def _():
            scan_move(i).wait_recv()
            state[...] += front_factors[i] * coming[i].astype(f32)

        going[i + 1] = state[...].astype(bf16)
        pl.when(t < chips - hops[i + 1])(scan_move(i + 1).start)
    third(2)
    second(3)
    i = len(steps)

    @pl.when(t >= 1)
    def _():
        scan_move(i).wait_recv()
        state[...] = from_prev * coming[i].astype(f32)

    @pl.when(t < 1)
    def _():
        state[...] = jnp.zeros_like(state)

    for h in range(heads):
        kc, vc = pl.ds(h * DK, DK), pl.ds(h * DV, DV)
        inside = state[kc]
        for n in range(spans):
            rows = pl.ds(n * SPAN, SPAN)
            added = r.entered[n, kc]
            r.entered[n, kc] = inside
            query_in = r.queries[rows, kc] * jnp.exp(r.cumul[rows, kc]) * r.within[rows]
            r.attn[rows, vc] = local_out[rows, vc] + low(query_in, inside)
            inside = r.keep[n, kc] * inside + added
        raw = r.attn[:, vc]
        gate = r.outgate[:, vc]
        r.gated[:, vc] = (
            raw * head_rms(raw) * head_gain * (gate * jax.nn.sigmoid(gate))
        ).astype(bf16)
    gated_copy.start()
    third(3)

    final(1)
    for copy in local_copies[1]:
        copy.wait()
    rows = tok // PAIR
    mine, away = pl.ds(pl.multiple_of(c * rows, 16), rows), pl.ds(pl.multiple_of((1 - c) * rows, 16), rows)
    for j, ref in ((0, outs[2]), (1, outs[3])):
        cols = pl.ds(j * half, half)
        out_away[:, cols] = dot32(r.gated[away], ref[...])
        r.resid[:, cols] = dot32(r.gated[mine], ref[...])
    out_copy.start()
    tokens = r.tokens[...].astype(f32)
    own_act = jnp.where(
        b == 0, tokens, jnp.concatenate([tokens[:, half:], tokens[:, :half]], axis=1)
    )
    out_copy.wait_recv()
    resid = own_act + r.resid[...] + out_come[...]
    r.resid[...] = resid
    r.normed_two[...] = (resid * rms_scale(resid) * gain_two).astype(bf16)

    final(2)
    final(3)
    for g in range(groups):

        def plane_sent(g=g):
            for kind in range(4):
                plane_copy(g, kind, False).wait_send()

        def x_sent(g=g):
            for copy in x_copies[g]:
                copy.wait_send()

        guarded(g, True, plane_sent)
        guarded(g, False, x_sent)
        if g > 1:
            for copy in local_copies[g]:
                copy.wait()
    pl.when(is_sender)(down_copy.wait)
    for copy in small + [token_copy, out_copy, normed_copy, gated_copy]:
        copy.wait_send()
    normed_copy.wait_recv()
    gated_copy.wait_recv()
    for there, _, move in seg_moves + factor_moves:
        pl.when(there)(move.wait_send)
    for i in range(len(hops)):
        pl.when(t < chips - hops[i])(scan_move(i).wait_send)


def attention_front(weights, tokens, seg_row, small, steps):
    f32, bf16 = jnp.float32, jnp.bfloat16
    w_query, w_key, w_value, w_outgate, w_output, w_gate, w_up, w_down = weights
    half = lambda a: a.shape[1] // PAIR
    proj, place = [], 0
    for arg, a in enumerate((w_query, w_key, w_value, w_outgate)):
        proj.append((arg, 0, half(a), half(a), place))
        place += half(a)
    dim_own, proj_w = w_query.shape[0], place
    out_rows = w_output.shape[0] // PAIR
    out_piece = [(4, out_rows, 0, w_output.shape[1], 0)]
    gu = [(5, 0, half(w_gate), half(w_gate), 0), (6, 0, half(w_up), half(w_up), half(w_gate))]
    gu_shape = (w_gate.shape[0], 2 * half(w_gate))
    down = [(7, 0, 0, w_down.shape[1], 0)]
    w_shapes = [(dim_own, proj_w)] * 2 + [(out_rows, w_output.shape[1])] * 2 + [gu_shape] * 2
    w_shapes.append(w_down.shape)
    own_tok, dim = tokens.shape
    tok = PAIR * own_tok
    spans, keys_w, vals_w = tok // SPAN, half(w_query), half(w_value)
    rank = small[4].shape[1]
    shape_of = dict(
        normed=((tok, dim), bf16), normed_far=((1, tok, dim_own), bf16),
        low_rank=((tok, rank), f32), logits=((tok, keys_w), f32), cumul=((tok, keys_w), f32),
        queries=((tok, keys_w), f32), keys=((tok, keys_w), f32), values=((tok, vals_w), f32),
        outgate=((tok, vals_w), f32), mask=((tok, tok), f32), within=((tok, 1), f32),
        end_doc=((tok, 1), f32), keep=((spans, keys_w, 1), f32),
        factors=((len(steps), keys_w, 1), f32), to_next=((1, 1), f32),
        entered=((spans, keys_w, DV), f32), attn=((tok, vals_w), f32), gated=((tok, vals_w), bf16),
        gated_far=((1, tok, vals_w), bf16), resid=((own_tok, dim), f32),
        normed_two=((own_tok, dim), bf16), gain_one_rel=((1, dim), f32),
        gain_two_rel=((1, dim), f32), head_gain_all=((1, DV), f32),
        rank_in_far=(small[4].shape, bf16), rank_out_core=((rank, keys_w), f32),
    )
    hops = len(steps) + 1
    vm, dma = pltpu.VMEM, pltpu.SemaphoreType.DMA
    scratch = [
        vm(tokens.shape, bf16), vm((4,) + seg_row.shape, f32), vm((4, 1, keys_w), f32),
        vm(small[0].shape, f32), vm(small[1].shape, f32), vm(small[2].shape, f32),
        vm(small[3].shape, f32), vm(small[5].shape, bf16),
        vm((tok, proj_w), f32), vm((tok, vals_w), f32), vm((keys_w, DV), f32),
        vm((hops, keys_w, DV), bf16), vm((hops, keys_w, DV), bf16),
        vm((own_tok, dim), f32), vm((own_tok, dim), f32),
        dma((4, 4)), dma((4, 4)), dma((4, 4)), dma((4, 4)), dma((4, 4)),
        dma((10,)), dma((10,)), dma((3, 4)), dma((3, 4)),
    ]
    any_spec, vmem = pl.BlockSpec(memory_space=pl.ANY), pl.BlockSpec(memory_space=pltpu.VMEM)
    out_shape = [jax.ShapeDtypeStruct(shape, bf16) for shape in w_shapes]
    out_shape += [jax.ShapeDtypeStruct(*shape_of[name]) for name in FrontOut._fields]
    got = pl.pallas_call(
        functools.partial(front_kernel, (proj, out_piece, gu, down), 3, tuple(steps)),
        out_shape=out_shape,
        in_specs=[any_spec] * 8 + [vmem] * len(FrontIn._fields),
        out_specs=[vmem] * len(out_shape),
        scratch_shapes=scratch,
        compiler_params=pltpu.CompilerParams(
            collective_id=0, has_side_effects=True, vmem_limit_bytes=48 * 2**20
        ),
        name="attention_front",
    )(*weights, tokens, seg_row, *small)
    return got[:7], FrontOut(*got[7:])


def core_cols(array_in, c):
    width = array_in.shape[1] // PAIR
    return lax.dynamic_slice_in_dim(array_in, c * width, width, 1)


def dot32(a, b):
    return jnp.dot(a, b, preferred_element_type=jnp.float32)


def dot_t(a, b):
    return lax.dot_general(a, b, (((1,), (1,)), ((), ())), preferred_element_type=jnp.float32)


def grad_dot(pairs_in):
    total = None
    for left, right in pairs_in:
        part = lax.dot_general(
            left, right, (((0,), (0,)), ((), ())), preferred_element_type=jnp.float32
        )
        total = part if total is None else total + part
    return total


def plain_front(at_place, weights, inputs, seg_ids, small, steps):
    f32, bf16 = jnp.float32, jnp.bfloat16
    nb, b, c, t = at_place.nb, at_place.b, at_place.c, at_place.t
    w_query, w_key, w_value, w_outgate, w_output, w_gate, w_up, w_down = weights
    w_rank_in, w_rank_out = small[4], small[5]
    rank = w_rank_in.shape[1]
    heads = HEADS // PAIR
    keys_w, vals_w = KEYS // PAIR, VALS // PAIR
    dim_own = inputs.shape[2] // nb

    in_pair = at_place.pair_all(inputs[0])
    seg_row = at_place.pair_all(seg_ids[0])
    tok_count = seg_row.shape[0]
    half_tok = tok_count // PAIR
    spans = tok_count // SPAN
    edges = jnp.stack([seg_row[0], seg_row[-1]])
    edges_wide = jnp.broadcast_to(edges[:, None], (2, 128)).astype(f32)
    prev_last = at_place.chip_shift(edges_wide, 1)[1, 0]
    next_first = at_place.chip_shift(edges_wide, -1)[0, 0]
    first_id, last_id = edges[0].astype(f32), edges[1].astype(f32)
    from_prev = jnp.logical_and(t > 0, prev_last == first_id).astype(f32)
    to_next = jnp.logical_and(t < at_place.chips - 1, next_first == last_id).astype(f32)
    whole_doc = (first_id == last_id).astype(f32)

    packed = jnp.concatenate([a.reshape(-1) for a in small])
    packed = jnp.stack([packed] + at_place.others(packed))
    parts, at = [], 0
    for a in small:
        parts.append(packed[:, at : at + a.size])
        at += a.size
    gain_one = parts[0].reshape(-1).astype(f32)
    gain_two = parts[1].reshape(-1).astype(f32)
    bias_all = at_place.to_abs(parts[2], 0).reshape(-1).astype(f32)
    bias_w = lax.dynamic_slice_in_dim(bias_all, c * keys_w, keys_w)
    head_gain32 = at_place.to_abs(parts[3], 0).reshape(-1).astype(f32)
    rank_in_w = parts[4].reshape(-1, rank)
    rank_out_all = (
        at_place.to_abs(parts[5], 0).reshape((nb,) + w_rank_out.shape).transpose(1, 0, 2)
        .reshape(rank, -1)
    )
    rank_out_w = core_cols(rank_out_all, c).astype(f32)

    proj_own = jnp.concatenate(
        [core_cols(a, c) for a in (w_query, w_key, w_value, w_outgate)], axis=1
    )
    out_own = lax.dynamic_slice_in_dim(w_output, c * vals_w, vals_w, 0)
    gu_own = jnp.concatenate([core_cols(w_gate, c), core_cols(w_up, c)], axis=1)
    proj_far, out_far, gu_far, down_far = (
        jnp.concatenate(at_place.others(a), axis=0) for a in (proj_own, out_own, gu_own, w_down)
    )
    down_all = at_place.to_abs(jnp.concatenate([w_down, down_far], axis=0), 0)
    ff_half = down_all.shape[0] // PAIR
    down_w = lax.dynamic_slice_in_dim(down_all, c * ff_half, ff_half, 0)
    activation = at_place.to_rel(in_pair, 1).astype(f32)
    scale_one = rms_scale(activation)
    unit_one = activation * scale_one
    normed = (unit_one * gain_one).astype(bf16)
    normed_far = [
        at_place.from_batch(normed[:, (nb - k) * dim_own : (nb - k + 1) * dim_own], k)
        for k in range(1, nb)
    ]

    low_rank = dot32(normed, rank_in_w)
    logits = jnp.dot(low_rank, rank_out_w, precision=top_prec) + bias_w
    decays = jax.nn.log_sigmoid(logits) / 16.0

    seg_s = seg_row.reshape(spans, SPAN)
    first_s, last_s = seg_s[:, 0], seg_s[:, -1]
    row_pos = lax.broadcasted_iota(jnp.int32, (SPAN, SPAN), 0)
    col_pos = lax.broadcasted_iota(jnp.int32, (SPAN, SPAN), 1)
    lower = (col_pos <= row_pos).astype(f32)
    allowed = lower[None] * (seg_s[:, :, None] == seg_s[:, None, :]).astype(f32)
    allowed = allowed[:, None]
    prior = jnp.concatenate([seg_row[:1], last_s[:-1]])
    enters = (first_s == prior).astype(f32)
    within = ((seg_s == first_s[:, None]).astype(f32) * enters[:, None])[:, None, :, None]
    end_doc = (seg_s == last_s[:, None]).astype(f32)[:, None, :, None]

    cumul = mm("ts,nsc->ntc", lower, decays.reshape(spans, SPAN, keys_w))
    total_log = jnp.sum(cumul[:, -1], axis=0)

    proj = dot32(normed[:, :dim_own], proj_own) + dot32(normed[:, dim_own:], proj_far)
    queries = to_spans(proj[:, :keys_w] * DK ** (-0.5), DK)
    keys_s = to_spans(proj[:, keys_w : 2 * keys_w], DK)
    values_s = to_spans(proj[:, 2 * keys_w : 2 * keys_w + vals_w], DV)
    outgate = proj[:, 2 * keys_w + vals_w :]

    cumul = cumul.reshape(spans, SPAN, heads, DK).transpose(0, 2, 1, 3)
    last_cumul = cumul[:, :, -1:, :]
    grow = jnp.exp(cumul)
    shrink = jnp.exp(-cumul)
    to_end = jnp.exp(last_cumul - cumul) * end_doc
    query_dec = queries * grow
    key_dec = keys_s * shrink
    key_end = keys_s * to_end
    query_in = query_dec * within
    keep = jnp.exp(last_cumul[:, :, 0, :]) * within[:, :, -1]
    scores = mm("nhtc,nhsc->nhts", query_dec, key_dec) * allowed
    local_out = mm("nhts,nhsv->nhtv", scores, values_s)
    added = mm("nhsc,nhsv->nhcv", key_end, values_s)

    local_state = added[0]
    for i in range(1, spans):
        local_state = keep[i][:, :, None] * local_state + added[i]

    reach_chips = -(-(SEG_MOST - 1) // tok_count)

    def chip_scan(state, factor, way):
        state = state.reshape(heads * DK, DV)
        step = 1
        pad = jnp.zeros((15, heads * DK), f32)
        while step < min(reach_chips, at_place.chips):
            packed = jnp.concatenate(
                [state, jnp.concatenate([factor[None], pad]).reshape(-1, DV)]
            )
            got = at_place.chip_shift(packed.astype(bf16), way * step).astype(f32)
            state = state + factor[:, None] * got[: heads * DK]
            factor = factor * got[heads * DK :].reshape(16, -1)[0]
            step *= 2
        got = at_place.chip_shift(state.astype(bf16), way)
        return got.astype(f32).reshape(heads, DK, DV)

    block_keep = jnp.exp(total_log) * whole_doc
    carried = from_prev * chip_scan(local_state, block_keep * from_prev, 1)
    enter_list = [carried]
    for i in range(spans - 1):
        enter_list.append(keep[i][:, :, None] * enter_list[i] + added[i])
    entered = jnp.stack(enter_list)

    attn_raw = from_spans(local_out + mm("nhtc,nhcv->nhtv", query_in, entered)).reshape(
        tok_count, heads, DV
    )
    head_scale = head_rms(attn_raw)
    head_norm = attn_raw * head_scale
    gate_h = outgate.reshape(tok_count, heads, DV)
    gate_sig = jax.nn.sigmoid(gate_h)
    gate_act = gate_h * gate_sig
    gated = (head_norm * head_gain32 * gate_act).reshape(tok_count, vals_w).astype(bf16)
    gated_far = at_place.others(gated)
    out_w = jnp.concatenate(
        [out_own] + [out_far[k * vals_w : (k + 1) * vals_w] for k in range(nb - 1)], axis=1
    )
    own_rows = lambda a: lax.dynamic_slice_in_dim(a, c * half_tok, half_tok, 0)
    resid = own_rows(activation) + at_place.pair_sum(dot32(gated, out_w))
    normed_two = (resid * rms_scale(resid) * gain_two).astype(bf16)
    col = lambda a: a.reshape(-1, 1)
    factor = block_keep * to_next
    factors = []
    for step in steps or [1]:
        factors.append(col(factor))
        if step != steps[-1]:
            factor = factor * at_place.chip_shift(factor, -step)
    in_span = jnp.arange(tok_count) // SPAN
    mask = jnp.logical_and(
        jnp.logical_and(in_span[:, None] == in_span, seg_row[:, None] == seg_row),
        jnp.tril(jnp.ones((tok_count, tok_count), bool)),
    )
    front = FrontOut(
        normed=normed, normed_far=jnp.stack(normed_far), low_rank=low_rank, logits=logits,
        cumul=from_spans(cumul), queries=from_spans(queries), keys=from_spans(keys_s),
        values=from_spans(values_s), outgate=outgate, mask=mask.astype(f32), within=col(within),
        end_doc=col(end_doc), keep=keep.reshape(spans, keys_w, 1), factors=jnp.stack(factors),
        to_next=to_next.reshape(1, 1), entered=entered.reshape(spans, keys_w, DV),
        attn=attn_raw.reshape(tok_count, vals_w), gated=gated, gated_far=jnp.stack(gated_far),
        resid=resid, normed_two=normed_two, gain_one_rel=gain_one[None],
        gain_two_rel=gain_two[None], head_gain_all=head_gain32[None],
        rank_in_far=rank_in_w[dim_own:], rank_out_core=rank_out_w,
    )
    return (proj_own, proj_far, out_own, out_far, gu_own, gu_far, down_w), front


def plain_end(
    at_place, front, small, inputs, rank_in_w, normed_grad, grad_logits, grad_headgain, grad_resid,
    grad_gain_two,
):
    f32, bf16 = jnp.float32, jnp.bfloat16
    nb, low_rank, normed = at_place.nb, front.low_rank, front.normed
    gain_one, rank_out_w, rank = front.gain_one_rel[0], front.rank_out_core, small[4].shape[1]
    grad_bias = jnp.sum(grad_logits, axis=0)
    grad_rank_out = jnp.dot(low_rank.T, grad_logits, precision=top_prec)
    grad_low = jnp.dot(grad_logits, rank_out_w.T, precision=top_prec).astype(bf16)
    normed_grad = normed_grad + dot_t(grad_low, rank_in_w)
    grad_normed = at_place.pair_sum(normed_grad)
    own_in = at_place.to_rel(inputs[0], 1).astype(f32)
    scale_one = rms_scale(own_in)
    unit_own = own_in * scale_one
    grad_gain_one = jnp.sum(grad_normed * unit_own, axis=0)
    scaled_one = grad_normed * gain_one
    grad_input = (
        grad_resid
        + scale_one
        * (scaled_one - unit_own * jnp.mean(scaled_one * unit_own, axis=-1, keepdims=True))
    ).astype(bf16)
    grad_rank_in = grad_dot([(normed, grad_low)])

    def own_slot(part):
        return at_place.by_core(part, jnp.zeros_like(part), part.ndim - 1)

    by_owner = jnp.concatenate(
        [
            grad_gain_one.reshape(nb, -1),
            grad_gain_two.reshape(nb, -1),
            at_place.to_rel(own_slot(grad_bias).reshape(nb, -1), 0),
            at_place.to_rel(grad_headgain.reshape(nb, -1), 0),
            grad_rank_in.reshape(nb, -1),
            at_place.to_rel(
                own_slot(grad_rank_out).reshape(rank, nb, -1).transpose(1, 0, 2).reshape(nb, -1), 0
            ),
        ],
        axis=1,
    )
    owned = at_place.total_sum(by_owner)
    outs, at = [], 0
    for a in small:
        outs.append(owned[at : at + a.size].reshape(a.shape))
        at += a.size
    return tuple(outs), at_place.to_abs(grad_input, 1)


def per_device(
    inputs,
    seg_ids,
    gain_attn,
    w_query,
    w_key,
    w_value,
    w_outgate,
    w_rank_in,
    w_rank_out,
    rank_bias,
    head_gain,
    w_output,
    gain_ffn,
    w_gate,
    w_up,
    w_down,
    cotangent,
):
    f32 = jnp.float32
    bf16 = jnp.bfloat16
    at_place = Places()
    nb, b, c, t = at_place.nb, at_place.b, at_place.c, at_place.t
    rank = w_rank_in.shape[1]
    heads = HEADS // PAIR
    keys_w, vals_w = KEYS // PAIR, VALS // PAIR
    dim = inputs.shape[2]
    dim_own = dim // nb

    weights = (w_query, w_key, w_value, w_outgate, w_output, w_gate, w_up, w_down)
    small = (gain_attn, gain_ffn, rank_bias, head_gain, w_rank_in, w_rank_out)
    tok_count = PAIR * inputs.shape[1]
    half_tok = inputs.shape[1]
    reach_chips = -(-(SEG_MOST - 1) // tok_count)
    steps, step = [], 1
    while step < min(reach_chips, at_place.chips):
        steps.append(step)
        step *= 2
    paired = nb == 2 and at_place.ns % 8 == 0 and len(steps) in (1, 2)
    if paired:
        rows = [a.reshape(1, -1).astype(f32) for a in small[:4]]
        moved, front = attention_front(
            weights, inputs[0], seg_ids.astype(f32), rows + [w_rank_in, w_rank_out], steps
        )
    else:
        moved, front = plain_front(at_place, weights, inputs, seg_ids, small, steps)
    proj_own, proj_far, out_own, out_far, gu_own, gu_far, down_w = moved
    gain_one, gain_two = front.gain_one_rel[0], front.gain_two_rel[0]
    normed, low_rank, resid = front.normed, front.low_rank, front.resid
    normed_two, rank_out_w = front.normed_two, front.rank_out_core
    rank_in_w = jnp.concatenate([w_rank_in, front.rank_in_far], axis=0)
    out_w = jnp.concatenate(
        [out_own] + [out_far[k * vals_w : (k + 1) * vals_w] for k in range(nb - 1)], axis=1
    )
    ff_c = down_w.shape[0]

    cot_own = cotangent[0]
    cot_pair = at_place.pair_all(cot_own)
    cot_far = [at_place.pair_all(a) for a in at_place.others(cot_own)]

    scale_two = rms_scale(resid)
    unit_two = resid * scale_two

    two_pair = at_place.pair_all(normed_two)
    two_far = [
        at_place.pair_all(jnp.roll(a, (k + 1) * dim_own, 1))
        for k, a in enumerate(at_place.others(normed_two))
    ]

    def feed_forward(two_rows, cot_rows):
        pre = dot32(two_rows[:, :dim_own], gu_own) + dot32(two_rows[:, dim_own:], gu_far)
        gate_pre, up_pre = pre[:, :ff_c], pre[:, ff_c:]
        sig = jax.nn.sigmoid(gate_pre)
        hidden = (gate_pre * sig * up_pre).astype(bf16)
        grad_hidden = dot_t(cot_rows, down_w)
        grad_gu = jnp.concatenate(
            [
                (grad_hidden * up_pre * silu_grad(gate_pre, sig)).astype(bf16),
                (grad_hidden * gate_pre * sig).astype(bf16),
            ],
            axis=1,
        )
        return hidden, grad_gu

    hidden, grad_gu = feed_forward(two_pair, cot_pair)
    down_sum = at_place.pair_sum(dot32(hidden, down_w))
    output = (at_place.to_abs(resid, 1) + down_sum).astype(bf16)

    two_grad = jnp.concatenate([dot_t(grad_gu, gu_own), dot_t(grad_gu, gu_far)], axis=1)
    grad_two = at_place.pair_sum(two_grad)

    hid_own = [at_place.pair_all(hidden, 1)]
    gu_pairs = [(two_pair[:, :dim_own], grad_gu)]
    down_cots = [cot_pair]
    for two_rows, cot_rows in zip(two_far, cot_far):
        far_hidden, far_grad = feed_forward(two_rows, cot_rows)
        gu_pairs.append((two_rows[:, :dim_own], far_grad))
        hid_own.append(at_place.pair_all(far_hidden, 1))
        down_cots.append(cot_rows)
    ff_own = hid_own[0].shape[1] // nb
    down_pairs = [
        (lax.dynamic_slice_in_dim(h, b * ff_own, ff_own, 1), core_cols(g, c))
        for h, g in zip(hid_own, down_cots)
    ]
    part_gate = grad_dot([(left, right[:, :ff_c]) for left, right in gu_pairs]).astype(bf16)
    part_up = grad_dot([(left, right[:, ff_c:]) for left, right in gu_pairs]).astype(bf16)
    part_down = grad_dot(down_pairs).astype(bf16)

    grad_gain_two = jnp.sum(grad_two * unit_two, axis=0)
    scaled_two = grad_two * gain_two
    grad_resid = at_place.to_rel(cot_own, 1).astype(f32) + scale_two * (
        scaled_two - unit_two * jnp.mean(scaled_two * unit_two, axis=-1, keepdims=True)
    )
    resid_pair = at_place.pair_all(grad_resid.astype(bf16))
    resid_far = [
        at_place.from_batch(resid_pair[:, (nb - k) * dim_own : (nb - k + 1) * dim_own], k)
        for k in range(1, nb)
    ]
    chunks = at_place.chips
    cut = lambda a: a.reshape(chunks, -1, a.shape[1])
    jobs = ((True, True), (False, True), (True, True), (True, True), (True, True))
    if paired:
        jobs += ((True, False),)
    order = (0, 1, 2, -1, 3, -1, 1, -1, -1, 0, 1, -1, -1, -1, 0, 1, 2, -1, 0, 1, 2, 3, -1, 0, 1, -1, 2, 3, -1, 0, -1, 1, 2, -1, 0, 3, -1, -1, 1, 2, -1, 0, 3, -1, -1, 1, -1, -1, 2, 3, -1, -1, -1, 0, -1, 4, 2, -1, 3, -1, 5, 3, 4, 4, 4, 2, 5, 4, 5, 3, 4, 5, 4, 5, 4, 5, 5, 5, 4, 5)
    mine, theirs, (normed_grad, grad_logits, headgain_row, grad_input) = attention_back(
        BackIn(
            **{k: v for k, v in front._asdict().items() if k in BackIn._fields},
            gate_part=cut(part_gate), down_part=cut(part_down), up_part=cut(part_up),
            resid_pair=resid_pair, resid_far=jnp.stack(resid_far), out_w=out_w,
            head_gain=front.head_gain_all, proj_own=proj_own, proj_far=proj_far,
            rank_in=rank_in_w, tokens=inputs[0], grad_resid=grad_resid,
            grad_gain_two=grad_gain_two[None],
        ),
        jobs, order, at_place.ny, at_place.nz, nb, steps,
    )
    if paired:
        rows = mine[5].reshape(-1, DV)
        gain_rows = dim_own // DV
        in_rows = rows[2 * rank :].reshape(gain_rows, rank, DV).transpose(0, 2, 1)
        small_grads = (
            rows[:gain_rows].reshape(-1), rows[2 : 2 + gain_rows].reshape(-1), rows[4],
            rows[5, : head_gain.shape[0]], in_rows.reshape(dim_own, rank), rows[rank : 2 * rank],
        )
    else:
        small_grads, grad_input = plain_end(
            at_place, front, small, inputs, rank_in_w, normed_grad, grad_logits, headgain_row[0],
            grad_resid, grad_gain_two,
        )
    g_gain_one, g_gain_two, g_bias, g_headgain, g_rank_in, g_rank_out = small_grads

    mine = [a.reshape(-1, a.shape[2]) for a in mine[:5]]
    theirs = [a.reshape(-1, a.shape[2]) for a in theirs]

    def both(i, lo, hi, axis=1):
        return at_place.by_core(mine[i][:, lo:hi], theirs[i][:, lo:hi], axis).astype(f32)

    g_gate = both(0, 0, ff_c)
    g_down = both(1, 0, part_down.shape[1])
    g_up = both(2, 0, ff_c)
    g_output = both(3, 0, dim_own, 0)
    g_query = both(4, 0, keys_w)
    g_key = both(4, keys_w, 2 * keys_w)
    g_value = both(4, 2 * keys_w, 2 * keys_w + vals_w)
    g_outgate = both(4, 2 * keys_w + vals_w, 2 * keys_w + 2 * vals_w)
    return (
        output[None],
        grad_input[None],
        g_gain_one,
        g_query,
        g_key,
        g_value,
        g_outgate,
        g_rank_in,
        g_rank_out,
        g_bias,
        g_headgain,
        g_output,
        g_gain_two,
        g_gate,
        g_up,
        g_down,
    )


def solution(mesh):
    in_specs = (
        P("batch", "seq", None),
        P("batch", "seq"),
        P("batch"),
        P("batch", None),
        P("batch", None),
        P("batch", None),
        P("batch", None),
        P("batch", None),
        P(None, "batch"),
        P("batch"),
        P("batch"),
        P(None, "batch"),
        P("batch"),
        P("batch", None),
        P("batch", None),
        P("batch", None),
        P("batch", "seq", None),
    )
    out_specs = (
        P("batch", "seq", None),
        P("batch", "seq", None),
        P("batch"),
        P("batch", None),
        P("batch", None),
        P("batch", None),
        P("batch", None),
        P("batch", None),
        P(None, "batch"),
        P("batch"),
        P("batch"),
        P(None, "batch"),
        P("batch"),
        P("batch", None),
        P("batch", None),
        P("batch", None),
    )
    return jax.shard_map(
        per_device, mesh=mesh, in_specs=in_specs, out_specs=out_specs, check_vma=False
    )
```

```python
import functools
from types import SimpleNamespace
from typing import Any, NamedTuple

import jax
import jax.numpy as jnp
from jax import lax
from jax.experimental import pallas as pl
from jax.experimental.pallas import tpu as pltpu
from jax.sharding import PartitionSpec as P

HEADS = 4
DK = 128
DV = 256
SPAN = 64
KEYS = 512
VALS = 1024


norm_eps = 1e-05
head_eps = 0.1
top_prec = lax.Precision.HIGHEST
BOTH = ("batch", "seq")
SEG_MOST = 1024
PAIR = 2


def rms_scale(values_in):
    return lax.rsqrt(jnp.mean(values_in * values_in, axis=-1, keepdims=True) + norm_eps)


def head_rms(values_in):
    return lax.rsqrt(jnp.mean(values_in * values_in, axis=-1, keepdims=True) + head_eps)


def silu_grad(pre_act, sig_val):
    return sig_val * (1.0 + pre_act * (1.0 - sig_val))


def mm(eq, a, b):
    return jnp.einsum(eq, a, b, precision=top_prec)


def to_spans(array_in, width):
    return array_in.reshape(-1, SPAN, array_in.shape[1] // width, width).transpose(0, 2, 1, 3)


def from_spans(array_in):
    spans, heads, span_len, width = array_in.shape
    return array_in.transpose(0, 2, 1, 3).reshape(spans * span_len, heads * width)


class Places:
    def __init__(self):
        self.nb = lax.axis_size("batch")
        self.ns = lax.axis_size("seq")
        self.b = lax.axis_index("batch")
        self.s = lax.axis_index("seq")
        self.c = self.s % PAIR
        self.t = self.s // PAIR
        self.chips = self.ns // PAIR
        self.ny = 2 if self.chips % 2 == 0 else 1
        self.nz = self.chips // self.ny
        self.y = self.t % self.ny
        self.z = self.t // self.ny

    def seq_hop(self, array_in, pairs):
        return lax.ppermute(array_in, "seq", pairs)

    def pair_hop(self, array_in):
        return self.seq_hop(array_in, [(i, i ^ 1) for i in range(self.ns)])

    def chip_shift(self, array_in, by):
        step = by * PAIR
        return self.seq_hop(
            array_in, [(i, i + step) for i in range(self.ns) if 0 <= i + step < self.ns]
        )

    def from_batch(self, array_in, k):
        nb = self.nb
        return lax.ppermute(array_in, "batch", [((d + k) % nb, d) for d in range(nb)])

    def others(self, array_in):
        return [self.from_batch(array_in, k) for k in range(1, self.nb)]

    def by_core(self, mine, other, axis):
        return jnp.where(
            self.c == 0,
            jnp.concatenate([mine, other], axis),
            jnp.concatenate([other, mine], axis),
        )

    def pair_all(self, mine, axis=0):
        return self.by_core(mine, self.pair_hop(mine), axis)

    def pair_sum(self, partial):
        rows = partial.shape[0] // PAIR
        own = lax.dynamic_slice_in_dim(partial, self.c * rows, rows, 0)
        away = lax.dynamic_slice_in_dim(partial, (1 - self.c) * rows, rows, 0)
        return own + self.pair_hop(away)

    def to_rel(self, array_in, axis):
        nb = self.nb
        width = array_in.shape[axis] // nb
        if nb == 2:
            low = lax.slice_in_dim(array_in, 0, width, axis=axis)
            high = lax.slice_in_dim(array_in, width, 2 * width, axis=axis)
            return jnp.where(
                self.b == 0,
                jnp.concatenate([low, high], axis),
                jnp.concatenate([high, low], axis),
            )
        return jnp.roll(array_in, -self.b * width, axis)

    def to_abs(self, array_in, axis):
        if self.nb == 2:
            return self.to_rel(array_in, axis)
        return jnp.roll(array_in, self.b * (array_in.shape[axis] // self.nb), axis)

    def total_sum(self, rel_rows):
        nb = self.nb
        total = rel_rows[0]
        for k in range(1, nb):
            total = total + self.from_batch(rel_rows[nb - k], k)
        step = 1
        while step < self.ns:
            total = total + self.seq_hop(total, [(i, i ^ step) for i in range(self.ns)])
            step *= 2
        return total


MESH_ID = pl.DeviceIdType.MESH


def plane_plans(ny, nz, jobs, grads, sums, swapped, first_in, second_in, halfway, sems, greet):
    send_sems, recv_sems = sems
    s = lax.axis_index("seq")
    t = s // PAIR
    y, z = lax.rem(t, ny), t // ny
    partner = s + 1 - 2 * lax.rem(s, PAIR)
    axes = {"y": (ny, y, PAIR), "z": (nz, z, PAIR * ny)}

    barrier = pltpu.get_barrier_semaphore()

    def signal(to, axis="seq"):
        pl.semaphore_signal(barrier, inc=1, device_id={axis: to}, device_id_type=MESH_ID)

    signal(partner)
    distances, nb = greet
    chips = ny * nz
    b = lax.axis_index("batch")
    for k in range(1, nb):
        signal(lax.rem(b + k, nb), "batch")
    for d in distances:
        pl.when(t >= d)(lambda: signal(s - PAIR * d))
        pl.when(t < chips - d)(lambda: signal(s + PAIR * d))
    for n, pos, stride in axes.values():
        if n > 1:
            pl.when(pos > 0)(lambda: signal(s - stride))
            pl.when(pos < n - 1)(lambda: signal(s + stride))
    peers = nb
    for n, pos, stride in axes.values():
        peers = peers + (pos + n - 1) // n + (2 * n - 2 - pos) // n
    for d in distances:
        peers = peers + (t + chips - d) // chips + (2 * chips - 1 - d - t) // chips
    pl.semaphore_wait(barrier, peers)

    def add_blocks(dst, left, right):
        def one(i, carry):
            dst[i] = (left[i].astype(jnp.float32) + right[i].astype(jnp.float32)).astype(dst.dtype)
            return carry

        lax.fori_loop(0, dst.shape[0], one, 0)

    def line(job, phase, axis):
        n, pos, stride = axes[axis]
        ways = []
        for way in (0, 1):
            q = pos if way == 0 else n - 1 - pos
            to = s + stride if way == 0 else s - stride

            def real(m, way=way):
                return m if way == 0 else n - 1 - m

            def copy(src, dst, step, way=way, to=to):
                return pltpu.make_async_remote_copy(
                    src_ref=src,
                    dst_ref=dst,
                    send_sem=send_sems.at[job, phase, way, step - 1],
                    recv_sem=recv_sems.at[job, phase, way, step - 1],
                    device_id={"seq": to},
                    device_id_type=MESH_ID,
                )

            ways.append((q, real, copy, way))
        return n, pos, ways

    def scatter_stages(job, phase, axis, src, size, arrivals, finish):
        n, pos, ways = line(job, phase, axis)

        def block(i):
            return src.at[pl.ds(i * size, size)]

        def step_stage(step):
            for q, real, copy, way in ways:
                slot = arrivals.at[way, step - 1]

                @pl.when(q == 0)
                def _():
                    copy(block(real(n - step)), slot, step).start()

                if step > 1:
                    before = arrivals.at[way, step - 2]

                    @pl.when(jnp.logical_and(q >= 1, q <= min(step - 1, n - 2)))
                    def _():
                        copy(before, before, step - 1).wait_recv()
                        add_blocks(before, before, block(real(q + n - step)))
                        copy(before, slot, step).start()

        def last():
            dst = finish()
            own = block(pos)
            (q0, _, copy0, _), (q1, _, copy1, _) = ways
            last_r, last_l = arrivals.at[0, n - 2], arrivals.at[1, n - 2]

            @pl.when(q0 == 0)
            def _():
                copy1(last_l, last_l, n - 1).wait_recv()
                add_blocks(dst, own, last_l)

            @pl.when(q0 > 0)
            def _():
                copy0(last_r, last_r, n - 1).wait_recv()
                add_blocks(dst, own, last_r)

            if n > 2:

                @pl.when(jnp.logical_and(q0 > 0, q1 > 0))
                def _():
                    copy1(last_l, last_l, n - 1).wait_recv()
                    add_blocks(dst, dst, last_l)

        def drain():
            for step in range(1, n):
                for q, real, copy, way in ways:
                    slot = arrivals.at[way, step - 1]
                    pl.when(q <= min(step - 1, n - 2))(
                        lambda copy=copy, slot=slot, step=step: copy(slot, slot, step).wait_send()
                    )

        return [functools.partial(step_stage, i) for i in range(1, n)], last, drain

    def gather_stages(job, phase, axis, buf, base, size):
        n, pos, ways = line(job, phase, axis)

        def block(i):
            return buf.at[pl.ds(base + i * size, size)]

        def stage(step):
            for q, real, copy, way in ways:
                if step > 1:
                    here = block(real(q - step + 1))
                    pl.when(q >= step - 1)(
                        lambda copy=copy, here=here: copy(here, here, step - 1).wait_recv()
                    )
                if step < n:
                    here = block(real(q - step + 1))
                    pl.when(jnp.logical_and(q >= step - 1, q <= n - 2))(
                        lambda copy=copy, here=here: copy(here, here, step).start()
                    )

        def drain():
            for step in range(1, n):
                for q, real, copy, way in ways:
                    here = block(real(q - step + 1))
                    pl.when(jnp.logical_and(q >= step - 1, q <= n - 2))(
                        lambda copy=copy, here=here, step=step: copy(here, here, step).wait_send()
                    )

        return [functools.partial(stage, i) for i in range(1, n + 1)], drain

    plans, drains = [], []
    for job, (y_first, swaps) in enumerate(jobs):
        one, two = ("y", "z") if y_first else ("z", "y")
        n_one, pos_one, _ = axes[one]
        n_two, pos_two, _ = axes[two]
        stages = []
        own_at = pos_one * n_two + pos_two
        source = grads[job]
        if n_one > 1:
            steps, last, drain = scatter_stages(
                job, 0, one, source, n_two, first_in[job], lambda job=job: halfway[job]
            )
            stages += steps
            drains.append(drain)
            close = last
        else:

            def close(job=job):
                def one_block(i, carry):
                    halfway[job][i] = grads[job][i]
                    return carry

                lax.fori_loop(0, halfway[job].shape[0], one_block, 0)

        if n_two > 1:
            steps, last, drain = scatter_stages(
                job,
                1,
                two,
                halfway[job],
                1,
                second_in[job],
                lambda job=job, own_at=own_at: sums[job].at[pl.ds(own_at, 1)],
            )
            drains.append(drain)
            stages.append(lambda close=close, step=steps[0]: (close(), step()))
            stages += steps[1:]
            close = last
        else:

            def close(job=job, own_at=own_at, before=close):
                before()
                sums[job][own_at] = halfway[job][0]

        gathers = []
        if n_two > 1:
            steps, drain = gather_stages(job, 2, two, sums[job], pos_one * n_two, 1)
            drains.append(drain)
            gathers += [steps]
        if n_one > 1:
            steps, drain = gather_stages(job, 3, one, sums[job], 0, n_two)
            drains.append(drain)
            gathers += [steps]
        pending = close
        for steps in gathers:
            stages.append(lambda pending=pending, step=steps[0]: (pending(), step()))
            stages += steps[1:-1]
            pending = steps[-1]

        if not swaps:
            stages.append(pending)
            plans.append(stages)
            continue

        def swap(job=job):
            return pltpu.make_async_remote_copy(
                src_ref=sums[job],
                dst_ref=swapped[job],
                send_sem=send_sems.at[job, 4, 0, 0],
                recv_sem=recv_sems.at[job, 4, 0, 0],
                device_id={"seq": partner},
                device_id_type=MESH_ID,
            )

        stages.append(lambda pending=pending, swap=swap: (pending(), swap().start()))
        drains.append(lambda swap=swap: swap().wait())
        plans.append(stages)

    return plans, drains


def high(a, b, dims=((1,), (0,))):
    return lax.dot_general(
        a, b, (dims, ((), ())), precision=top_prec, preferred_element_type=jnp.float32
    )


def low(a, b, dims=((1,), (0,))):
    a, b = a.astype(jnp.bfloat16), b.astype(jnp.bfloat16)
    return lax.dot_general(a, b, (dims, ((), ())), preferred_element_type=jnp.float32)


def split(a):
    top = a.astype(jnp.bfloat16)
    return top, (a - top.astype(jnp.float32)).astype(jnp.bfloat16)


def mid(a, b, dims=((1,), (0,))):
    (a_top, a_rest), (b_top, b_rest) = split(a), split(b)
    return low(a_top, b_top, dims) + (low(a_top, b_rest, dims) + low(a_rest, b_top, dims))


def counted(ones, b, dims=((1,), (0,))):
    top, rest = split(b)
    return low(ones, top, dims) + low(ones, rest, dims)


ROWS_OF = ((1,), (1,))
COLS_OF = ((0,), (0,))
class BackIn(NamedTuple):
    gate_part: Any = None
    down_part: Any = None
    up_part: Any = None
    resid_pair: Any = None
    resid_far: Any = None
    gated: Any = None
    gated_far: Any = None
    out_w: Any = None
    attn: Any = None
    outgate: Any = None
    head_gain: Any = None
    queries: Any = None
    keys: Any = None
    values: Any = None
    cumul: Any = None
    entered: Any = None
    mask: Any = None
    within: Any = None
    end_doc: Any = None
    keep: Any = None
    factors: Any = None
    to_next: Any = None
    logits: Any = None
    normed: Any = None
    normed_far: Any = None
    proj_own: Any = None
    proj_far: Any = None
    rank_in: Any = None
    rank_out_core: Any = None
    low_rank: Any = None
    tokens: Any = None
    grad_resid: Any = None
    gain_one_rel: Any = None
    grad_gain_two: Any = None


class BackOut(NamedTuple):
    normed_grad: Any = None
    grad_logits: Any = None
    grad_headgain: Any = None
    grad_input: Any = None


class BackTmp(NamedTuple):
    out_part: Any = None
    proj_part: Any = None
    grad_o: Any = None
    reach: Any = None
    grad_qd: Any = None
    grad_kd: Any = None
    grad_v: Any = None
    proj_grad: Any = None
    proj_grad_far: Any = None
    proj_acc: Any = None
    grad_rows: Any = None
    rows_away: Any = None
    rows_come: Any = None
    small_own: Any = None
    small_other: Any = None
    small_come: Any = None
    small_part: Any = None


def back_kernel(ny, nz, nb, steps, jobs, order, *refs):
    f32, bf16 = jnp.float32, jnp.bfloat16
    nj = len(jobs)
    refs = list(refs)

    def take(n):
        out = refs[:n]
        del refs[:n]
        return out

    r = SimpleNamespace(**dict(zip(BackIn._fields, take(len(BackIn._fields)))))
    sums = take(nj)
    swapped = take(5)
    vars(r).update(zip(BackOut._fields, take(len(BackOut._fields))))
    first_in, second_in, halfway = take(nj), take(nj), take(nj)
    vars(r).update(zip(BackTmp._fields, take(len(BackTmp._fields))))
    going, coming = take(2)
    sems, scan_sems, batch_sems, small_sems = take(2), take(2), take(2), take(2)
    grads = [r.gate_part, r.down_part, r.up_part, r.out_part, r.proj_part, r.small_part][:nj]
    ends_here = nj > 5
    plans, drains = plane_plans(
        ny, nz, jobs, grads, sums, swapped, first_in, second_in, halfway, sems, (steps, nb)
    )
    s, b = lax.axis_index("seq"), lax.axis_index("batch")
    t = s // PAIR
    chips = ny * nz
    spans = r.entered.shape[0]
    heads = r.queries.shape[1] // DK
    keys_w, vals_w = heads * DK, heads * DV
    dim_own = r.resid_far.shape[2]

    def put_chunks(ref, value):
        rows = ref.shape[1]
        for i in range(ref.shape[0]):
            ref[i] = value[i * rows : (i + 1) * rows].astype(ref.dtype)

    if ends_here:
        r.normed_grad[...] = jnp.zeros_like(r.normed_grad)
    else:
        r.grad_input[...] = jnp.zeros_like(r.grad_input)

    def out_grad():
        total = lax.dot_general(
            r.gated[...], r.resid_pair[:, :dim_own], (COLS_OF, ((), ())),
            preferred_element_type=f32,
        )
        for k in range(nb - 1):
            total = total + lax.dot_general(
                r.gated_far[k], r.resid_far[k], (COLS_OF, ((), ())),
                preferred_element_type=f32,
            )
        put_chunks(r.out_part, total)

    def head_back(h):
        gains = r.head_gain[...]
        total = jnp.zeros_like(gains) if h == 0 else r.grad_headgain[...]
        for h in (h,):
            cols = pl.ds(h * DV, DV)
            grad_gated = dot_t(r.resid_pair[...], r.out_w[cols, :])
            raw = r.attn[:, cols]
            scale = head_rms(raw)
            norm = raw * scale
            gate = r.outgate[:, cols]
            sig = jax.nn.sigmoid(gate)
            act = gate * sig
            total = total + jnp.sum(grad_gated * norm * act, axis=0, keepdims=True)
            r.proj_grad[:, pl.ds(2 * keys_w + vals_w + h * DV, DV)] = (
                grad_gated * norm * gains * silu_grad(gate, sig)
            ).astype(bf16)
            weighted = grad_gated * gains * act
            r.grad_o[:, cols] = scale * (
                weighted - norm * jnp.mean(weighted * norm, axis=-1, keepdims=True)
            )
        r.grad_headgain[...] = total

    def span_parts(n, h):
        rows, kc, vc = pl.ds(n * SPAN, SPAN), pl.ds(h * DK, DK), pl.ds(h * DV, DV)
        cum = r.cumul[rows, kc]
        last = cum[SPAN - 1 : SPAN]
        to_end = jnp.exp(last - cum) * r.end_doc[rows]
        keys = r.keys[rows, kc]
        grow, shrink = jnp.exp(cum), jnp.exp(-cum)
        return dict(
            rows=rows, kc=kc, vc=vc, last=last, grow=grow, shrink=shrink, to_end=to_end,
            query_dec=r.queries[rows, kc] * grow,
            key_dec=keys * shrink,
            key_end=keys * to_end,
            values=r.values[rows, vc],
            grad_o=r.grad_o[rows, vc],
            within=r.within[rows],
        )

    def keep_of(n, h):
        return r.keep[n, pl.ds(h * DK, DK)]

    def scan_copy(step, by):
        return pltpu.make_async_remote_copy(
            src_ref=going.at[step],
            dst_ref=coming.at[step],
            send_sem=scan_sems[0].at[step],
            recv_sem=scan_sems[1].at[step],
            device_id={"seq": s - PAIR * by},
            device_id_type=MESH_ID,
        )

    hops = list(steps) + [1]

    def reach_local(h):
        for h in (h,):
            local = None
            for n in reversed(range(spans)):
                p = span_parts(n, h)
                reach = low(p["query_dec"] * p["within"], p["grad_o"], COLS_OF)
                r.reach[n, pl.ds(h * DK, DK)] = reach
                local = reach if local is None else keep_of(n, h) * local + reach
            going[0, pl.ds(h * DK, DK)] = local.astype(bf16)
            r.reach[spans, pl.ds(h * DK, DK)] = local

    def scan_start(i):
        pl.when(t >= hops[i])(lambda: scan_copy(i, hops[i]).start())

    def scan_join(i):
        @pl.when(t < chips - hops[i])
        def _():
            scan_copy(i, hops[i]).wait_recv()
            r.reach[spans] += r.factors[i] * coming[i].astype(f32)

        going[i + 1] = r.reach[spans].astype(bf16)
        scan_start(i + 1)

    def scan_end():
        i = len(hops) - 1

        @pl.when(t < chips - 1)
        def _():
            scan_copy(i, 1).wait_recv()
            r.reach[spans] = r.to_next[...] * coming[i].astype(f32)

        @pl.when(t == chips - 1)
        def _():
            r.reach[spans] = jnp.zeros_like(r.reach[spans])

    def local_back(h):
        seen = r.mask[...] > 0.0
        for h in (h,):
            kc, vc = pl.ds(h * DK, DK), pl.ds(h * DV, DV)
            cum = r.cumul[:, kc]
            query_dec = r.queries[:, kc] * jnp.exp(cum)
            key_dec = r.keys[:, kc] * jnp.exp(-cum)
            grad_o = r.grad_o[:, vc]
            scores = jnp.where(seen, low(query_dec, key_dec, ROWS_OF), 0.0)
            r.grad_v[:, vc] = low(scores, grad_o, COLS_OF)
            grad_scores = jnp.where(seen, mid(grad_o, r.values[:, vc], ROWS_OF), 0.0)
            r.grad_qd[:, kc] = mid(grad_scores, key_dec)
            r.grad_kd[:, kc] = mid(grad_scores, query_dec, COLS_OF)
            for n in range(spans):
                rows = pl.ds(n * SPAN, SPAN)
                r.grad_qd[rows, kc] += r.within[rows] * mid(
                    r.grad_o[rows, vc], r.entered[n, kc], ROWS_OF
                )

    def state_back(h):
        row_pos = lax.broadcasted_iota(jnp.int32, (SPAN, SPAN), 0)
        col_pos = lax.broadcasted_iota(jnp.int32, (SPAN, SPAN), 1)
        lower = (col_pos <= row_pos).astype(f32)
        ones = jnp.ones((8, DV), f32)
        for h in (h,):
            hk = pl.ds(h * DK, DK)
            ends = r.reach[spans, hk]
            for n in reversed(range(spans)):
                p = span_parts(n, h)
                rows, kc, vc = p["rows"], p["kc"], p["vc"]
                r.proj_grad[rows, pl.ds(2 * keys_w + h * DV, DV)] = (
                    r.grad_v[rows, vc] + low(p["key_end"], ends)
                ).astype(bf16)
                grad_ke = mid(p["values"], ends, ROWS_OF)
                moved = grad_ke * p["key_end"]
                kept = jnp.exp(p["last"]) * p["within"][SPAN - 1 : SPAN]
                across = counted(ones, ends * r.entered[n, hk], ROWS_OF)[:1]
                grad_last = jnp.sum(moved, axis=0, keepdims=True) + kept * across
                grad_qd, grad_kd = r.grad_qd[rows, kc], r.grad_kd[rows, kc]
                grad_cumul = grad_qd * p["query_dec"] - grad_kd * p["key_dec"] - moved
                grad_d = counted(lower, grad_cumul, COLS_OF) + grad_last
                r.grad_logits[rows, kc] = grad_d * jax.nn.sigmoid(-r.logits[rows, kc]) / 16.0
                r.proj_grad[rows, kc] = (grad_qd * p["grow"] * DK ** (-0.5)).astype(bf16)
                r.proj_grad[rows, pl.ds(keys_w + h * DK, DK)] = (
                    grad_kd * p["shrink"] + grad_ke * p["to_end"]
                ).astype(bf16)
                ends = keep_of(n, h) * ends + r.reach[n, hk]

    def send_batch():
        for copy in batch_copies:
            copy.start()

    batch_copies = [
        pltpu.make_async_remote_copy(
            src_ref=r.proj_grad,
            dst_ref=r.proj_grad_far.at[nb - 1 - k],
            send_sem=batch_sems[0].at[k - 1],
            recv_sem=batch_sems[1].at[nb - 1 - k],
            device_id={"batch": lax.rem(b + k, nb)},
            device_id_type=MESH_ID,
        )
        for k in range(1, nb)
    ]

    wide = 512

    def proj_back(at):
        cols = pl.ds(at, wide)
        r.proj_acc[:, cols] = lax.dot_general(
            r.normed[:, :dim_own], r.proj_grad[:, cols], (COLS_OF, ((), ())),
            preferred_element_type=f32,
        )

    def rows_back():
        target = r.grad_rows if ends_here else r.normed_grad
        target[:, :dim_own] = dot_t(r.proj_grad[...], r.proj_own[...])
        far = r.proj_far.shape[0]
        for at in range(0, far, dim_own):
            target[:, pl.ds(dim_own + at, dim_own)] = dot_t(
                r.proj_grad[...], r.proj_far[pl.ds(at, dim_own)]
            )

    def far_arrived():
        for k in range(1, nb):
            pltpu.make_async_remote_copy(
                src_ref=r.proj_grad,
                dst_ref=r.proj_grad_far.at[k - 1],
                send_sem=batch_sems[0].at[k - 1],
                recv_sem=batch_sems[1].at[k - 1],
                device_id={"batch": lax.rem(b + k, nb)},
                device_id_type=MESH_ID,
            ).wait_recv()

    def proj_far_back(at):
        cols = pl.ds(at, wide)
        acc = r.proj_acc[:, cols]
        for k in range(nb - 1):
            acc = acc + lax.dot_general(
                r.normed_far[k], r.proj_grad_far[k, :, cols], (COLS_OF, ((), ())),
                preferred_element_type=f32,
            )
        rows = r.proj_part.shape[1]
        for i in range(r.proj_part.shape[0]):
            r.proj_part[i, :, cols] = acc[i * rows : (i + 1) * rows].astype(bf16)

    def last_wait():
        for i, by in enumerate(hops):
            pl.when(t >= by)(lambda: scan_copy(i, by).wait_send())
        for copy in batch_copies:
            copy.wait_send()

    c = lax.rem(s, PAIR)
    own_tok = r.tokens.shape[0]
    same = jnp.where(c == b, 1.0, 0.0)

    def small_move(i, src, dst, to):
        return pltpu.make_async_remote_copy(
            src_ref=src,
            dst_ref=dst,
            send_sem=small_sems[0].at[i],
            recv_sem=small_sems[1].at[i],
            device_id=to,
            device_id_type=MESH_ID,
        )

    by_pair, by_batch = {"seq": s + 1 - 2 * c}, {"batch": 1 - b}
    row_moves = small_move(0, r.rows_away, r.rows_come, by_pair)
    small_moves = [
        small_move(1, r.small_other, r.small_come.at[0], by_batch),
        small_move(2, r.small_own, r.small_come.at[1], by_pair),
    ]

    def rank_back():
        grad_low = mid(r.grad_logits[...], r.rank_out_core[...], ROWS_OF).astype(bf16)
        r.grad_rows[...] += dot_t(grad_low, r.rank_in[...])
        start = pl.multiple_of((1 - c) * own_tok, 8)
        r.rows_away[...] = r.grad_rows[pl.ds(start, own_tok)]
        row_moves.start()
        bias = jnp.sum(r.grad_logits[...], axis=0, keepdims=True)
        out_rows = mid(r.low_rank[...], r.grad_logits[...], COLS_OF)
        in_rows = lax.dot_general(
            grad_low, r.normed[...], (COLS_OF, ((), ())), preferred_element_type=f32
        )
        gains = r.grad_headgain[...]
        width = gains.shape[1] // 2
        low, upper = gains[:, :width], gains[:, width:]
        rank = out_rows.shape[0]
        for i, ref in enumerate((r.small_own, r.small_other)):
            mine = same if i == 0 else 1.0 - same
            ref[...] = jnp.zeros_like(ref)
            for j in range(dim_own // DV):
                at = i * dim_own + j * DV
                ref[2 + j : 3 + j] = r.grad_gain_two[:, at : at + DV]
                ref[(2 + j) * rank : (3 + j) * rank] = in_rows[:, at : at + DV]
            ref[4:5] = bias * mine
            ref[5:6, :width] = jnp.where(b == i, low, upper)
            ref[rank : 2 * rank] = out_rows * mine

    def end_back():
        row_moves.wait_recv()
        start = pl.multiple_of(c * own_tok, 8)
        grad_normed = r.grad_rows[pl.ds(start, own_tok)] + r.rows_come[...]
        tokens = r.tokens[...].astype(f32)
        rel = jnp.where(
            b == 0, tokens, jnp.concatenate([tokens[:, dim_own:], tokens[:, :dim_own]], axis=1)
        )
        scale = rms_scale(rel)
        unit = rel * scale
        gain_grad = jnp.sum(grad_normed * unit, axis=0, keepdims=True)
        for i, ref in enumerate((r.small_own, r.small_other)):
            for j in range(dim_own // DV):
                at = i * dim_own + j * DV
                ref[j : j + 1] = gain_grad[:, at : at + DV]
        small_moves[0].start()
        scaled = grad_normed * r.gain_one_rel[...]
        grad = r.grad_resid[...] + scale * (
            scaled - unit * jnp.mean(scaled * unit, axis=-1, keepdims=True)
        )
        grad = jnp.where(
            b == 0, grad, jnp.concatenate([grad[:, dim_own:], grad[:, :dim_own]], axis=1)
        )
        r.grad_input[...] = grad.astype(bf16)

    def batch_small():
        small_moves[0].wait_recv()
        r.small_own[...] += r.small_come[0]
        small_moves[1].start()

    def pair_small():
        small_moves[1].wait_recv()
        rows = r.small_part.shape[1]
        for i in range(r.small_part.shape[0]):
            at = pl.ds(i * rows, rows)
            r.small_part[i] = r.small_own[at] + r.small_come[1, at]

    cuts = range(0, r.proj_grad.shape[1], wide)
    each = lambda body, over: [functools.partial(body, i) for i in over]
    work = [out_grad] + each(head_back, range(heads)) + each(reach_local, range(heads))
    work += [lambda: scan_start(0)] + each(local_back, range(heads))
    work += each(scan_join, range(len(hops) - 1)) + [scan_end] + each(state_back, range(heads))
    work += [send_batch, rows_back]
    if ends_here:
        work += [rank_back, end_back]
    work += each(proj_back, cuts) + [far_arrived] + each(proj_far_back, cuts)
    if ends_here:
        work += [batch_small, pair_small]
    work, plans = iter(work), [iter(stages) for stages in plans]

    def advance(what):
        body = next(what, None)
        if body is not None:
            body()
        return body is not None

    for job in order:
        if job < nj:
            advance(work if job < 0 else plans[job])
    while advance(work):
        pass
    while any([advance(stages) for stages in plans]):
        pass
    for drain in drains:
        drain()
    last_wait()
    if ends_here:
        for move in [row_moves] + small_moves:
            move.wait_send()


def attention_back(inputs, jobs, order, ny, nz, nb, steps):
    f32, bf16 = jnp.float32, jnp.bfloat16
    chips = ny * nz
    arrays = list(inputs)
    tok, keys_w = inputs.queries.shape
    vals_w = inputs.values.shape[1]
    spans = inputs.entered.shape[0]
    dim_own = inputs.proj_own.shape[0]
    proj_w = inputs.proj_own.shape[1]
    shapes = [inputs.gate_part.shape, inputs.down_part.shape, inputs.up_part.shape]
    shapes.append((chips, vals_w // chips, dim_own))
    shapes.append((chips, dim_own // chips, proj_w))
    kinds = [bf16] * 5
    ends_here = len(jobs) > 5
    rank, own_tok = inputs.rank_in.shape[1], inputs.tokens.shape[0]
    small_rows = rank * (2 + dim_own // DV) if ends_here else chips
    if ends_here:
        shapes.append((chips, small_rows // chips, DV))
        kinds.append(f32)
    scratch_one, scratch_two, scratch_mid = [], [], []
    for (_, rows, cols), (y_first, _), kind in zip(shapes, jobs, kinds):
        n_one, n_two = (ny, nz) if y_first else (nz, ny)
        scratch_one.append(pltpu.VMEM((2, max(n_one - 1, 1), n_two, rows, cols), kind))
        scratch_two.append(pltpu.VMEM((2, max(n_two - 1, 1), 1, rows, cols), kind))
        scratch_mid.append(pltpu.VMEM((n_two, rows, cols), kind))
    tmp = [
        pltpu.VMEM(shapes[3], bf16),
        pltpu.VMEM(shapes[4], bf16),
        pltpu.VMEM((tok, vals_w), f32),
        pltpu.VMEM((spans + 1, keys_w, DV), f32),
        pltpu.VMEM((tok, keys_w), f32),
        pltpu.VMEM((tok, keys_w), f32),
        pltpu.VMEM((tok, vals_w), f32),
        pltpu.VMEM((tok, proj_w), bf16),
        pltpu.VMEM((max(nb - 1, 1), tok, proj_w), bf16),
        pltpu.VMEM((dim_own, proj_w), f32),
        pltpu.VMEM((tok, dim_own * nb), f32),
        pltpu.VMEM((own_tok, dim_own * nb), f32),
        pltpu.VMEM((own_tok, dim_own * nb), f32),
        pltpu.VMEM((small_rows, DV), f32),
        pltpu.VMEM((small_rows, DV), f32),
        pltpu.VMEM((2, small_rows, DV), f32),
        pltpu.VMEM((chips, small_rows // chips, DV), f32),
    ]
    hops = len(steps) + 1
    tmp += [pltpu.VMEM((hops, keys_w, DV), bf16)] * 2
    dma = pltpu.SemaphoreType.DMA
    sems = [dma((len(jobs), 5, 2, max(ny, nz, 2) - 1))] * 2
    sems += [dma((hops,))] * 2 + [dma((max(nb - 1, 1),))] * 2 + [dma((3,))] * 2
    vmem = pl.BlockSpec(memory_space=pltpu.VMEM)
    out_shape = [jax.ShapeDtypeStruct(shape, kind) for shape, kind in zip(shapes, kinds)]
    out_shape += out_shape[:5]
    out_shape += [
        jax.ShapeDtypeStruct((8, 128) if ends_here else (tok, dim_own * nb), f32),
        jax.ShapeDtypeStruct((tok, keys_w), f32),
        jax.ShapeDtypeStruct((1, DV), f32),
        jax.ShapeDtypeStruct((own_tok, dim_own * nb), bf16),
    ]
    outs = pl.pallas_call(
        functools.partial(back_kernel, ny, nz, nb, tuple(steps), tuple(jobs), tuple(order)),
        out_shape=out_shape,
        in_specs=[vmem] * len(arrays),
        out_specs=[vmem] * len(out_shape),
        scratch_shapes=scratch_one + scratch_two + scratch_mid + tmp + sems,
        compiler_params=pltpu.CompilerParams(
            collective_id=1, has_side_effects=True, vmem_limit_bytes=60 * 2**20
        ),
        name="attention_back",
    )(*arrays)
    nj = len(jobs)
    return outs[:nj], outs[nj : nj + 5], outs[nj + 5 :]


class FrontIn(NamedTuple):
    tokens: Any = None
    seg: Any = None
    gain_one: Any = None
    gain_two: Any = None
    bias: Any = None
    head_gain: Any = None
    rank_in: Any = None
    rank_out: Any = None


class FrontOut(NamedTuple):
    normed: Any = None
    normed_far: Any = None
    low_rank: Any = None
    logits: Any = None
    cumul: Any = None
    queries: Any = None
    keys: Any = None
    values: Any = None
    outgate: Any = None
    mask: Any = None
    within: Any = None
    end_doc: Any = None
    keep: Any = None
    factors: Any = None
    to_next: Any = None
    entered: Any = None
    attn: Any = None
    gated: Any = None
    gated_far: Any = None
    resid: Any = None
    normed_two: Any = None
    gain_one_rel: Any = None
    gain_two_rel: Any = None
    head_gain_all: Any = None
    rank_in_far: Any = None
    rank_out_core: Any = None


def front_kernel(pieces, down_at, steps, *refs):
    f32, bf16 = jnp.float32, jnp.bfloat16
    refs = list(refs)

    def take(n):
        out = refs[:n]
        del refs[:n]
        return out

    ins = take(8)
    r = SimpleNamespace(**dict(zip(FrontIn._fields, take(len(FrontIn._fields)))))
    outs = take(7)
    vars(r).update(zip(FrontOut._fields, take(len(FrontOut._fields))))
    tokens_far, seg_slots, factor_rows, gain_one_far, gain_two_far, bias_far, head_far, rank_out_far = take(8)
    proj, local_out, state, going, coming, out_away, out_come, local_sems = take(8)
    send_x, recv_x, send_p, recv_p, send_s, recv_s, send_c, recv_c = take(8)
    b, s = lax.axis_index("batch"), lax.axis_index("seq")
    ns = lax.axis_size("seq")
    chips = ns // PAIR
    c = lax.rem(s, PAIR)
    t = s // PAIR
    k = lax.rem(s // 2, 4)
    k_y = k + 1 - 2 * lax.rem(k, 2)
    k_z = k + 2 - 4 * (k // 2)
    k_far = 3 - k
    by_x = {"batch": 1 - b}
    by_y = {"seq": s + 2 * (k_y - k)}
    by_z = {"seq": s + 2 * (k_z - k)}
    by_c = {"seq": s + 1 - 2 * c}

    seg_slots[...] = jnp.zeros_like(seg_slots)
    factor_rows[...] = jnp.zeros_like(factor_rows)
    barrier = pltpu.get_barrier_semaphore()

    def signal(to):
        pl.semaphore_signal(barrier, inc=1, device_id=to, device_id_type=MESH_ID)

    signal(by_x)
    peers = 1
    for d in sorted({1, 2, 4} | {PAIR * d for d in steps}):
        pl.when(s >= d)(lambda: signal({"seq": s - d}))
        pl.when(s < ns - d)(lambda: signal({"seq": s + d}))
        peers = peers + (s + ns - d) // ns + (2 * ns - 1 - d - s) // ns
    pl.semaphore_wait(barrier, peers)

    def remote(src, dst, send, recv, to):
        return pltpu.make_async_remote_copy(
            src_ref=src, dst_ref=dst, send_sem=send, recv_sem=recv, device_id=to, device_id_type=MESH_ID
        )

    def source(arg, row_step, col_step, width, start, count):
        rows = pl.ds(pl.multiple_of(c * row_step + start, 16), count)
        if col_step:
            return ins[arg].at[rows, pl.ds(pl.multiple_of(c * col_step, 128), width)]
        return ins[arg].at[rows]

    far_refs = [outs[1], outs[3], outs[5], outs[6]]
    groups = len(pieces)
    x_copies = []
    for g, group in enumerate(pieces):
        far = far_refs[g]
        quarter = far.shape[0] // 4
        mine = []
        for i, (arg, row_step, col_step, width, place) in enumerate(group):
            src = source(arg, row_step, col_step, width, k * quarter, quarter)
            rows = pl.ds(pl.multiple_of(k * quarter, 16), quarter)
            dst = far.at[rows, pl.ds(place, width)]
            mine.append(remote(src, dst, send_x.at[g, i], recv_x.at[g, i], by_x))
        x_copies.append(mine)

    is_sender, is_taker = c == b, c != b

    def guarded(g, taker, body):
        if g == down_at:
            pl.when(is_taker if taker else is_sender)(body)
        else:
            body()

    def start_x(g):
        def body():
            for copy in x_copies[g]:
                copy.start()

        guarded(g, False, body)

    local_copies = []
    for g, group in enumerate(pieces):
        mine = []
        if g != down_at:
            own = outs[2 * g]
            for i, (arg, row_step, col_step, width, place) in enumerate(group):
                src = source(arg, row_step, col_step, width, 0, own.shape[0])
                mine.append(
                    pltpu.make_async_copy(src, own.at[:, pl.ds(place, width)], local_sems.at[g, i])
                )
        local_copies.append(mine)
    down_copy = pltpu.make_async_copy(ins[7], outs[6], local_sems.at[down_at, 0])

    def rows_of(g, q, part):
        far = far_refs[g]
        quarter = far.shape[0] // 4
        if part is None:
            return far.at[pl.ds(pl.multiple_of(q * quarter, 16), quarter)]
        eighth = quarter // 2
        return far.at[pl.ds(pl.multiple_of(q * quarter + part * eighth, 16), eighth)]

    def plane_copy(g, kind, coming_in):
        to, q, part = (
            (by_y, k_y if coming_in else k, None),
            (by_z, k_z if coming_in else k, None),
            (by_y, k_far if coming_in else k_z, 0),
            (by_z, k_far if coming_in else k_y, 1),
        )[kind]
        ref = rows_of(g, q, part)
        return remote(ref, ref, send_p.at[g, kind], recv_p.at[g, kind], to)

    def second(g):
        def body():
            for copy in x_copies[g]:
                copy.wait_recv()
            plane_copy(g, 0, False).start()
            plane_copy(g, 1, False).start()

        guarded(g, True, body)

    def third(g):
        def body():
            plane_copy(g, 1, True).wait_recv()
            plane_copy(g, 2, False).start()
            plane_copy(g, 0, True).wait_recv()
            plane_copy(g, 3, False).start()

        guarded(g, True, body)

    def final(g):
        def body():
            plane_copy(g, 2, True).wait_recv()
            plane_copy(g, 3, True).wait_recv()

        guarded(g, True, body)

    small = [
        remote(src, dst, send_s.at[i], recv_s.at[i], by_x)
        for i, (src, dst) in enumerate(
            (
                (r.gain_one, gain_one_far),
                (r.gain_two, gain_two_far),
                (r.bias, bias_far),
                (r.head_gain, head_far),
                (r.rank_in, r.rank_in_far),
                (r.rank_out, rank_out_far),
            )
        )
    ]
    at = len(small)
    token_copy = remote(r.tokens, tokens_far, send_s.at[at], recv_s.at[at], by_c)
    out_copy = remote(out_away, out_come, send_s.at[at + 1], recv_s.at[at + 1], by_c)
    dim_own = outs[0].shape[0]
    normed_copy = remote(
        r.normed.at[:, pl.ds(dim_own, dim_own)], r.normed_far.at[0],
        send_s.at[at + 2], recv_s.at[at + 2], by_x,
    )
    gated_copy = remote(
        r.gated, r.gated_far.at[0], send_s.at[at + 3], recv_s.at[at + 3], by_x
    )
    seg_moves = []
    for i, d in enumerate((2, 1, -1, -2)):
        there = s < ns - d if d > 0 else s >= -d
        here = s >= d if d > 0 else s < ns + d
        move = remote(
            r.seg, seg_slots.at[i], send_c.at[0, i], recv_c.at[0, i], {"seq": s + d}
        )
        seg_moves.append((there, here, move))
    factor_moves = []
    for i, d in enumerate((1, -1)):
        there = t < chips - d if d > 0 else t >= -d
        here = t >= d if d > 0 else t < chips + d
        move = remote(
            factor_rows.at[2 + i], factor_rows.at[i], send_c.at[1, i], recv_c.at[1, i],
            {"seq": s + PAIR * d},
        )
        factor_moves.append((there, here, move))
    hops = list(steps) + [1]

    def scan_move(i):
        return remote(
            going.at[i], coming.at[i], send_c.at[2, i], recv_c.at[2, i], {"seq": s + PAIR * hops[i]}
        )

    start_x(0)
    token_copy.start()
    for there, _, move in seg_moves:
        pl.when(there)(move.start)
    for copy in small:
        copy.start()
    start_x(1)
    for mine in local_copies:
        for copy in mine:
            copy.start()
    pl.when(is_sender)(down_copy.start)

    tok = r.normed.shape[0]
    spans = tok // SPAN
    keys_w, vals_w = r.queries.shape[1], r.values.shape[1]
    heads = keys_w // DK

    def iotas(n):
        return (
            lax.broadcasted_iota(jnp.int32, (n, n), 0),
            lax.broadcasted_iota(jnp.int32, (n, n), 1),
        )

    def to_col(row):
        i, j = iotas(row.shape[1])
        return jnp.sum(jnp.where(i == j, row, 0.0), axis=1, keepdims=True)

    def by_core(mine, other, axis):
        return jnp.where(
            c == 0, jnp.concatenate([mine, other], axis), jnp.concatenate([other, mine], axis)
        )

    for _, here, move in seg_moves:
        pl.when(here)(move.wait_recv)
    seg_own = r.seg[...]
    seg_row = by_core(seg_own, jnp.where(c == 0, seg_slots[2], seg_slots[1]), 1)
    prev_last = jnp.where(c == 0, seg_slots[1], seg_slots[0])[:, -1:]
    next_first = jnp.where(c == 0, seg_slots[3], seg_slots[2])[:, :1]
    first_id, last_id = seg_row[:, :1], seg_row[:, -1:]
    has_prev = jnp.where(t > 0, 1.0, 0.0)
    has_next = jnp.where(t < chips - 1, 1.0, 0.0)
    from_prev = has_prev * (prev_last == first_id).astype(f32)
    to_next = has_next * (next_first == last_id).astype(f32)
    whole_doc = (first_id == last_id).astype(f32)
    r.to_next[...] = to_next
    seg_col = to_col(seg_row)
    i_pos, j_pos = iotas(tok)

    def span_of(pos):
        return sum((pos >= n * SPAN).astype(jnp.int32) for n in range(1, spans))

    mask = jnp.where(
        jnp.logical_and(
            jnp.logical_and(span_of(i_pos) == span_of(j_pos), j_pos <= i_pos), seg_col == seg_row
        ),
        1.0,
        0.0,
    )
    r.mask[...] = mask
    before = seg_col[:1]
    for n in range(spans):
        rows = pl.ds(n * SPAN, SPAN)
        mine = seg_col[n * SPAN : (n + 1) * SPAN]
        first, last = mine[:1], mine[-1:]
        r.within[rows] = (mine == first).astype(f32) * (first == before).astype(f32)
        r.end_doc[rows] = (mine == last).astype(f32)
        before = last

    second(0)
    start_x(2)

    for copy in small:
        copy.wait_recv()
    gain_one = jnp.concatenate([r.gain_one[...], gain_one_far[...]], axis=1)
    r.gain_one_rel[...] = gain_one
    gain_two = jnp.concatenate([r.gain_two[...], gain_two_far[...]], axis=1)
    r.gain_two_rel[...] = gain_two
    head_gain = jnp.where(
        b == 0,
        jnp.concatenate([r.head_gain[...], head_far[...]], axis=1),
        jnp.concatenate([head_far[...], r.head_gain[...]], axis=1),
    )
    r.head_gain_all[...] = head_gain
    same = jnp.where(is_sender, 1.0, 0.0)
    bias = same * r.bias[...] + (1.0 - same) * bias_far[...]
    rank_out = same * r.rank_out[...].astype(f32) + (1.0 - same) * rank_out_far[...].astype(f32)
    r.rank_out_core[...] = rank_out
    token_copy.wait_recv()
    both = by_core(r.tokens[...].astype(f32), tokens_far[...].astype(f32), 0)
    half = both.shape[1] // 2
    activation = jnp.where(
        b == 0, both, jnp.concatenate([both[:, half:], both[:, :half]], axis=1)
    )
    r.normed[...] = (activation * rms_scale(activation) * gain_one).astype(bf16)
    normed_copy.start()
    low_rank = dot32(r.normed[:, :half], r.rank_in[...]) + dot32(
        r.normed[:, half:], r.rank_in_far[...]
    )
    r.low_rank[...] = low_rank
    logits = high(low_rank, rank_out) + bias
    r.logits[...] = logits
    decays = (jnp.minimum(logits, 0.0) - jnp.log1p(jnp.exp(-jnp.abs(logits)))) / 16.0
    i_span, j_span = iotas(SPAN)
    lower = (j_span <= i_span).astype(f32)
    total = jnp.zeros((1, keys_w), f32)
    for n in range(spans):
        rows = pl.ds(n * SPAN, SPAN)
        part = high(lower, decays[n * SPAN : (n + 1) * SPAN])
        r.cumul[rows] = part
        last = part[SPAN - 1 :]
        total = total + last
        r.keep[n] = to_col(jnp.exp(last)) * r.within[pl.ds((n + 1) * SPAN - 1, 1)]
    block_keep = jnp.exp(total) * whole_doc
    factor_rows[2] = block_keep * from_prev
    factor_rows[3] = block_keep * to_next
    for there, _, move in factor_moves:
        pl.when(there)(move.start)

    second(1)
    start_x(3)
    for copy in local_copies[0]:
        copy.wait()
    wide = 512

    def columns(body):
        for at in range(0, proj.shape[1], wide):
            body(pl.ds(at, wide))

    def own_proj(cols):
        proj[:, cols] = dot32(r.normed[:, :half], outs[0][:, cols])

    def far_proj(cols):
        proj[:, cols] += dot32(r.normed[:, half:], outs[1][:, cols])

    columns(own_proj)
    third(0)
    third(1)
    final(0)
    columns(far_proj)
    r.queries[...] = proj[:, :keys_w] * DK ** (-0.5)
    r.keys[...] = proj[:, pl.ds(keys_w, keys_w)]
    r.values[...] = proj[:, pl.ds(2 * keys_w, vals_w)]
    r.outgate[...] = proj[:, pl.ds(2 * keys_w + vals_w, vals_w)]

    for h in range(heads):
        kc, vc = pl.ds(h * DK, DK), pl.ds(h * DV, DV)
        local = None
        for n in range(spans):
            rows = pl.ds(n * SPAN, SPAN)
            cum = r.cumul[rows, kc]
            key_end = r.keys[rows, kc] * jnp.exp(cum[SPAN - 1 :] - cum) * r.end_doc[rows]
            added = low(key_end, r.values[rows, vc], COLS_OF)
            r.entered[n, kc] = added
            local = added if local is None else r.keep[n, kc] * local + added
        state[kc] = local
    going[0] = state[...].astype(bf16)
    pl.when(t < chips - hops[0])(scan_move(0).start)
    second(2)

    for _, here, move in factor_moves:
        pl.when(here)(move.wait_recv)
    front, back = to_col(factor_rows[2]), to_col(factor_rows[3])
    r.factors[0] = back
    front_factors = [front]
    if len(steps) > 1:
        r.factors[1] = back * to_col(factor_rows[1])
        front_factors.append(front * to_col(factor_rows[0]))

    for h in range(heads):
        kc, vc = pl.ds(h * DK, DK), pl.ds(h * DV, DV)
        cum = r.cumul[:, kc]
        scores = jnp.where(
            r.mask[...] > 0.0,
            low(r.queries[:, kc] * jnp.exp(cum), r.keys[:, kc] * jnp.exp(-cum), ROWS_OF),
            0.0,
        )
        local_out[:, vc] = low(scores, r.values[:, vc])

    for i in range(len(steps)):

        @pl.when(t >= hops[i])
        def _():
            scan_move(i).wait_recv()
            state[...] += front_factors[i] * coming[i].astype(f32)

        going[i + 1] = state[...].astype(bf16)
        pl.when(t < chips - hops[i + 1])(scan_move(i + 1).start)
    third(2)
    second(3)
    i = len(steps)

    @pl.when(t >= 1)
    def _():
        scan_move(i).wait_recv()
        state[...] = from_prev * coming[i].astype(f32)

    @pl.when(t < 1)
    def _():
        state[...] = jnp.zeros_like(state)

    for h in range(heads):
        kc, vc = pl.ds(h * DK, DK), pl.ds(h * DV, DV)
        inside = state[kc]
        for n in range(spans):
            rows = pl.ds(n * SPAN, SPAN)
            added = r.entered[n, kc]
            r.entered[n, kc] = inside
            query_in = r.queries[rows, kc] * jnp.exp(r.cumul[rows, kc]) * r.within[rows]
            r.attn[rows, vc] = local_out[rows, vc] + low(query_in, inside)
            inside = r.keep[n, kc] * inside + added
        raw = r.attn[:, vc]
        gate = r.outgate[:, vc]
        r.gated[:, vc] = (
            raw * head_rms(raw) * head_gain * (gate * jax.nn.sigmoid(gate))
        ).astype(bf16)
    gated_copy.start()
    third(3)

    final(1)
    for copy in local_copies[1]:
        copy.wait()
    rows = tok // PAIR
    mine, away = pl.ds(pl.multiple_of(c * rows, 16), rows), pl.ds(pl.multiple_of((1 - c) * rows, 16), rows)
    for j, ref in ((0, outs[2]), (1, outs[3])):
        cols = pl.ds(j * half, half)
        out_away[:, cols] = dot32(r.gated[away], ref[...])
        r.resid[:, cols] = dot32(r.gated[mine], ref[...])
    out_copy.start()
    tokens = r.tokens[...].astype(f32)
    own_act = jnp.where(
        b == 0, tokens, jnp.concatenate([tokens[:, half:], tokens[:, :half]], axis=1)
    )
    out_copy.wait_recv()
    resid = own_act + r.resid[...] + out_come[...]
    r.resid[...] = resid
    r.normed_two[...] = (resid * rms_scale(resid) * gain_two).astype(bf16)

    final(2)
    final(3)
    for g in range(groups):

        def plane_sent(g=g):
            for kind in range(4):
                plane_copy(g, kind, False).wait_send()

        def x_sent(g=g):
            for copy in x_copies[g]:
                copy.wait_send()

        guarded(g, True, plane_sent)
        guarded(g, False, x_sent)
        if g > 1:
            for copy in local_copies[g]:
                copy.wait()
    pl.when(is_sender)(down_copy.wait)
    for copy in small + [token_copy, out_copy, normed_copy, gated_copy]:
        copy.wait_send()
    normed_copy.wait_recv()
    gated_copy.wait_recv()
    for there, _, move in seg_moves + factor_moves:
        pl.when(there)(move.wait_send)
    for i in range(len(hops)):
        pl.when(t < chips - hops[i])(scan_move(i).wait_send)


def attention_front(weights, tokens, seg_row, small, steps):
    f32, bf16 = jnp.float32, jnp.bfloat16
    w_query, w_key, w_value, w_outgate, w_output, w_gate, w_up, w_down = weights
    half = lambda a: a.shape[1] // PAIR
    proj, place = [], 0
    for arg, a in enumerate((w_query, w_key, w_value, w_outgate)):
        proj.append((arg, 0, half(a), half(a), place))
        place += half(a)
    dim_own, proj_w = w_query.shape[0], place
    out_rows = w_output.shape[0] // PAIR
    out_piece = [(4, out_rows, 0, w_output.shape[1], 0)]
    gu = [(5, 0, half(w_gate), half(w_gate), 0), (6, 0, half(w_up), half(w_up), half(w_gate))]
    gu_shape = (w_gate.shape[0], 2 * half(w_gate))
    down = [(7, 0, 0, w_down.shape[1], 0)]
    w_shapes = [(dim_own, proj_w)] * 2 + [(out_rows, w_output.shape[1])] * 2 + [gu_shape] * 2
    w_shapes.append(w_down.shape)
    own_tok, dim = tokens.shape
    tok = PAIR * own_tok
    spans, keys_w, vals_w = tok // SPAN, half(w_query), half(w_value)
    rank = small[4].shape[1]
    shape_of = dict(
        normed=((tok, dim), bf16), normed_far=((1, tok, dim_own), bf16),
        low_rank=((tok, rank), f32), logits=((tok, keys_w), f32), cumul=((tok, keys_w), f32),
        queries=((tok, keys_w), f32), keys=((tok, keys_w), f32), values=((tok, vals_w), f32),
        outgate=((tok, vals_w), f32), mask=((tok, tok), f32), within=((tok, 1), f32),
        end_doc=((tok, 1), f32), keep=((spans, keys_w, 1), f32),
        factors=((len(steps), keys_w, 1), f32), to_next=((1, 1), f32),
        entered=((spans, keys_w, DV), f32), attn=((tok, vals_w), f32), gated=((tok, vals_w), bf16),
        gated_far=((1, tok, vals_w), bf16), resid=((own_tok, dim), f32),
        normed_two=((own_tok, dim), bf16), gain_one_rel=((1, dim), f32),
        gain_two_rel=((1, dim), f32), head_gain_all=((1, DV), f32),
        rank_in_far=(small[4].shape, bf16), rank_out_core=((rank, keys_w), f32),
    )
    hops = len(steps) + 1
    vm, dma = pltpu.VMEM, pltpu.SemaphoreType.DMA
    scratch = [
        vm(tokens.shape, bf16), vm((4,) + seg_row.shape, f32), vm((4, 1, keys_w), f32),
        vm(small[0].shape, f32), vm(small[1].shape, f32), vm(small[2].shape, f32),
        vm(small[3].shape, f32), vm(small[5].shape, bf16),
        vm((tok, proj_w), f32), vm((tok, vals_w), f32), vm((keys_w, DV), f32),
        vm((hops, keys_w, DV), bf16), vm((hops, keys_w, DV), bf16),
        vm((own_tok, dim), f32), vm((own_tok, dim), f32),
        dma((4, 4)), dma((4, 4)), dma((4, 4)), dma((4, 4)), dma((4, 4)),
        dma((10,)), dma((10,)), dma((3, 4)), dma((3, 4)),
    ]
    any_spec, vmem = pl.BlockSpec(memory_space=pl.ANY), pl.BlockSpec(memory_space=pltpu.VMEM)
    out_shape = [jax.ShapeDtypeStruct(shape, bf16) for shape in w_shapes]
    out_shape += [jax.ShapeDtypeStruct(*shape_of[name]) for name in FrontOut._fields]
    got = pl.pallas_call(
        functools.partial(front_kernel, (proj, out_piece, gu, down), 3, tuple(steps)),
        out_shape=out_shape,
        in_specs=[any_spec] * 8 + [vmem] * len(FrontIn._fields),
        out_specs=[vmem] * len(out_shape),
        scratch_shapes=scratch,
        compiler_params=pltpu.CompilerParams(
            collective_id=0, has_side_effects=True, vmem_limit_bytes=48 * 2**20
        ),
        name="attention_front",
    )(*weights, tokens, seg_row, *small)
    return got[:7], FrontOut(*got[7:])


def core_cols(array_in, c):
    width = array_in.shape[1] // PAIR
    return lax.dynamic_slice_in_dim(array_in, c * width, width, 1)


def dot32(a, b):
    return jnp.dot(a, b, preferred_element_type=jnp.float32)


def dot_t(a, b):
    return lax.dot_general(a, b, (((1,), (1,)), ((), ())), preferred_element_type=jnp.float32)


def grad_dot(pairs_in):
    total = None
    for left, right in pairs_in:
        part = lax.dot_general(
            left, right, (((0,), (0,)), ((), ())), preferred_element_type=jnp.float32
        )
        total = part if total is None else total + part
    return total


def plain_front(at_place, weights, inputs, seg_ids, small, steps):
    f32, bf16 = jnp.float32, jnp.bfloat16
    nb, b, c, t = at_place.nb, at_place.b, at_place.c, at_place.t
    w_query, w_key, w_value, w_outgate, w_output, w_gate, w_up, w_down = weights
    w_rank_in, w_rank_out = small[4], small[5]
    rank = w_rank_in.shape[1]
    heads = HEADS // PAIR
    keys_w, vals_w = KEYS // PAIR, VALS // PAIR
    dim_own = inputs.shape[2] // nb

    in_pair = at_place.pair_all(inputs[0])
    seg_row = at_place.pair_all(seg_ids[0])
    tok_count = seg_row.shape[0]
    half_tok = tok_count // PAIR
    spans = tok_count // SPAN
    edges = jnp.stack([seg_row[0], seg_row[-1]])
    edges_wide = jnp.broadcast_to(edges[:, None], (2, 128)).astype(f32)
    prev_last = at_place.chip_shift(edges_wide, 1)[1, 0]
    next_first = at_place.chip_shift(edges_wide, -1)[0, 0]
    first_id, last_id = edges[0].astype(f32), edges[1].astype(f32)
    from_prev = jnp.logical_and(t > 0, prev_last == first_id).astype(f32)
    to_next = jnp.logical_and(t < at_place.chips - 1, next_first == last_id).astype(f32)
    whole_doc = (first_id == last_id).astype(f32)

    packed = jnp.concatenate([a.reshape(-1) for a in small])
    packed = jnp.stack([packed] + at_place.others(packed))
    parts, at = [], 0
    for a in small:
        parts.append(packed[:, at : at + a.size])
        at += a.size
    gain_one = parts[0].reshape(-1).astype(f32)
    gain_two = parts[1].reshape(-1).astype(f32)
    bias_all = at_place.to_abs(parts[2], 0).reshape(-1).astype(f32)
    bias_w = lax.dynamic_slice_in_dim(bias_all, c * keys_w, keys_w)
    head_gain32 = at_place.to_abs(parts[3], 0).reshape(-1).astype(f32)
    rank_in_w = parts[4].reshape(-1, rank)
    rank_out_all = (
        at_place.to_abs(parts[5], 0).reshape((nb,) + w_rank_out.shape).transpose(1, 0, 2)
        .reshape(rank, -1)
    )
    rank_out_w = core_cols(rank_out_all, c).astype(f32)

    proj_own = jnp.concatenate(
        [core_cols(a, c) for a in (w_query, w_key, w_value, w_outgate)], axis=1
    )
    out_own = lax.dynamic_slice_in_dim(w_output, c * vals_w, vals_w, 0)
    gu_own = jnp.concatenate([core_cols(w_gate, c), core_cols(w_up, c)], axis=1)
    proj_far, out_far, gu_far, down_far = (
        jnp.concatenate(at_place.others(a), axis=0) for a in (proj_own, out_own, gu_own, w_down)
    )
    down_all = at_place.to_abs(jnp.concatenate([w_down, down_far], axis=0), 0)
    ff_half = down_all.shape[0] // PAIR
    down_w = lax.dynamic_slice_in_dim(down_all, c * ff_half, ff_half, 0)
    activation = at_place.to_rel(in_pair, 1).astype(f32)
    scale_one = rms_scale(activation)
    unit_one = activation * scale_one
    normed = (unit_one * gain_one).astype(bf16)
    normed_far = [
        at_place.from_batch(normed[:, (nb - k) * dim_own : (nb - k + 1) * dim_own], k)
        for k in range(1, nb)
    ]

    low_rank = dot32(normed, rank_in_w)
    logits = jnp.dot(low_rank, rank_out_w, precision=top_prec) + bias_w
    decays = jax.nn.log_sigmoid(logits) / 16.0

    seg_s = seg_row.reshape(spans, SPAN)
    first_s, last_s = seg_s[:, 0], seg_s[:, -1]
    row_pos = lax.broadcasted_iota(jnp.int32, (SPAN, SPAN), 0)
    col_pos = lax.broadcasted_iota(jnp.int32, (SPAN, SPAN), 1)
    lower = (col_pos <= row_pos).astype(f32)
    allowed = lower[None] * (seg_s[:, :, None] == seg_s[:, None, :]).astype(f32)
    allowed = allowed[:, None]
    prior = jnp.concatenate([seg_row[:1], last_s[:-1]])
    enters = (first_s == prior).astype(f32)
    within = ((seg_s == first_s[:, None]).astype(f32) * enters[:, None])[:, None, :, None]
    end_doc = (seg_s == last_s[:, None]).astype(f32)[:, None, :, None]

    cumul = mm("ts,nsc->ntc", lower, decays.reshape(spans, SPAN, keys_w))
    total_log = jnp.sum(cumul[:, -1], axis=0)

    proj = dot32(normed[:, :dim_own], proj_own) + dot32(normed[:, dim_own:], proj_far)
    queries = to_spans(proj[:, :keys_w] * DK ** (-0.5), DK)
    keys_s = to_spans(proj[:, keys_w : 2 * keys_w], DK)
    values_s = to_spans(proj[:, 2 * keys_w : 2 * keys_w + vals_w], DV)
    outgate = proj[:, 2 * keys_w + vals_w :]

    cumul = cumul.reshape(spans, SPAN, heads, DK).transpose(0, 2, 1, 3)
    last_cumul = cumul[:, :, -1:, :]
    grow = jnp.exp(cumul)
    shrink = jnp.exp(-cumul)
    to_end = jnp.exp(last_cumul - cumul) * end_doc
    query_dec = queries * grow
    key_dec = keys_s * shrink
    key_end = keys_s * to_end
    query_in = query_dec * within
    keep = jnp.exp(last_cumul[:, :, 0, :]) * within[:, :, -1]
    scores = mm("nhtc,nhsc->nhts", query_dec, key_dec) * allowed
    local_out = mm("nhts,nhsv->nhtv", scores, values_s)
    added = mm("nhsc,nhsv->nhcv", key_end, values_s)

    local_state = added[0]
    for i in range(1, spans):
        local_state = keep[i][:, :, None] * local_state + added[i]

    reach_chips = -(-(SEG_MOST - 1) // tok_count)

    def chip_scan(state, factor, way):
        state = state.reshape(heads * DK, DV)
        step = 1
        pad = jnp.zeros((15, heads * DK), f32)
        while step < min(reach_chips, at_place.chips):
            packed = jnp.concatenate(
                [state, jnp.concatenate([factor[None], pad]).reshape(-1, DV)]
            )
            got = at_place.chip_shift(packed.astype(bf16), way * step).astype(f32)
            state = state + factor[:, None] * got[: heads * DK]
            factor = factor * got[heads * DK :].reshape(16, -1)[0]
            step *= 2
        got = at_place.chip_shift(state.astype(bf16), way)
        return got.astype(f32).reshape(heads, DK, DV)

    block_keep = jnp.exp(total_log) * whole_doc
    carried = from_prev * chip_scan(local_state, block_keep * from_prev, 1)
    enter_list = [carried]
    for i in range(spans - 1):
        enter_list.append(keep[i][:, :, None] * enter_list[i] + added[i])
    entered = jnp.stack(enter_list)

    attn_raw = from_spans(local_out + mm("nhtc,nhcv->nhtv", query_in, entered)).reshape(
        tok_count, heads, DV
    )
    head_scale = head_rms(attn_raw)
    head_norm = attn_raw * head_scale
    gate_h = outgate.reshape(tok_count, heads, DV)
    gate_sig = jax.nn.sigmoid(gate_h)
    gate_act = gate_h * gate_sig
    gated = (head_norm * head_gain32 * gate_act).reshape(tok_count, vals_w).astype(bf16)
    gated_far = at_place.others(gated)
    out_w = jnp.concatenate(
        [out_own] + [out_far[k * vals_w : (k + 1) * vals_w] for k in range(nb - 1)], axis=1
    )
    own_rows = lambda a: lax.dynamic_slice_in_dim(a, c * half_tok, half_tok, 0)
    resid = own_rows(activation) + at_place.pair_sum(dot32(gated, out_w))
    normed_two = (resid * rms_scale(resid) * gain_two).astype(bf16)
    col = lambda a: a.reshape(-1, 1)
    factor = block_keep * to_next
    factors = []
    for step in steps or [1]:
        factors.append(col(factor))
        if step != steps[-1]:
            factor = factor * at_place.chip_shift(factor, -step)
    in_span = jnp.arange(tok_count) // SPAN
    mask = jnp.logical_and(
        jnp.logical_and(in_span[:, None] == in_span, seg_row[:, None] == seg_row),
        jnp.tril(jnp.ones((tok_count, tok_count), bool)),
    )
    front = FrontOut(
        normed=normed, normed_far=jnp.stack(normed_far), low_rank=low_rank, logits=logits,
        cumul=from_spans(cumul), queries=from_spans(queries), keys=from_spans(keys_s),
        values=from_spans(values_s), outgate=outgate, mask=mask.astype(f32), within=col(within),
        end_doc=col(end_doc), keep=keep.reshape(spans, keys_w, 1), factors=jnp.stack(factors),
        to_next=to_next.reshape(1, 1), entered=entered.reshape(spans, keys_w, DV),
        attn=attn_raw.reshape(tok_count, vals_w), gated=gated, gated_far=jnp.stack(gated_far),
        resid=resid, normed_two=normed_two, gain_one_rel=gain_one[None],
        gain_two_rel=gain_two[None], head_gain_all=head_gain32[None],
        rank_in_far=rank_in_w[dim_own:], rank_out_core=rank_out_w,
    )
    return (proj_own, proj_far, out_own, out_far, gu_own, gu_far, down_w), front


def plain_end(
    at_place, front, small, inputs, rank_in_w, normed_grad, grad_logits, grad_headgain, grad_resid,
    grad_gain_two,
):
    f32, bf16 = jnp.float32, jnp.bfloat16
    nb, low_rank, normed = at_place.nb, front.low_rank, front.normed
    gain_one, rank_out_w, rank = front.gain_one_rel[0], front.rank_out_core, small[4].shape[1]
    grad_bias = jnp.sum(grad_logits, axis=0)
    grad_rank_out = jnp.dot(low_rank.T, grad_logits, precision=top_prec)
    grad_low = jnp.dot(grad_logits, rank_out_w.T, precision=top_prec).astype(bf16)
    normed_grad = normed_grad + dot_t(grad_low, rank_in_w)
    grad_normed = at_place.pair_sum(normed_grad)
    own_in = at_place.to_rel(inputs[0], 1).astype(f32)
    scale_one = rms_scale(own_in)
    unit_own = own_in * scale_one
    grad_gain_one = jnp.sum(grad_normed * unit_own, axis=0)
    scaled_one = grad_normed * gain_one
    grad_input = (
        grad_resid
        + scale_one
        * (scaled_one - unit_own * jnp.mean(scaled_one * unit_own, axis=-1, keepdims=True))
    ).astype(bf16)
    grad_rank_in = grad_dot([(normed, grad_low)])

    def own_slot(part):
        return at_place.by_core(part, jnp.zeros_like(part), part.ndim - 1)

    by_owner = jnp.concatenate(
        [
            grad_gain_one.reshape(nb, -1),
            grad_gain_two.reshape(nb, -1),
            at_place.to_rel(own_slot(grad_bias).reshape(nb, -1), 0),
            at_place.to_rel(grad_headgain.reshape(nb, -1), 0),
            grad_rank_in.reshape(nb, -1),
            at_place.to_rel(
                own_slot(grad_rank_out).reshape(rank, nb, -1).transpose(1, 0, 2).reshape(nb, -1), 0
            ),
        ],
        axis=1,
    )
    owned = at_place.total_sum(by_owner)
    outs, at = [], 0
    for a in small:
        outs.append(owned[at : at + a.size].reshape(a.shape))
        at += a.size
    return tuple(outs), at_place.to_abs(grad_input, 1)


def per_device(
    inputs,
    seg_ids,
    gain_attn,
    w_query,
    w_key,
    w_value,
    w_outgate,
    w_rank_in,
    w_rank_out,
    rank_bias,
    head_gain,
    w_output,
    gain_ffn,
    w_gate,
    w_up,
    w_down,
    cotangent,
):
    f32 = jnp.float32
    bf16 = jnp.bfloat16
    at_place = Places()
    nb, b, c, t = at_place.nb, at_place.b, at_place.c, at_place.t
    rank = w_rank_in.shape[1]
    heads = HEADS // PAIR
    keys_w, vals_w = KEYS // PAIR, VALS // PAIR
    dim = inputs.shape[2]
    dim_own = dim // nb

    weights = (w_query, w_key, w_value, w_outgate, w_output, w_gate, w_up, w_down)
    small = (gain_attn, gain_ffn, rank_bias, head_gain, w_rank_in, w_rank_out)
    tok_count = PAIR * inputs.shape[1]
    half_tok = inputs.shape[1]
    reach_chips = -(-(SEG_MOST - 1) // tok_count)
    steps, step = [], 1
    while step < min(reach_chips, at_place.chips):
        steps.append(step)
        step *= 2
    paired = nb == 2 and at_place.ns % 8 == 0 and len(steps) in (1, 2)
    if paired:
        rows = [a.reshape(1, -1).astype(f32) for a in small[:4]]
        moved, front = attention_front(
            weights, inputs[0], seg_ids.astype(f32), rows + [w_rank_in, w_rank_out], steps
        )
    else:
        moved, front = plain_front(at_place, weights, inputs, seg_ids, small, steps)
    proj_own, proj_far, out_own, out_far, gu_own, gu_far, down_w = moved
    gain_one, gain_two = front.gain_one_rel[0], front.gain_two_rel[0]
    normed, low_rank, resid = front.normed, front.low_rank, front.resid
    normed_two, rank_out_w = front.normed_two, front.rank_out_core
    rank_in_w = jnp.concatenate([w_rank_in, front.rank_in_far], axis=0)
    out_w = jnp.concatenate(
        [out_own] + [out_far[k * vals_w : (k + 1) * vals_w] for k in range(nb - 1)], axis=1
    )
    ff_c = down_w.shape[0]

    cot_own = cotangent[0]
    cot_pair = at_place.pair_all(cot_own)
    cot_far = [at_place.pair_all(a) for a in at_place.others(cot_own)]

    scale_two = rms_scale(resid)
    unit_two = resid * scale_two

    two_pair = at_place.pair_all(normed_two)
    two_far = [
        at_place.pair_all(jnp.roll(a, (k + 1) * dim_own, 1))
        for k, a in enumerate(at_place.others(normed_two))
    ]

    def feed_forward(two_rows, cot_rows):
        pre = dot32(two_rows[:, :dim_own], gu_own) + dot32(two_rows[:, dim_own:], gu_far)
        gate_pre, up_pre = pre[:, :ff_c], pre[:, ff_c:]
        sig = jax.nn.sigmoid(gate_pre)
        hidden = (gate_pre * sig * up_pre).astype(bf16)
        grad_hidden = dot_t(cot_rows, down_w)
        grad_gu = jnp.concatenate(
            [
                (grad_hidden * up_pre * silu_grad(gate_pre, sig)).astype(bf16),
                (grad_hidden * gate_pre * sig).astype(bf16),
            ],
            axis=1,
        )
        return hidden, grad_gu

    hidden, grad_gu = feed_forward(two_pair, cot_pair)
    down_sum = at_place.pair_sum(dot32(hidden, down_w))
    output = (at_place.to_abs(resid, 1) + down_sum).astype(bf16)

    two_grad = jnp.concatenate([dot_t(grad_gu, gu_own), dot_t(grad_gu, gu_far)], axis=1)
    grad_two = at_place.pair_sum(two_grad)

    hid_own = [at_place.pair_all(hidden, 1)]
    gu_pairs = [(two_pair[:, :dim_own], grad_gu)]
    down_cots = [cot_pair]
    for two_rows, cot_rows in zip(two_far, cot_far):
        far_hidden, far_grad = feed_forward(two_rows, cot_rows)
        gu_pairs.append((two_rows[:, :dim_own], far_grad))
        hid_own.append(at_place.pair_all(far_hidden, 1))
        down_cots.append(cot_rows)
    ff_own = hid_own[0].shape[1] // nb
    down_pairs = [
        (lax.dynamic_slice_in_dim(h, b * ff_own, ff_own, 1), core_cols(g, c))
        for h, g in zip(hid_own, down_cots)
    ]
    part_gate = grad_dot([(left, right[:, :ff_c]) for left, right in gu_pairs]).astype(bf16)
    part_up = grad_dot([(left, right[:, ff_c:]) for left, right in gu_pairs]).astype(bf16)
    part_down = grad_dot(down_pairs).astype(bf16)

    grad_gain_two = jnp.sum(grad_two * unit_two, axis=0)
    scaled_two = grad_two * gain_two
    grad_resid = at_place.to_rel(cot_own, 1).astype(f32) + scale_two * (
        scaled_two - unit_two * jnp.mean(scaled_two * unit_two, axis=-1, keepdims=True)
    )
    resid_pair = at_place.pair_all(grad_resid.astype(bf16))
    resid_far = [
        at_place.from_batch(resid_pair[:, (nb - k) * dim_own : (nb - k + 1) * dim_own], k)
        for k in range(1, nb)
    ]
    chunks = at_place.chips
    cut = lambda a: a.reshape(chunks, -1, a.shape[1])
    jobs = ((True, True), (False, True), (True, True), (True, True), (True, True))
    if paired:
        jobs += ((True, False),)
    order = (0, 1, 2, -1, 3, -1, 1, -1, -1, 0, 1, -1, -1, -1, 0, 1, 2, -1, 0, 1, 2, 3, -1, 0, 1, -1, 2, 3, -1, 0, -1, 1, 2, -1, 0, 3, -1, -1, 1, 2, -1, 0, 3, -1, -1, 1, -1, -1, 2, 3, -1, -1, -1, 0, -1, 4, 2, -1, 3, -1, 5, 3, 4, 4, 4, 2, 5, 4, 5, 3, 4, 5, 4, 5, 4, 5, 5, 5, 4, 5)
    mine, theirs, (normed_grad, grad_logits, headgain_row, grad_input) = attention_back(
        BackIn(
            **{k: v for k, v in front._asdict().items() if k in BackIn._fields},
            gate_part=cut(part_gate), down_part=cut(part_down), up_part=cut(part_up),
            resid_pair=resid_pair, resid_far=jnp.stack(resid_far), out_w=out_w,
            head_gain=front.head_gain_all, proj_own=proj_own, proj_far=proj_far,
            rank_in=rank_in_w, tokens=inputs[0], grad_resid=grad_resid,
            grad_gain_two=grad_gain_two[None],
        ),
        jobs, order, at_place.ny, at_place.nz, nb, steps,
    )
    if paired:
        rows = mine[5].reshape(-1, DV)
        gain_rows = dim_own // DV
        in_rows = rows[2 * rank :].reshape(gain_rows, rank, DV).transpose(0, 2, 1)
        small_grads = (
            rows[:gain_rows].reshape(-1), rows[2 : 2 + gain_rows].reshape(-1), rows[4],
            rows[5, : head_gain.shape[0]], in_rows.reshape(dim_own, rank), rows[rank : 2 * rank],
        )
    else:
        small_grads, grad_input = plain_end(
            at_place, front, small, inputs, rank_in_w, normed_grad, grad_logits, headgain_row[0],
            grad_resid, grad_gain_two,
        )
    g_gain_one, g_gain_two, g_bias, g_headgain, g_rank_in, g_rank_out = small_grads

    mine = [a.reshape(-1, a.shape[2]) for a in mine[:5]]
    theirs = [a.reshape(-1, a.shape[2]) for a in theirs]

    def both(i, lo, hi, axis=1):
        return at_place.by_core(mine[i][:, lo:hi], theirs[i][:, lo:hi], axis).astype(f32)

    g_gate = both(0, 0, ff_c)
    g_down = both(1, 0, part_down.shape[1])
    g_up = both(2, 0, ff_c)
    g_output = both(3, 0, dim_own, 0)
    g_query = both(4, 0, keys_w)
    g_key = both(4, keys_w, 2 * keys_w)
    g_value = both(4, 2 * keys_w, 2 * keys_w + vals_w)
    g_outgate = both(4, 2 * keys_w + vals_w, 2 * keys_w + 2 * vals_w)
    return (
        output[None],
        grad_input[None],
        g_gain_one,
        g_query,
        g_key,
        g_value,
        g_outgate,
        g_rank_in,
        g_rank_out,
        g_bias,
        g_headgain,
        g_output,
        g_gain_two,
        g_gate,
        g_up,
        g_down,
    )


def solution(mesh):
    in_specs = (
        P("batch", "seq", None),
        P("batch", "seq"),
        P("batch"),
        P("batch", None),
        P("batch", None),
        P("batch", None),
        P("batch", None),
        P("batch", None),
        P(None, "batch"),
        P("batch"),
        P("batch"),
        P(None, "batch"),
        P("batch"),
        P("batch", None),
        P("batch", None),
        P("batch", None),
        P("batch", "seq", None),
    )
    out_specs = (
        P("batch", "seq", None),
        P("batch", "seq", None),
        P("batch"),
        P("batch", None),
        P("batch", None),
        P("batch", None),
        P("batch", None),
        P("batch", None),
        P(None, "batch"),
        P("batch"),
        P("batch"),
        P(None, "batch"),
        P("batch"),
        P("batch", None),
        P("batch", None),
        P("batch", None),
    )
    return jax.shard_map(
        per_device, mesh=mesh, in_specs=in_specs, out_specs=out_specs, check_vma=False
    )
```
